32 devices in a mesh: dp: 8 (over z, y), tensor: 4 (over x, core).
Axes of the slice: x: 2, y: 2, z: 4, core: 2. Of those that a mesh axis runs over, the one named last changes fastest.
Arguments:
- block_weights: float32 [2, 9216, 768], P(None, ('dp', 'tensor')), as said below
- head_weights: float32 [2, 5120, 1024], P(None, ('dp', 'tensor')), as said below
- head_rest: float32 [4992, 1024], P('dp', 'tensor'), as said below
- embed_tables: float32 [768, 1723], P('dp'), as said below
- bias_rows: float32 [212, 128], replicated, as said below
- first_blocks: float32 [2, 9216, 768], P(None, ('dp', 'tensor')), as said below
- second_blocks: float32 [2, 9216, 768], P(None, ('dp', 'tensor')), as said below
- first_head: float32 [2, 5120, 1024], P(None, ('dp', 'tensor')), as said below
- second_head: float32 [2, 5120, 1024], P(None, ('dp', 'tensor')), as said below
- first_rest: float32 [4992, 1024], P('dp', 'tensor'), as said below
- second_rest: float32 [4992, 1024], P('dp', 'tensor'), as said below
- first_tables: float32 [768, 1723], P('dp'), as said below
- second_tables: float32 [768, 1723], P('dp'), as said below
- first_bias: float32 [212, 128], replicated, as said below
- second_bias: float32 [212, 128], replicated, as said below
- patches: bfloat16 [8, 256, 64], P('dp'), may hold values from -6 to 6
- noise: bfloat16 [1, 8, 256, 64], P(None, 'dp'), may hold values from -6 to 6
- token_mask: int32 [8, 256], P('dp'), may hold values 0 or 1
- labels: int32 [8], P('dp'), may hold values from 0 to 999
- drop_marks: int32 [8], P('dp'), may hold values 0 or 1
- timesteps: int32 [1, 8, 256], P(None, 'dp'), may hold values from 0 to 999
- step_weights: float32 [1000], replicated, may hold values from 0.3 to 3
- step_count: int32 [1], replicated, may hold values from 1 to 20
Outputs:
- loss_value: float32 [], replicated
- grad_norm: float32 [], replicated
- blocks_new: float32 [2, 9216, 768], P(None, ('dp', 'tensor'))
- blocks_first: float32 [2, 9216, 768], P(None, ('dp', 'tensor'))
- blocks_second: float32 [2, 9216, 768], P(None, ('dp', 'tensor'))
- blocks_low: bfloat16 [2, 9216, 768], P(None, ('dp', 'tensor'))
- head_new: float32 [2, 5120, 1024], P(None, ('dp', 'tensor'))
- head_first: float32 [2, 5120, 1024], P(None, ('dp', 'tensor'))
- head_second: float32 [2, 5120, 1024], P(None, ('dp', 'tensor'))
- head_low: bfloat16 [2, 5120, 1024], P(None, ('dp', 'tensor'))
- rest_new: float32 [4992, 1024], P('dp', 'tensor')
- rest_first: float32 [4992, 1024], P('dp', 'tensor')
- rest_second: float32 [4992, 1024], P('dp', 'tensor')
- rest_low: bfloat16 [4992, 1024], P('dp', 'tensor')
- tables_new: float32 [768, 1723], P('dp')
- tables_first: float32 [768, 1723], P('dp')
- tables_second: float32 [768, 1723], P('dp')
- tables_low: bfloat16 [768, 1723], P('dp')
- bias_new: float32 [212, 128], replicated
- bias_first: float32 [212, 128], replicated
- bias_second: float32 [212, 128], replicated
- bias_low: bfloat16 [212, 128], replicated
The draws below stay inside these ranges and needn't reach their ends.
Inputs may be any that keep to these rules, and one draw needn't show every extreme that they name: `block_weights`: real values. `head_weights`: real values. `head_rest`: real values. `embed_tables`: real values. `bias_rows`: real values. `first_blocks`: real values. `second_blocks`: positive. `first_head`: real values. `second_head`: positive. `first_rest`: real values. `second_rest`: positive. `first_tables`: real values. `second_tables`: positive. `first_bias`: real values. `second_bias`: positive.
All inputs are finite; a program needn't handle non-finite values. No bound on the sum of `token_mask` or of `drop_marks` on one device may be relied on, other than what follows from the above.
Results may differ from the reference program's by a relative error of at most 0.0019.
The reference program's roundings to bfloat16 on the way count: a program that leaves them out, or rounds other values in their place, can miss the bound.
Values may be sent and summed in bfloat16 or wider, within the bound.
A program may use at most 256 MiB of HBM per device.

```python
import math
import jax
import jax.numpy as jnp
from jax import lax

D = 768
HEADS = 12
HEAD = 64
FF = 3072
HW = 1024
TOKD = 64
CLASSES = 1000
BUF = 64
TOK = 256
T_STEPS = 1000
COPIES = 1
LAYERS = 2
HB = 2
IMAGES = 8
SEQ = 320
N_DP = 8
N_TENSOR = 4


clip_limit = 0.002


def piecewise(counts, values):
    return jnp.concatenate([jnp.full((count,), value, jnp.float32) for count, value in zip(counts, values)])


def param_count():
    seq_rows = TOK + BUF
    return LAYERS * ((D + 1) * (3 * D + FF) + (D + FF) * D) + HB * (HW + 1) * 5 * HW + (D + 2 * TOKD + 4 * HW + 6) * HW + (TOKD + CLASSES + 2 * seq_rows + 7 + 6 * LAYERS) * D


def blocks_scale():
    total_rows = 4 * D + 2 * FF
    slab = total_rows // (N_DP * N_TENSOR)
    row = jnp.arange(total_rows)
    within = row // slab // N_TENSOR * slab + row % slab
    inner_end = (3 * D + FF) // N_TENSOR
    proj_end = (4 * D + FF) // N_TENSOR
    scale = jnp.where(within < inner_end, D ** (-0.5), jnp.where(within < proj_end, 3.0 * D ** (-0.5), FF ** (-0.5)))
    return scale.astype(jnp.float32)[:, None]


def rest_scale():
    return piecewise((D, TOKD, TOKD, 4 * HW), (D ** (-0.5), TOKD ** (-0.5), HW ** (-0.5), HW ** (-0.5)))[:, None]


def tables_profile():
    counts = (TOKD, 1, CLASSES + 1, 2 * (TOK + BUF), 1)
    head_scale = piecewise(counts, (TOKD ** (-0.5), 0.3, 0.1, 0.1, 0.5))
    head_kind = piecewise(counts, (1.0, 4.0, 1.0, 1.0, 1.0))
    position = jnp.arange(6 * LAYERS + 4)
    gains = (position % 2 == 0) & ((position % 6 != 4) | (position >= 6 * LAYERS))
    tail_scale = jnp.where(gains, 0.2, 0.3).astype(jnp.float32)
    tail_offset = jnp.where(gains, 1.0, 0.0).astype(jnp.float32)
    scale_cols = jnp.concatenate([head_scale, tail_scale])[None, :]
    offset = jnp.concatenate([0.0 * head_scale, tail_offset])[None, :]
    kind_cols = jnp.concatenate([head_kind, 4.0 + 0.0 * tail_scale])[None, :]
    return (scale_cols, offset, kind_cols)


def master_draw(key, array_shape, scale, offset):
    return jax.random.normal(key, array_shape, jnp.float32) * scale + offset


def first_draw(key, array_shape, kind):
    typical = clip_limit * param_count() ** (-0.5) * kind
    return jax.random.normal(key, array_shape, jnp.float32) * (0.1 / 0.9) * typical


def second_draw(key, array_shape, kind):
    typical = clip_limit * param_count() ** (-0.5) * kind
    return jax.random.uniform(key, array_shape, jnp.float32, 1.0, 4.0) * (0.05 / 0.95) * typical * typical


def blocks_shape():
    return (LAYERS, 4 * D + 2 * FF, D)


def head_shape():
    return (HB, 5 * HW, HW)


def rest_shape():
    return (D + 2 * TOKD + 4 * HW, HW)


def tables_shape():
    return (D, TOKD + CLASSES + 2 * (TOK + BUF) + 7 + 6 * LAYERS)


def bias_shape():
    return ((6 + 5 * HB) * HW // 128 + LAYERS * (3 * D + FF) // 128, 128)


def draw_block_weights(key, part):
    return master_draw(key, blocks_shape(), blocks_scale(), 0.0)


def draw_first_blocks(key, part):
    return first_draw(key, blocks_shape(), 1.0)


def draw_second_blocks(key, part):
    return second_draw(key, blocks_shape(), 1.0)


def draw_head_weights(key, part):
    return master_draw(key, head_shape(), HW ** (-0.5), 0.0)


def draw_first_head(key, part):
    return first_draw(key, head_shape(), 1.0)


def draw_second_head(key, part):
    return second_draw(key, head_shape(), 1.0)


def draw_head_rest(key, part):
    return master_draw(key, rest_shape(), rest_scale(), 0.0)


def draw_first_rest(key, part):
    return first_draw(key, rest_shape(), 1.0)


def draw_second_rest(key, part):
    return second_draw(key, rest_shape(), 1.0)


def draw_embed_tables(key, part):
    scale_cols, offset, kind_cols = tables_profile()
    return master_draw(key, tables_shape(), scale_cols, offset)


def draw_first_tables(key, part):
    scale_cols, offset, kind_cols = tables_profile()
    return first_draw(key, tables_shape(), kind_cols)


def draw_second_tables(key, part):
    scale_cols, offset, kind_cols = tables_profile()
    return second_draw(key, tables_shape(), kind_cols)


def draw_bias_rows(key, part):
    return master_draw(key, bias_shape(), 0.3, 0.0)


def draw_first_bias(key, part):
    return first_draw(key, bias_shape(), 4.0)


def draw_second_bias(key, part):
    return second_draw(key, bias_shape(), 4.0)


def plant(result, key, low, largest):
    shape = result.shape
    spot = [jax.random.randint(jax.random.fold_in(key, axis), (), 0, shape[axis]) for axis in range(len(shape))]
    result = result.at[tuple(spot)].set(low)
    longest = shape.index(max(shape))
    spot[longest] = (spot[longest] + 1) % shape[longest]
    return result.at[tuple(spot)].set(largest)


def steps_of(stream_key, dims, shards, low, top_value):
    def one(axis_at, shards_of):
        draws = jax.random.uniform(jax.random.fold_in(jax.random.fold_in(stream_key, 6), axis_at), (shards_of,), jnp.float32, low / len(shards), top_value / len(shards))
        return jnp.repeat(jnp.exp(draws), dims[axis_at] // shards_of).reshape((-1,) + (1,) * (len(dims) - axis_at - 1))

    level = one(*shards[0])
    for cut in shards[1:]:
        level = level * one(*cut)
    return level


def gaussian(rng, shape, deviation, most, cuts=(), held_as=jnp.bfloat16):
    loudness = steps_of(rng, shape, cuts, -0.22, 0.18) if cuts else 1.0
    values = jax.random.normal(rng, shape, jnp.float32) * deviation * loudness
    return jnp.minimum(jnp.maximum(values, -most), most).astype(held_as)


def setup_inputs(seed: int = 0) -> dict:
    streams_of = jax.random.split(jax.random.key(seed), 24)
    return {
        "block_weights": draw_block_weights(jax.random.fold_in(streams_of[23], 71), 0),
        "head_weights": draw_head_weights(jax.random.fold_in(streams_of[23], 71), 0),
        "head_rest": draw_head_rest(jax.random.fold_in(streams_of[23], 71), 0),
        "embed_tables": draw_embed_tables(jax.random.fold_in(streams_of[23], 71), 0),
        "bias_rows": draw_bias_rows(jax.random.fold_in(streams_of[23], 71), 0),
        "first_blocks": draw_first_blocks(jax.random.fold_in(streams_of[23], 71), 0),
        "second_blocks": draw_second_blocks(jax.random.fold_in(streams_of[23], 71), 0),
        "first_head": draw_first_head(jax.random.fold_in(streams_of[23], 71), 0),
        "second_head": draw_second_head(jax.random.fold_in(streams_of[23], 71), 0),
        "first_rest": draw_first_rest(jax.random.fold_in(streams_of[23], 71), 0),
        "second_rest": draw_second_rest(jax.random.fold_in(streams_of[23], 71), 0),
        "first_tables": draw_first_tables(jax.random.fold_in(streams_of[23], 71), 0),
        "second_tables": draw_second_tables(jax.random.fold_in(streams_of[23], 71), 0),
        "first_bias": draw_first_bias(jax.random.fold_in(streams_of[23], 71), 0),
        "second_bias": draw_second_bias(jax.random.fold_in(streams_of[23], 71), 0),
        "patches": gaussian(streams_of[15], (IMAGES, TOK, TOKD), 1.0, 6.0, ((0, 8),)),
        "noise": gaussian(streams_of[16], (COPIES, IMAGES, TOK, TOKD), 1.0, 6.0, ((1, 8),)),
        "token_mask": plant((jax.random.randint(streams_of[17], (IMAGES, TOK), 0, 5) < 4).astype(jnp.int32), jax.random.fold_in(streams_of[17], 1), 0, 1),
        "labels": plant(jax.random.randint(streams_of[18], (IMAGES,), 0, CLASSES), jax.random.fold_in(streams_of[18], 1), 0, CLASSES - 1).astype(jnp.int32),
        "drop_marks": plant((jax.random.randint(streams_of[19], (IMAGES,), 0, 10) < 1).astype(jnp.int32), jax.random.fold_in(streams_of[19], 1), 0, 1),
        "timesteps": plant(jax.random.randint(streams_of[20], (COPIES, IMAGES, TOK), 0, T_STEPS), jax.random.fold_in(streams_of[20], 1), 0, T_STEPS - 1).astype(jnp.int32),
        "step_weights": jnp.clip(jnp.exp(jax.random.uniform(streams_of[21], (T_STEPS,), jnp.float32, math.log(0.3), math.log(3.0))), 0.3, 3.0),
        "step_count": jax.random.randint(streams_of[22], (1,), 1, 21).astype(jnp.int32),
    }


@jax.custom_vjp
def low(v):
    return lax.optimization_barrier(v.astype(jnp.bfloat16)).astype(jnp.float32)

@jax.custom_vjp
def low_back(v):
    return v

def low_keep(v):
    return (low(v), None)

def low_pass(kept, grad):
    return (grad,)

def back_keep(v):
    return (v, None)

def back_low(kept, grad):
    return (low(grad),)
low.defvjp(low_keep, low_pass)
low_back.defvjp(back_keep, back_low)
highest = lax.Precision.HIGHEST
norm_eps = 1e-06
beta_first = 0.9
beta_second = 0.95
adam_eps = 1e-08
learn_rate = 0.02
decay_rate = 0.05
clip_limit = 0.002

def matmul(left, right):
    return jnp.dot(left, right, precision=highest)

def round_both(inputs):
    return low(low_back(inputs))

def layer_norm(inputs, gain_vec, offset_vec):
    average = lax.optimization_barrier(jnp.mean(inputs, axis=-1, keepdims=True))
    centred = inputs - average
    spread = lax.optimization_barrier(jnp.mean(centred * centred, axis=-1, keepdims=True))
    return centred * lax.rsqrt(spread + norm_eps) * gain_vec + offset_vec

def modulate(inputs, shift_vec, scale_vec):
    return layer_norm(inputs, 1.0, 0.0) * (1.0 + scale_vec) + shift_vec

def sinusoid(step_ids):
    half_width = HW // 2
    frequency = jnp.exp(-math.log(10000.0) * jnp.arange(half_width, dtype=jnp.float32) / half_width)
    angles = step_ids.astype(jnp.float32)[..., None] * frequency
    return jnp.concatenate([jnp.cos(angles), jnp.sin(angles)], axis=-1)

def cut_rows(packed, counts):
    pieces = []
    begin_at = 0
    for count in counts:
        pieces.append(packed[begin_at:begin_at + count])
        begin_at = begin_at + count
    return pieces

def group_rows(packed, widths):
    leading = packed.shape[:-2]
    width = packed.shape[-1]
    slab = packed.shape[-2] // (N_DP * N_TENSOR)
    grouped = packed.reshape(leading + (N_DP, N_TENSOR, slab, width))
    grouped = jnp.swapaxes(grouped, -4, -3).reshape(leading + (N_TENSOR, N_DP * slab, width))
    pieces = []
    begin_at = 0
    for section in widths:
        pieces.append(grouped[..., begin_at:begin_at + section, :].reshape(leading + (N_TENSOR * section, width)))
        begin_at = begin_at + section
    return pieces

def block(stream, visible, row_list, bias_vec, vectors):
    query_w, key_w, value_w, up_w, proj_w, down_w = row_list
    normed = low(layer_norm(stream, vectors[0], vectors[1]))

    def project(weights, bias):
        return round_both(matmul(normed, weights.T) + bias).reshape(SEQ, HEADS, HEAD)
    queries = project(query_w, bias_vec[:D])
    key_rows = project(key_w, bias_vec[D:2 * D])
    value_rows = project(value_w, bias_vec[2 * D:3 * D])
    scores = low_back(jnp.einsum('qhd,khd->hqk', queries, key_rows, precision=highest) * HEAD ** (-0.5))
    scores = scores + (visible[None, None, :] - 1.0) * 1000000000.0
    chance = low(jax.nn.softmax(scores, axis=-1))
    attended = round_both(jnp.einsum('hqk,khd->qhd', chance, value_rows, precision=highest)).reshape(SEQ, D)
    middle = stream + low_back(matmul(attended, proj_w) + vectors[4])
    second = low(layer_norm(middle, vectors[2], vectors[3]))
    inner = low_back(matmul(second, up_w.T) + bias_vec[3 * D:])
    active = low(jax.nn.gelu(inner, approximate=False))
    return middle + low_back(matmul(active, down_w) + vectors[5])

def adam_update(weight, moment_one, moment_two, gradient, factor, step_num):
    gradient = gradient * factor
    moment_one = beta_first * moment_one + (1.0 - beta_first) * gradient
    moment_two = beta_second * moment_two + (1.0 - beta_second) * gradient * gradient
    fixed_one = moment_one / (1.0 - beta_first ** step_num)
    fixed_two = moment_two / (1.0 - beta_second ** step_num)
    weight = weight - learn_rate * (fixed_one / (jnp.sqrt(fixed_two) + adam_eps) + decay_rate * weight)
    return (weight, moment_one, moment_two)

def reference(block_weights, head_weights, head_rest, embed_tables, bias_rows, first_blocks, second_blocks, first_head, second_head, first_rest, second_rest, first_tables, second_tables, first_bias, second_bias, patches, noise, token_mask, labels, drop_marks, timesteps, step_weights, step_count):
    mask_float = token_mask.astype(jnp.float32)
    row_weight = step_weights[timesteps] * mask_float[None]
    weight_total = jnp.sum(row_weight)
    image_items = (patches.astype(jnp.float32), jnp.moveaxis(noise, 1, 0).astype(jnp.float32), mask_float, labels, drop_marks, jnp.moveaxis(timesteps, 1, 0), jnp.moveaxis(row_weight, 1, 0))
    local_width = D // N_TENSOR
    local_ff = FF // N_TENSOR

    def forward(block_master, head_master, rest_master, table_master, bias_master):
        block_parts = group_rows(low(block_master), (local_width,) * 3 + (local_ff, local_width, local_ff))
        head_parts = group_rows(low(head_master), (HW // N_TENSOR,) * 5)
        rest_parts = cut_rows(rest_master, (D, TOKD, TOKD, HW, HW, HW, HW))
        cond_weight, input_weight, output_weight, time_first, time_second, final_shift, final_scale = [low(piece) for piece in rest_parts]
        flat_bias = bias_master.reshape(-1)
        rest_bias = flat_bias[:6 * HW].reshape(6, HW)
        head_bias = flat_bias[6 * HW:6 * HW + 5 * HB * HW].reshape(HB, 5, HW)
        column_bias = flat_bias[6 * HW + 5 * HB * HW:].reshape(LAYERS, 3 * D + FF)
        table_parts = cut_rows(table_master.T, (TOKD, 1, CLASSES + 1, SEQ, SEQ, 1, 6 * LAYERS, 4))
        layer_vectors = table_parts[6].reshape(LAYERS, 6, D)
        final_norms = table_parts[7]

        def layer_args(layer_idx):
            return ([piece[layer_idx] for piece in block_parts], column_bias[layer_idx], layer_vectors[layer_idx])

        def section(slot, segment, cond_act):
            return matmul(cond_act, head_parts[slot][segment].T) + head_bias[segment, slot]

        def one_image(items):
            patch_rows, noise_rows, mask_one, label_one, drop_one, step_ids, weight_rows = items
            chosen = jnp.where(drop_one == 1, CLASSES, label_one)
            picker = (jnp.arange(CLASSES + 1) == chosen).astype(jnp.float32)
            class_row = matmul(picker, table_parts[2])
            tokens = low_back(matmul(patch_rows, low(table_parts[0])) + table_parts[1][0])
            stream = jnp.concatenate([jnp.broadcast_to(class_row, (BUF, D)), tokens], axis=0) + table_parts[3]
            visible = jnp.concatenate([jnp.ones((BUF,), jnp.float32), 1.0 - mask_one])
            stream = block(stream, visible, *layer_args(0))
            stream = layer_norm(stream, final_norms[0], final_norms[1])
            hidden_rows = jnp.concatenate([jnp.zeros((BUF,), jnp.float32), mask_one])[:, None]
            stream = stream * (1.0 - hidden_rows) + table_parts[5][0] * hidden_rows + table_parts[4]
            stream = block(stream, jnp.ones((SEQ,), jnp.float32), *layer_args(1))
            latent = low(layer_norm(stream, final_norms[2], final_norms[3])[BUF:])
            condition = matmul(latent, cond_weight) + rest_bias[0]
            time_feat = low(sinusoid(step_ids))
            time_pre = low_back(matmul(time_feat, time_first) + rest_bias[2])
            time_embed = matmul(low(jax.nn.silu(time_pre)), time_second) + rest_bias[3]
            cond_vec = low_back(condition[None] + time_embed)
            cond_act = low(jax.nn.silu(cond_vec))
            phase = step_ids.astype(jnp.float32)[..., None] * (math.pi / (2 * T_STEPS))
            signal_coef = jnp.cos(phase)
            noise_coef = jnp.sin(phase)
            noisy_rows = low(signal_coef * patch_rows + noise_coef * noise_rows)
            target = signal_coef * noise_rows - noise_coef * patch_rows
            hidden_state = low_back(matmul(noisy_rows, input_weight) + rest_bias[1])
            for segment in range(HB):
                shift_vec = low_back(section(0, segment, cond_act))
                scale_vec = low_back(section(1, segment, cond_act))
                gate_vec = low_back(section(2, segment, cond_act))
                modulated = low(modulate(hidden_state, shift_vec, scale_vec))
                inner = low_back(section(3, segment, modulated))
                branch = low_back(matmul(low(jax.nn.silu(inner)), head_parts[4][segment]) + head_bias[segment, 4])
                hidden_state = hidden_state + gate_vec * branch
            shift_last = low_back(matmul(cond_act, final_shift) + rest_bias[4])
            scale_last = low_back(matmul(cond_act, final_scale) + rest_bias[5])
            predicted = low_back(matmul(low(modulate(hidden_state, shift_last, scale_last)), output_weight.T))
            sq_error = lax.optimization_barrier(jnp.mean((predicted - target) ** 2, axis=-1))
            return jnp.sum(weight_rows * sq_error)
        return jnp.sum(lax.map(jax.checkpoint(one_image), image_items)) / weight_total
    masters = (block_weights, head_weights, head_rest, embed_tables, bias_rows)
    loss_value, pull = jax.vjp(forward, *masters)
    grads = pull(jnp.ones_like(loss_value))
    grad_norm = jnp.sqrt(sum((jnp.sum(piece * piece) for piece in grads)))
    factor = jnp.minimum(1.0, clip_limit / (grad_norm + 1e-06))
    step_num = step_count[0].astype(jnp.float32)
    blocks_new, blocks_first, blocks_second = adam_update(block_weights, first_blocks, second_blocks, grads[0], factor, step_num)
    head_new, head_first, head_second = adam_update(head_weights, first_head, second_head, grads[1], factor, step_num)
    rest_new, rest_first, rest_second = adam_update(head_rest, first_rest, second_rest, grads[2], factor, step_num)
    tables_new, tables_first, tables_second = adam_update(embed_tables, first_tables, second_tables, grads[3], factor, step_num)
    bias_new, bias_first, bias_second = adam_update(bias_rows, first_bias, second_bias, grads[4], factor, step_num)
    return (loss_value, grad_norm, blocks_new, blocks_first, blocks_second, blocks_new.astype(jnp.bfloat16), head_new, head_first, head_second, head_new.astype(jnp.bfloat16), rest_new, rest_first, rest_second, rest_new.astype(jnp.bfloat16), tables_new, tables_first, tables_second, tables_new.astype(jnp.bfloat16), bias_new, bias_first, bias_second, bias_new.astype(jnp.bfloat16))
```

```python
import math

import jax
import jax.numpy as jnp
from jax import lax
from jax.sharding import PartitionSpec as P

D = 768
HEAD = 64
FF = 3072
HW = 1024
TOKD = 64
CLASSES = 1000
BUF = 64
TOK = 256
T_STEPS = 1000
COPIES = 1
LAYERS = 2
HB = 2


highest = lax.Precision.HIGHEST
norm_eps = 1e-06
beta_first = 0.9
beta_second = 0.95
adam_eps = 1e-08
learn_rate = 0.02
decay_rate = 0.05
clip_limit = 0.002


def layer_norm(inputs, gain_vec, offset_vec):
    average = jnp.mean(inputs, axis=-1, keepdims=True)
    centred = inputs - average
    spread = jnp.mean(centred * centred, axis=-1, keepdims=True)
    return centred * lax.rsqrt(spread + norm_eps) * gain_vec + offset_vec


def modulate(inputs, shift_vec, scale_vec):
    return layer_norm(inputs, 1.0, 0.0) * (1.0 + scale_vec) + shift_vec


def exact_gelu(inputs):
    return jax.nn.gelu(inputs, approximate=False)


def local_back(function, inputs, incoming):
    return jax.vjp(function, inputs)[1](incoming)[0]


def sinusoid(step_ids):
    half_width = HW // 2
    frequency = jnp.exp(-math.log(10000.0) * jnp.arange(half_width, dtype=jnp.float32) / half_width)
    angles = step_ids.astype(jnp.float32)[..., None] * frequency
    return jnp.concatenate([jnp.cos(angles), jnp.sin(angles)], axis=-1)


def cut_rows(packed, counts):
    pieces = []
    begin_at = 0
    for count in counts:
        pieces.append(packed[begin_at : begin_at + count])
        begin_at = begin_at + count
    return pieces


def narrow(inputs):
    return inputs.astype(jnp.bfloat16)


def product(left, right):
    return jnp.dot(left, right, preferred_element_type=jnp.float32)


def product_left(left, right):
    return lax.dot_general(
        left, right, (((0,), (0,)), ((), ())), preferred_element_type=jnp.float32
    )


def product_right(left, right):
    return lax.dot_general(
        left, right, (((1,), (1,)), ((), ())), preferred_element_type=jnp.float32
    )


def column_sum(inputs):
    return jnp.sum(inputs.astype(jnp.float32), axis=0)


def swap(value, axis, step):
    return lax.ppermute(value, axis, [(i, i ^ step) for i in range(lax.axis_size(axis))])


def tensor_sum(partial_term, cross_type):
    if lax.axis_size("tensor") != 4:
        return lax.psum(partial_term, "tensor")
    low = lax.axis_index("tensor") % 2
    half = partial_term.shape[0] // 2
    keep = lax.dynamic_slice_in_dim(partial_term, low * half, half, 0)
    give = lax.dynamic_slice_in_dim(partial_term, (1 - low) * half, half, 0)
    pair = (keep + swap(give, "tensor", 1)).astype(cross_type)
    total = pair.astype(jnp.float32) + swap(pair, "tensor", 2).astype(jnp.float32)
    back = swap(total, "tensor", 1)
    first = jnp.where(low == 0, total, back)
    second = jnp.where(low == 0, back, total)
    return jnp.concatenate([first, second], axis=0)


def branch_sum(partial_term):
    return tensor_sum(partial_term, jnp.float32)


def input_sum(partial_term):
    return tensor_sum(partial_term, jnp.bfloat16)


def tensor_blocks(piece):
    if lax.axis_size("tensor") != 4:
        return list(lax.all_gather(piece, "tensor"))
    rank = lax.axis_index("tensor")
    near = swap(piece, "tensor", 1)
    far = swap(piece, "tensor", 2)
    cross = swap(far, "tensor", 1)
    blocks = []
    for index in range(4):
        same_pair = jnp.where(rank == index, piece, near)
        other_pair = jnp.where(rank == index ^ 2, far, cross)
        blocks.append(jnp.where(rank // 2 == index // 2, same_pair, other_pair))
    return blocks


def tensor_columns(piece):
    return jnp.concatenate(tensor_blocks(piece), axis=1)


def sum_everywhere(value, axes):
    for axis in axes:
        step = 1
        while step < lax.axis_size(axis):
            value = value + swap(value, axis, step)
            step = 2 * step
    return value


def pick(blocks, index):
    return lax.dynamic_index_in_dim(blocks, index, 0, keepdims=False)


def coded(values, level):
    body = (values * jnp.exp2(13.0 - level)).astype(jnp.float16)
    return jnp.concatenate([body, jnp.full((16, values.shape[1]), level).astype(jnp.float16)])


def decoded(message):
    level = message[-1, 0].astype(jnp.float32)
    return message[:-16].astype(jnp.float32) * jnp.exp2(level - 13.0), level


def scatter_sum(grad):
    if lax.axis_size("dp") != 8:
        return lax.psum_scatter(grad, "dp", scatter_dimension=0, tiled=True)
    rank = lax.axis_index("dp")
    low, high = rank % 2, rank // 2
    slab, columns = grad.shape[0] // 8, grad.shape[1]
    blocks = grad.reshape(4, 2 * slab, columns)
    peak = jnp.maximum(jnp.max(jnp.abs(grad)), 2.0**-100)
    level = jnp.ceil(jnp.log2(peak))
    keep = lax.dynamic_slice_in_dim(blocks, low * slab, slab, 1)
    give = lax.dynamic_slice_in_dim(blocks, (1 - low) * slab, slab, 1)
    got, got_level = decoded(swap(coded(give.reshape(4 * slab, columns), level), "dp", 1))
    pairs = keep + got.reshape(4, slab, columns)
    level = jnp.maximum(level, got_level) + 1.0
    total = pick(pairs, high)
    arrived = [
        decoded(swap(coded(pick(pairs, high ^ step), level), "dp", 2 * step))[0]
        for step in (1, 2, 3)
    ]
    return total + arrived[0] + arrived[1] + arrived[2]


def scatter_small(grad):
    if lax.axis_size("dp") != 8:
        return lax.psum_scatter(grad, "dp", scatter_dimension=0, tiled=True)
    rank = lax.axis_index("dp")
    low, high = rank % 2, rank // 2
    slab, columns = grad.shape[0] // 8, grad.shape[1]
    blocks = grad.reshape(4, 2 * slab, columns)
    keep = lax.dynamic_slice_in_dim(blocks, low * slab, slab, 1)
    give = lax.dynamic_slice_in_dim(blocks, (1 - low) * slab, slab, 1)
    pairs = keep + swap(give, "dp", 1)
    total = pick(pairs, high)
    for step in (1, 2, 3):
        total = total + swap(pick(pairs, high ^ step), "dp", 2 * step)
    return total


def take_pieces(vector, starts, counts):
    return jnp.concatenate(
        [lax.dynamic_slice_in_dim(vector, start, count) for start, count in zip(starts, counts)]
    )


def place_pieces(total, pieces, starts):
    full = jnp.zeros((total,), jnp.float32)
    for piece, start in zip(pieces, starts):
        full = lax.dynamic_update_slice_in_dim(full, piece, start, 0)
    return full


def score_block(queries, key_rows, visible):
    scores = jnp.einsum(
        "bqhd,bkhd->bhqk", queries, key_rows, preferred_element_type=jnp.float32
    ) * HEAD ** (-0.5)
    return scores + (visible[:, None, None, :] - 1.0) * 1000000000.0


def attention(queries, key_rows, value_rows, visible):
    scores = score_block(queries, key_rows, visible)
    largest = jnp.max(scores, axis=-1, keepdims=True)
    exponent = jnp.exp(scores - largest)
    normaliser = jnp.sum(exponent, axis=-1, keepdims=True)
    chance = narrow(exponent / normaliser)
    attended = narrow(
        jnp.einsum("bhqk,bkhd->bqhd", chance, value_rows, preferred_element_type=jnp.float32)
    )
    return (attended, largest + jnp.log(normaliser))


def attention_back(queries, key_rows, value_rows, visible, log_total, grad_attended):
    chance = jnp.exp(score_block(queries, key_rows, visible) - log_total)
    grad_values = jnp.einsum(
        "bhqk,bqhd->bkhd", narrow(chance), grad_attended, preferred_element_type=jnp.float32
    )
    grad_chance = jnp.einsum(
        "bqhd,bkhd->bhqk", grad_attended, value_rows, preferred_element_type=jnp.float32
    )
    grad_scores = narrow(
        chance * (grad_chance - jnp.sum(chance * grad_chance, axis=-1, keepdims=True))
    )
    grad_queries = jnp.einsum(
        "bhqk,bkhd->bqhd", grad_scores, key_rows, preferred_element_type=jnp.float32
    ) * HEAD ** (-0.5)
    grad_keys = jnp.einsum(
        "bhqk,bqhd->bkhd", grad_scores, queries, preferred_element_type=jnp.float32
    ) * HEAD ** (-0.5)
    return (grad_queries, grad_keys, grad_values)


def block_forward(stream, visible, layer_rows, layer_bias, vectors):
    images = visible.shape[0]
    local_width = D // lax.axis_size("tensor")
    local_ff = FF // lax.axis_size("tensor")
    heads_here = local_width // HEAD
    flat = stream.reshape(-1, D)
    normed = narrow(layer_norm(flat, vectors[0], vectors[1]))
    mixed = narrow(
        product_right(normed, layer_rows[: 3 * local_width]) + layer_bias[: 3 * local_width]
    )
    parts = [
        mixed[:, slot * local_width : (slot + 1) * local_width].reshape(
            images, -1, heads_here, HEAD
        )
        for slot in range(3)
    ]
    attended, log_total = attention(parts[0], parts[1], parts[2], visible)
    attended = attended.reshape(-1, local_width)
    middle = (
        flat
        + branch_sum(
            product(attended, layer_rows[3 * local_width + local_ff : 4 * local_width + local_ff])
        )
        + vectors[4]
    )
    second = narrow(layer_norm(middle, vectors[2], vectors[3]))
    inner = (
        product_right(second, layer_rows[3 * local_width : 3 * local_width + local_ff])
        + layer_bias[3 * local_width :]
    )
    active = narrow(exact_gelu(inner))
    result = (
        middle + branch_sum(product(active, layer_rows[4 * local_width + local_ff :])) + vectors[5]
    )
    return (
        result.reshape(stream.shape),
        (flat, normed, parts, log_total, attended, middle, second, inner, active),
    )


def block_back(incoming, visible, layer_rows, vectors, stored):
    flat, normed, parts, log_total, attended, middle, second, inner, active = stored
    local_width = D // lax.axis_size("tensor")
    local_ff = FF // lax.axis_size("tensor")
    mix_rows = layer_rows[: 3 * local_width]
    up_rows = layer_rows[3 * local_width : 3 * local_width + local_ff]
    proj_rows = layer_rows[3 * local_width + local_ff : 4 * local_width + local_ff]
    down_rows = layer_rows[4 * local_width + local_ff :]
    flow = incoming.reshape(-1, D)
    grad_branch = narrow(flow)
    grad_down = product_left(active, grad_branch)
    grad_active = product_right(grad_branch, down_rows)
    grad_inner = narrow(local_back(exact_gelu, inner, grad_active))
    grad_up = product_left(grad_inner, second)
    grad_second = input_sum(product(grad_inner, up_rows))
    grad_middle, grad_gain_two, grad_shift_two = jax.vjp(
        layer_norm, middle, vectors[2], vectors[3]
    )[1](grad_second)
    grad_middle = flow + grad_middle
    grad_attn = narrow(grad_middle)
    grad_proj = product_left(attended, grad_attn)
    grad_attended = narrow(product_right(grad_attn, proj_rows)).reshape(parts[0].shape)
    grads_mixed = attention_back(parts[0], parts[1], parts[2], visible, log_total, grad_attended)
    grad_mixed = narrow(
        jnp.concatenate([piece.reshape(-1, local_width) for piece in grads_mixed], axis=1)
    )
    grad_mix = product_left(grad_mixed, normed)
    grad_normed = input_sum(product(grad_mixed, mix_rows))
    grad_flat, grad_gain_one, grad_shift_one = jax.vjp(layer_norm, flat, vectors[0], vectors[1])[1](
        grad_normed
    )
    grad_rows = jnp.concatenate([grad_mix, grad_up, grad_proj, grad_down], axis=0)
    grad_bias = jnp.concatenate([column_sum(grad_mixed), column_sum(grad_inner)])
    grad_vectors = jnp.stack(
        [
            grad_gain_one,
            grad_shift_one,
            grad_gain_two,
            grad_shift_two,
            column_sum(grad_attn),
            column_sum(grad_branch),
        ]
    )
    return ((grad_middle + grad_flat).reshape(incoming.shape), grad_rows, grad_bias, grad_vectors)


def gathered_parts(columns, count):
    width = columns.shape[1] // count
    blocks = tensor_blocks(columns)
    return [
        jnp.concatenate([block[:, slot * width : (slot + 1) * width] for block in blocks], axis=1)
        for slot in range(count)
    ]


def adaptive_vectors(cond_act, segment_rows, segment_bias):
    local_hidden = HW // lax.axis_size("tensor")
    adaptive = (
        product_right(cond_act, segment_rows[: 3 * local_hidden]) + segment_bias[: 3 * local_hidden]
    )
    return gathered_parts(adaptive, 3)


def head_block(hidden_state, vectors, segment_rows, segment_bias, last_bias):
    local_hidden = HW // lax.axis_size("tensor")
    shift_vec, scale_vec, gate_vec = vectors
    modulated = narrow(modulate(hidden_state, shift_vec, scale_vec))
    inner = (
        product_right(modulated, segment_rows[3 * local_hidden : 4 * local_hidden])
        + segment_bias[3 * local_hidden :]
    )
    active = narrow(jax.nn.silu(inner))
    branch = branch_sum(product(active, segment_rows[4 * local_hidden :])) + last_bias
    return (
        hidden_state + gate_vec * branch,
        (hidden_state, shift_vec, scale_vec, gate_vec, modulated, inner, active, branch),
    )


def head_block_back(incoming, cond_act, segment_rows, offset, stored):
    hidden_state, shift_vec, scale_vec, gate_vec, modulated, inner, active, branch = stored
    local_hidden = HW // lax.axis_size("tensor")
    grad_gate = incoming * branch
    grad_branch = narrow(incoming * gate_vec)
    grad_down = product_left(active, grad_branch)
    grad_active = product_right(grad_branch, segment_rows[4 * local_hidden :])
    grad_inner = narrow(local_back(jax.nn.silu, inner, grad_active))
    grad_up = product_left(grad_inner, modulated)
    grad_modulated = input_sum(
        product(grad_inner, segment_rows[3 * local_hidden : 4 * local_hidden])
    )
    grad_hidden, grad_shift, grad_scale = jax.vjp(modulate, hidden_state, shift_vec, scale_vec)[1](
        grad_modulated
    )
    grad_adaptive = narrow(
        jnp.concatenate(
            [
                lax.dynamic_slice_in_dim(piece, offset, local_hidden, 1)
                for piece in (grad_shift, grad_scale, grad_gate)
            ],
            axis=1,
        )
    )
    grad_ada = product_left(grad_adaptive, cond_act)
    grad_cond = product(grad_adaptive, segment_rows[: 3 * local_hidden])
    grad_rows = jnp.concatenate([grad_ada, grad_up, grad_down], axis=0)
    grad_bias = jnp.concatenate([column_sum(grad_adaptive), column_sum(grad_inner)])
    return (incoming + grad_hidden, grad_cond, grad_rows, grad_bias, column_sum(grad_branch))


def adam_update(weight, moment_one, moment_two, gradient, factor, step_num):
    gradient = gradient * factor
    moment_one = beta_first * moment_one + (1.0 - beta_first) * gradient
    moment_two = beta_second * moment_two + (1.0 - beta_second) * gradient * gradient
    fixed_one = moment_one / (1.0 - beta_first**step_num)
    fixed_two = moment_two / (1.0 - beta_second**step_num)
    weight = weight - learn_rate * (
        fixed_one / (jnp.sqrt(fixed_two) + adam_eps) + decay_rate * weight
    )
    return (weight, moment_one, moment_two)


def local(
    block_weights,
    head_weights,
    head_rest,
    embed_tables,
    bias_rows,
    first_blocks,
    second_blocks,
    first_head,
    second_head,
    first_rest,
    second_rest,
    first_tables,
    second_tables,
    first_bias,
    second_bias,
    patches,
    noise,
    token_mask,
    labels,
    drop_marks,
    timesteps,
    step_weights,
    step_count,
):
    tensor_size = lax.axis_size("tensor")
    tensor_index = lax.axis_index("tensor")
    local_width = D // tensor_size
    local_ff = FF // tensor_size
    local_hidden = HW // tensor_size
    offset = tensor_index * local_hidden
    column_starts = [slot * D + tensor_index * local_width for slot in range(3)] + [
        3 * D + tensor_index * local_ff
    ]
    column_counts = [local_width] * 3 + [local_ff]
    head_starts = [slot * HW + offset for slot in range(4)]
    dp_size = lax.axis_size("dp")
    dp_index = lax.axis_index("dp")
    images = patches.shape[0]
    all_images = dp_size * images
    mask_float = token_mask.astype(jnp.float32)
    matches = timesteps[..., None] == jnp.arange(T_STEPS)
    row_weight = (
        jnp.sum(jnp.where(matches, step_weights, 0.0), axis=-1) * mask_float[None]
    ).reshape(-1)
    chosen = jnp.where(drop_marks == 1, CLASSES, labels)
    shared_values = lax.dynamic_update_slice_in_dim(
        jnp.zeros((all_images,), jnp.float32), chosen.astype(jnp.float32), dp_index * images, 0
    )
    shared_values = sum_everywhere(
        jnp.concatenate([shared_values, jnp.sum(row_weight)[None]]), ("dp",)
    )
    weight_total = shared_values[all_images]
    picker = (shared_values[:all_images, None] == jnp.arange(CLASSES + 1)[None, :]).astype(
        jnp.float32
    )
    class_at = TOKD + 1
    class_end = class_at + CLASSES + 1
    table_share = jnp.concatenate(
        [
            embed_tables[:, :class_at],
            embed_tables[:, class_end:],
            lax.dot_general(
                embed_tables[:, class_at:class_end],
                picker,
                (((1,), (1,)), ((), ())),
                precision=highest,
            ),
        ],
        axis=1,
    )
    block_share = narrow(block_weights)
    block_all = [lax.all_gather(block_share[0], "dp", axis=0, tiled=True)]
    table_cols = lax.all_gather(table_share, "dp", axis=0, tiled=True)
    for layer in range(1, LAYERS):
        block_all.append(lax.all_gather(block_share[layer], "dp", axis=0, tiled=True))
    rest_rows = lax.all_gather(narrow(head_rest), "dp", axis=0, tiled=True)
    head_share = narrow(head_weights)
    head_all = [
        lax.all_gather(head_share[segment], "dp", axis=0, tiled=True) for segment in range(HB)
    ]
    cond_mine, input_mine, output_mine, time_first, second_mine, final_shift, final_scale = cut_rows(
        rest_rows, (D, TOKD, TOKD, HW, HW, HW, HW)
    )
    cond_weight, input_weight, output_weight, time_second = cut_rows(
        tensor_columns(jnp.concatenate([cond_mine, input_mine, output_mine, second_mine], axis=0)),
        (D, TOKD, TOKD, HW),
    )
    flat_bias = bias_rows.reshape(-1)
    rest_bias = flat_bias[: 6 * HW].reshape(6, HW)
    head_bias = flat_bias[6 * HW : 6 * HW + 5 * HB * HW].reshape(HB, 5 * HW)
    column_bias = flat_bias[6 * HW + 5 * HB * HW :].reshape(LAYERS, 3 * D + FF)
    table_parts = cut_rows(
        table_cols.T, (TOKD, 1, TOK + BUF, TOK + BUF, 1, 6 * LAYERS, 4, all_images)
    )
    layer_vectors = table_parts[5].reshape(LAYERS, 6, D)
    final_norms = table_parts[6]
    class_rows = lax.dynamic_slice_in_dim(table_parts[7], dp_index * images, images, 0)
    patch_flat = patches.reshape(-1, TOKD)
    tokens = product(patch_flat, narrow(table_parts[0])) + table_parts[1][0]
    stream = (
        jnp.concatenate(
            [
                jnp.broadcast_to(class_rows[:, None, :], (images, BUF, D)),
                tokens.reshape(images, TOK, D),
            ],
            axis=1,
        )
        + table_parts[2]
    )
    buffer_ones = jnp.ones((images, BUF), jnp.float32)
    visible_enc = jnp.concatenate([buffer_ones, 1.0 - mask_float], axis=1)
    visible_all = jnp.ones((images, TOK + BUF), jnp.float32)
    hidden_rows = jnp.concatenate([0.0 * buffer_ones, mask_float], axis=1)[..., None]
    layer_bias = [
        take_pieces(column_bias[layer], column_starts, column_counts) for layer in range(LAYERS)
    ]
    encoded, stored_enc = block_forward(
        stream, visible_enc, block_all[0], layer_bias[0], layer_vectors[0]
    )
    enc_normed = layer_norm(encoded, final_norms[0], final_norms[1])
    decoder_in = enc_normed * (1.0 - hidden_rows) + table_parts[4][0] * hidden_rows + table_parts[3]
    decoded, stored_dec = block_forward(
        decoder_in, visible_all, block_all[1], layer_bias[1], layer_vectors[1]
    )
    latent = narrow(layer_norm(decoded, final_norms[2], final_norms[3])[:, BUF:].reshape(-1, D))
    condition = product(latent, cond_weight) + rest_bias[0]
    step_rows = timesteps.reshape(COPIES, -1)
    time_feat = narrow(sinusoid(step_rows).reshape(-1, HW))
    time_pre = product(time_feat, time_first) + lax.dynamic_slice_in_dim(
        rest_bias[2], offset, local_hidden
    )
    time_act = tensor_columns(narrow(jax.nn.silu(time_pre)))
    time_embed = product(time_act, time_second) + rest_bias[3]
    cond_vec = (condition[None] + time_embed.reshape(COPIES, -1, HW)).reshape(-1, HW)
    cond_act = narrow(jax.nn.silu(cond_vec))
    phase = step_rows.astype(jnp.float32)[..., None] * (math.pi / (2 * T_STEPS))
    signal_coef = jnp.cos(phase)
    noise_coef = jnp.sin(phase)
    clean = patch_flat.astype(jnp.float32)[None]
    noise_rows = noise.reshape(COPIES, -1, TOKD).astype(jnp.float32)
    noisy_rows = narrow((signal_coef * clean + noise_coef * noise_rows).reshape(-1, TOKD))
    target = (signal_coef * noise_rows - noise_coef * clean).reshape(-1, TOKD)
    hidden_state = product(noisy_rows, input_weight) + rest_bias[1]
    stored_head = []
    segment_biases = [
        take_pieces(head_bias[segment], head_starts, [local_hidden] * 4) for segment in range(HB)
    ]
    head_vectors = [
        adaptive_vectors(cond_act, head_all[segment], segment_biases[segment])
        for segment in range(HB)
    ]
    last_pair = jnp.concatenate(
        [product(cond_act, final_shift), product(cond_act, final_scale)], axis=1
    ) + take_pieces(flat_bias, [4 * HW + offset, 5 * HW + offset], [local_hidden] * 2)
    shift_last, scale_last = gathered_parts(last_pair, 2)
    for segment in range(HB):
        hidden_state, stored = head_block(
            hidden_state,
            head_vectors[segment],
            head_all[segment],
            segment_biases[segment],
            head_bias[segment, 4 * HW :],
        )
        stored_head.append(stored)
    final_in = narrow(modulate(hidden_state, shift_last, scale_last))
    predicted = product_right(final_in, output_weight)
    sq_error = jnp.mean((predicted - target) ** 2, axis=-1)
    numerator = jnp.sum(row_weight * sq_error)
    grad_pred = narrow(2.0 / (TOKD * weight_total) * row_weight[:, None] * (predicted - target))
    grad_final = product(grad_pred, output_weight)
    grad_hidden, grad_shift_last, grad_scale_last = jax.vjp(
        modulate, hidden_state, shift_last, scale_last
    )[1](grad_final)

    def own_columns(value):
        return lax.dynamic_slice_in_dim(value, offset, local_hidden, 1)

    grad_shift_last = narrow(own_columns(grad_shift_last))
    grad_scale_last = narrow(own_columns(grad_scale_last))
    cond_split = product_right(grad_shift_last, final_shift) + product_right(
        grad_scale_last, final_scale
    )
    head_grads = []
    head_bias_grads = []
    for segment in reversed(range(HB)):
        grad_hidden, grad_cond, grad_segment, grad_segment_bias, grad_last_bias = head_block_back(
            grad_hidden, cond_act, head_all[segment], offset, stored_head[segment]
        )
        cond_split = cond_split + grad_cond
        head_grads.insert(0, grad_segment)
        pieces = [
            grad_segment_bias[slot * local_hidden : (slot + 1) * local_hidden] for slot in range(4)
        ] + [grad_last_bias / tensor_size]
        head_bias_grads.insert(0, place_pieces(5 * HW, pieces, head_starts + [4 * HW]))
    grad_input = narrow(grad_hidden)
    grad_cond_vec = narrow(local_back(jax.nn.silu, cond_vec, input_sum(cond_split)))
    cond_bias_grad = column_sum(grad_cond_vec)
    grad_time_act = product_right(
        grad_cond_vec, lax.dynamic_slice_in_dim(time_second, offset, local_hidden, 0)
    )
    grad_time_pre = narrow(local_back(jax.nn.silu, time_pre, grad_time_act))
    grad_latent = jnp.sum(product(grad_cond_vec, cond_weight.T).reshape(COPIES, -1, D), axis=0)
    grad_cond_mine = own_columns(grad_cond_vec)
    grad_rest = jnp.concatenate(
        [
            product_left(jnp.tile(latent, (COPIES, 1)), grad_cond_mine),
            product_left(noisy_rows, own_columns(grad_input)),
            product_left(grad_pred, own_columns(final_in)),
            product_left(time_feat, grad_time_pre),
            product_left(time_act, grad_cond_mine),
            product_left(cond_act, grad_shift_last),
            product_left(cond_act, grad_scale_last),
        ],
        axis=0,
    )
    rest_bias_grad = place_pieces(
        6 * HW,
        [
            cond_bias_grad / tensor_size,
            column_sum(grad_input) / tensor_size,
            column_sum(grad_time_pre),
            cond_bias_grad / tensor_size,
            column_sum(grad_shift_last),
            column_sum(grad_scale_last),
        ],
        [0, HW, 2 * HW + offset, 3 * HW, 4 * HW + offset, 5 * HW + offset],
    )
    owned_head = jnp.stack([scatter_sum(grad) for grad in head_grads])
    owned_rest = scatter_sum(grad_rest)
    grad_top = jnp.concatenate(
        [jnp.zeros((images, BUF, D), jnp.float32), grad_latent.reshape(images, TOK, D)], axis=1
    )
    grad_decoded, grad_gain_dec, grad_shift_dec = jax.vjp(
        layer_norm, decoded, final_norms[2], final_norms[3]
    )[1](grad_top)
    grad_dec_in, grad_rows_dec, grad_bias_dec, grad_vec_dec = block_back(
        grad_decoded, visible_all, block_all[1], layer_vectors[1], stored_dec
    )
    grad_encoded, grad_gain_enc, grad_shift_enc = jax.vjp(
        layer_norm, encoded, final_norms[0], final_norms[1]
    )[1](grad_dec_in * (1.0 - hidden_rows))
    grad_stream, grad_rows_enc, grad_bias_enc, grad_vec_enc = block_back(
        grad_encoded, visible_enc, block_all[0], layer_vectors[0], stored_enc
    )
    grad_tokens = narrow(grad_stream[:, BUF:].reshape(-1, D))
    grad_class = lax.dynamic_update_slice_in_dim(
        jnp.zeros((all_images, D), jnp.float32),
        jnp.sum(grad_stream[:, :BUF], axis=1),
        dp_index * images,
        0,
    )
    grad_tables = jnp.concatenate(
        [
            product_left(patch_flat, grad_tokens),
            column_sum(grad_tokens)[None],
            jnp.sum(grad_stream, axis=0),
            jnp.sum(grad_dec_in, axis=0),
            jnp.sum(grad_dec_in * hidden_rows, axis=(0, 1))[None],
            jnp.stack([grad_vec_enc, grad_vec_dec]).reshape(6 * LAYERS, D),
            jnp.stack([grad_gain_enc, grad_shift_enc, grad_gain_dec, grad_shift_dec]),
            grad_class,
        ],
        axis=0,
    )
    table_count = grad_tables.shape[0]
    quarter = -(-table_count // (8 * tensor_size)) * 8
    grad_tables = jnp.pad(grad_tables, ((0, quarter * tensor_size - table_count), (0, 0)))
    grad_tables = lax.dynamic_slice_in_dim(grad_tables, tensor_index * quarter, quarter, 0)
    owned_cols = tensor_columns(scatter_small(grad_tables.T))
    kept_cols = table_count - all_images
    owned_tables = jnp.concatenate(
        [
            owned_cols[:, :class_at],
            jnp.dot(owned_cols[:, kept_cols:table_count], picker, precision=highest),
            owned_cols[:, class_at:kept_cols],
        ],
        axis=1,
    )
    owned_blocks = jnp.stack([scatter_sum(grad_rows_enc), scatter_sum(grad_rows_dec)])
    column_grads = []
    for grad_local in (grad_bias_enc, grad_bias_dec):
        pieces = [
            grad_local[slot * local_width : (slot + 1) * local_width] for slot in range(3)
        ] + [grad_local[3 * local_width :]]
        column_grads.append(place_pieces(3 * D + FF, pieces, column_starts))
    lanes = bias_rows.shape[1]
    both = ("tensor", "dp")
    bias_head = sum_everywhere(
        jnp.concatenate([rest_bias_grad] + head_bias_grads).reshape(-1, lanes), both
    )
    bias_layers = [sum_everywhere(grad.reshape(-1, lanes), both) for grad in column_grads]
    bias_grad = jnp.concatenate([bias_head] + bias_layers, axis=0)
    split_squares = (
        jnp.sum(owned_blocks * owned_blocks)
        + jnp.sum(owned_head * owned_head)
        + jnp.sum(owned_rest * owned_rest)
    )
    shared_squares = jnp.sum(owned_tables * owned_tables) / tensor_size
    every_squares = jnp.sum(bias_grad * bias_grad) / (tensor_size * lax.axis_size("dp"))
    last_sums = sum_everywhere(
        jnp.stack([split_squares + shared_squares + every_squares, numerator / tensor_size]), both
    )
    norm_square = last_sums[0]
    loss_value = last_sums[1] / weight_total
    grad_norm = jnp.sqrt(norm_square)
    factor = jnp.minimum(1.0, clip_limit / (grad_norm + 1e-06))
    step_num = step_count[0].astype(jnp.float32)
    blocks_new, blocks_first, blocks_second = adam_update(
        block_weights, first_blocks, second_blocks, owned_blocks, factor, step_num
    )
    head_new, head_first, head_second = adam_update(
        head_weights, first_head, second_head, owned_head, factor, step_num
    )
    rest_new, rest_first, rest_second = adam_update(
        head_rest, first_rest, second_rest, owned_rest, factor, step_num
    )
    tables_new, tables_first, tables_second = adam_update(
        embed_tables, first_tables, second_tables, owned_tables, factor, step_num
    )
    bias_new, bias_first, bias_second = adam_update(
        bias_rows, first_bias, second_bias, bias_grad, factor, step_num
    )
    return (
        loss_value,
        grad_norm,
        blocks_new,
        blocks_first,
        blocks_second,
        narrow(blocks_new),
        head_new,
        head_first,
        head_second,
        narrow(head_new),
        rest_new,
        rest_first,
        rest_second,
        narrow(rest_new),
        tables_new,
        tables_first,
        tables_second,
        narrow(tables_new),
        bias_new,
        bias_first,
        bias_second,
        narrow(bias_new),
    )


def solution(mesh):
    in_specs = (
        P(None, ("dp", "tensor"), None),
        P(None, ("dp", "tensor"), None),
        P("dp", "tensor"),
        P("dp", None),
        P(),
        P(None, ("dp", "tensor"), None),
        P(None, ("dp", "tensor"), None),
        P(None, ("dp", "tensor"), None),
        P(None, ("dp", "tensor"), None),
        P("dp", "tensor"),
        P("dp", "tensor"),
        P("dp", None),
        P("dp", None),
        P(),
        P(),
        P("dp", None, None),
        P(None, "dp", None, None),
        P("dp", None),
        P("dp"),
        P("dp"),
        P(None, "dp", None),
        P(),
        P(),
    )
    out_specs = (
        P(),
        P(),
        P(None, ("dp", "tensor"), None),
        P(None, ("dp", "tensor"), None),
        P(None, ("dp", "tensor"), None),
        P(None, ("dp", "tensor"), None),
        P(None, ("dp", "tensor"), None),
        P(None, ("dp", "tensor"), None),
        P(None, ("dp", "tensor"), None),
        P(None, ("dp", "tensor"), None),
        P("dp", "tensor"),
        P("dp", "tensor"),
        P("dp", "tensor"),
        P("dp", "tensor"),
        P("dp", None),
        P("dp", None),
        P("dp", None),
        P("dp", None),
        P(),
        P(),
        P(),
        P(),
    )
    return jax.shard_map(local, mesh=mesh, in_specs=in_specs, out_specs=out_specs, check_vma=False)
```

```python
import functools
import math

import jax
import jax.numpy as jnp
from jax import lax
from jax.experimental import pallas as pl
from jax.experimental.pallas import tpu as pltpu
from jax.sharding import PartitionSpec as P

D = 768
HEAD = 64
FF = 3072
HW = 1024
TOKD = 64
CLASSES = 1000
BUF = 64
TOK = 256
T_STEPS = 1000
COPIES = 1
LAYERS = 2
HB = 2


highest = lax.Precision.HIGHEST
norm_eps = 1e-06
beta_first = 0.9
beta_second = 0.95
adam_eps = 1e-08
learn_rate = 0.02
decay_rate = 0.05
clip_limit = 0.002
dp_axis, tensor_axis = "dp", "tensor"


def layer_norm(inputs, gain_vec, offset_vec):
    average = jnp.mean(inputs, axis=-1, keepdims=True)
    centred = inputs - average
    spread = jnp.mean(centred * centred, axis=-1, keepdims=True)
    return centred * lax.rsqrt(spread + norm_eps) * gain_vec + offset_vec


def modulate(inputs, shift_vec, scale_vec):
    return layer_norm(inputs, 1.0, 0.0) * (1.0 + scale_vec) + shift_vec


def exact_gelu(inputs):
    return jax.nn.gelu(inputs, approximate=False)


def local_back(function, inputs, incoming):
    return jax.vjp(function, inputs)[1](incoming)[0]


def sinusoid(step_ids):
    half_width = HW // 2
    frequency = jnp.exp(-math.log(10000.0) * jnp.arange(half_width, dtype=jnp.float32) / half_width)
    angles = step_ids.astype(jnp.float32)[..., None] * frequency
    return jnp.concatenate([jnp.cos(angles), jnp.sin(angles)], axis=-1)


def cut_rows(packed, counts):
    pieces = []
    begin_at = 0
    for count in counts:
        pieces.append(packed[begin_at : begin_at + count])
        begin_at = begin_at + count
    return pieces


def narrow(inputs):
    return inputs.astype(jnp.bfloat16)


def product(left, right):
    return jnp.dot(left, right, preferred_element_type=jnp.float32)


def product_left(left, right):
    return lax.dot_general(
        left, right, (((0,), (0,)), ((), ())), preferred_element_type=jnp.float32
    )


def product_right(left, right):
    return lax.dot_general(
        left, right, (((1,), (1,)), ((), ())), preferred_element_type=jnp.float32
    )


def column_sum(inputs):
    return jnp.sum(inputs.astype(jnp.float32), axis=0)


def swap(value, axis, step):
    return lax.ppermute(value, axis, [(i, i ^ step) for i in range(lax.axis_size(axis))])


MESH = pl.DeviceIdType.MESH
(
    first_gather,
    last_sums_kernel,
    encoder_forward,
    decoder_forward,
    head_forward,
    back_head,
    back_cond,
    back_decoder,
    back_encoder,
) = (0, 1, 2, 4, 6, 8, 10, 11, 13)
rest_group, mix_group = 100, 101


class RingGather:
    def __init__(self, shares, wholes, local_sem, send_sem, recv_sem):
        rank = lax.axis_index(dp_axis)
        self.rank, self.low, self.high = rank, lax.rem(rank, 2), lax.div(rank, 2)
        self.beside = rank + 1 - 2 * self.low
        self.ahead = 2 * lax.rem(self.high + 1, 4) + self.low
        self.behind = 2 * lax.rem(self.high + 3, 4) + self.low
        self.shares, self.wholes = shares, wholes
        self.send_sem, self.recv_sem = send_sem, recv_sem
        self.items = range(len(shares))
        self.sent = []
        self.own = [
            pltpu.make_async_copy(shares[item], wholes[item].at[rank], local_sem.at[item])
            for item in self.items
        ]

    def copy(self, item, source, place, peer, slot):
        return pltpu.make_async_remote_copy(
            src_ref=source,
            dst_ref=self.wholes[item].at[place],
            send_sem=self.send_sem.at[item, slot],
            recv_sem=self.recv_sem.at[item, slot],
            device_id={dp_axis: peer},
            device_id_type=MESH,
        )

    def send(self, *arguments):
        self.sent.append(self.copy(*arguments))
        self.sent[-1].start()

    def begin(self):
        for item in self.items:
            self.send(item, self.shares[item], self.rank, self.ahead, 0)
            self.send(item, self.shares[item], self.rank, self.beside, 4)
            self.own[item].start()

    def advance(self, step):
        place = 2 * lax.rem(self.high + 4 - step, 4) + self.low
        for item in self.items:
            source = self.wholes[item].at[place]
            self.copy(item, source, place, self.ahead, step - 1).wait_recv()
            if step < 3:
                self.send(item, source, place, self.ahead, step)
            self.send(item, source, place, self.beside, 4 + step)

    def finish(self):
        for step in range(4):
            place = 2 * lax.rem(self.high + 4 - step, 4) + 1 - self.low
            for item in self.items:
                source = self.wholes[item].at[place]
                self.copy(item, source, place, self.beside, 4 + step).wait_recv()
        for sent in self.sent:
            sent.wait_send()
        for kept in self.own:
            kept.wait()


def ring_scratch(count):
    return [
        pltpu.SemaphoreType.DMA((count,)),
        pltpu.SemaphoreType.DMA((count, 8)),
        pltpu.SemaphoreType.DMA((count, 8)),
    ]


def sum_kernel(count, cross_type, *refs):
    partial, shares = refs[0], refs[1 : 1 + count]
    total, wholes = refs[1 + count], refs[2 + count : 2 + 2 * count]
    near, pair, far, send_sem, recv_sem = refs[2 + 2 * count : 7 + 2 * count]
    rank = lax.axis_index(tensor_axis)
    low = lax.rem(rank, 2)
    partner, across = rank + 1 - 2 * low, lax.rem(rank + 2, 4)
    ring = RingGather(shares, wholes, *refs[7 + 2 * count :]) if count else None
    barrier = pltpu.get_barrier_semaphore()
    for peer in (partner, across):
        pl.semaphore_signal(barrier, inc=1, device_id={tensor_axis: peer}, device_id_type=MESH)
    if ring:
        for peer in (ring.beside, ring.behind):
            pl.semaphore_signal(barrier, inc=1, device_id={dp_axis: peer}, device_id_type=MESH)
    pl.semaphore_wait(barrier, 4 if ring else 2)
    half = partial.shape[0] // 2
    mine = pl.ds(pl.multiple_of(low * half, 8), half)
    others = pl.ds(pl.multiple_of((1 - low) * half, 8), half)

    def copy(source, target, peer, slot):
        return pltpu.make_async_remote_copy(
            src_ref=source,
            dst_ref=target,
            send_sem=send_sem.at[slot],
            recv_sem=recv_sem.at[slot],
            device_id={tensor_axis: peer},
            device_id_type=MESH,
        )

    give = copy(partial.at[others], near, partner, 0)
    cross = copy(pair, far, across, 1)
    back = copy(total.at[mine], total.at[mine], partner, 2)
    give.start()
    if ring:
        ring.begin()
    give.wait()
    pair[...] = (partial[mine, :] + near[...]).astype(cross_type)
    cross.start()
    if ring:
        ring.advance(1)
        ring.advance(2)
    cross.wait()
    total[mine, :] = pair[...].astype(jnp.float32) + far[...].astype(jnp.float32)
    back.start()
    if ring:
        ring.advance(3)
    back.wait()
    if ring:
        ring.finish()


def tensor_sum(partial_term, cross_type, kernel, shares=()):
    ring_here = lax.axis_size(dp_axis) == 8
    wholes = [] if ring_here else [lax.all_gather(share, dp_axis) for share in shares]
    shares = shares if ring_here else ()
    if lax.axis_size(tensor_axis) != 4:
        return lax.psum(partial_term, tensor_axis), wholes
    rows, columns = partial_term.shape
    count = len(shares)
    vmem, anywhere = pl.BlockSpec(memory_space=pltpu.VMEM), pl.BlockSpec(memory_space=pl.ANY)
    outs = pl.pallas_call(
        functools.partial(sum_kernel, count, cross_type),
        out_shape=[jax.ShapeDtypeStruct(partial_term.shape, jnp.float32)]
        + [jax.ShapeDtypeStruct((8,) + share.shape, share.dtype) for share in shares],
        in_specs=[vmem] + [anywhere] * count,
        out_specs=[vmem] + [anywhere] * count,
        scratch_shapes=[
            pltpu.VMEM((rows // 2, columns), jnp.float32),
            pltpu.VMEM((rows // 2, columns), cross_type),
            pltpu.VMEM((rows // 2, columns), cross_type),
            pltpu.SemaphoreType.DMA((3,)),
            pltpu.SemaphoreType.DMA((3,)),
        ]
        + (ring_scratch(count) if count else []),
        compiler_params=pltpu.CompilerParams(
            collective_id=kernel, has_side_effects=True, vmem_limit_bytes=16 << 20
        ),
        cost_estimate=pl.CostEstimate(flops=0, bytes_accessed=2_000_000, transcendentals=0),
    )(partial_term, *shares)
    return outs[0], outs[1:] if ring_here else wholes


def branch_sum(partial_term, kernel, shares=()):
    return tensor_sum(partial_term, jnp.bfloat16, kernel, shares)


def spread(block, slots, axis, send_sem, recv_sem):
    rank, size = lax.axis_index(axis), lax.axis_size(axis)
    copies = []
    for step in range(1, size):
        peer = lax.rem(rank + step, size)
        copies.append(
            pltpu.make_async_remote_copy(
                src_ref=block,
                dst_ref=slots.at[rank],
                send_sem=send_sem.at[step - 1],
                recv_sem=recv_sem.at[step - 1],
                device_id={axis: peer},
                device_id_type=MESH,
            )
        )
        copies[-1].start()
    return copies


def greet(barrier, axes):
    count = 0
    for axis in axes:
        rank, size = lax.axis_index(axis), lax.axis_size(axis)
        for step in range(1, size):
            peer = lax.rem(rank + step, size)
            pl.semaphore_signal(barrier, inc=1, device_id={axis: peer}, device_id_type=MESH)
            count += 1
    pl.semaphore_wait(barrier, count)


def small_sum_kernel(value, total, middle, near, far, near_send, near_recv, far_send, far_recv):
    greet(pltpu.get_barrier_semaphore(), (tensor_axis, dp_axis))
    near[lax.axis_index(tensor_axis)] = value[...]
    for copy in spread(value, near, tensor_axis, near_send, near_recv):
        copy.wait()
    middle[...] = functools.reduce(jnp.add, [near[slot] for slot in range(near.shape[0])])
    far[lax.axis_index(dp_axis)] = middle[...]
    for copy in spread(middle, far, dp_axis, far_send, far_recv):
        copy.wait()
    total[...] = functools.reduce(jnp.add, [far[slot] for slot in range(far.shape[0])])


def small_sums(values):
    sizes = [lax.axis_size(tensor_axis), lax.axis_size(dp_axis)]
    if max(sizes) > 8:
        return sum_everywhere(jnp.stack(values), (tensor_axis, dp_axis))
    rows = lax.broadcasted_iota(jnp.int32, (8, 128), 0)
    block = jnp.zeros((8, 128), jnp.float32)
    for row, value in enumerate(values):
        block = jnp.where(rows == row, value, block)
    scratch = [pltpu.VMEM((8, 128), jnp.float32)]
    scratch += [pltpu.VMEM((size, 8, 128), jnp.float32) for size in sizes]
    for size in sizes:
        scratch += [pltpu.SemaphoreType.DMA((size - 1,))] * 2
    total = pl.pallas_call(
        small_sum_kernel,
        out_shape=jax.ShapeDtypeStruct((8, 128), jnp.float32),
        in_specs=[pl.BlockSpec(memory_space=pltpu.VMEM)],
        out_specs=pl.BlockSpec(memory_space=pltpu.VMEM),
        scratch_shapes=scratch,
        compiler_params=pltpu.CompilerParams(
            collective_id=last_sums_kernel, has_side_effects=True
        ),
    )(block)
    return total[:, 0]


def tensor_blocks(piece):
    if lax.axis_size(tensor_axis) != 4:
        return list(lax.all_gather(piece, tensor_axis))
    rank = lax.axis_index(tensor_axis)
    near = swap(piece, tensor_axis, 1)
    far = swap(piece, tensor_axis, 2)
    cross = swap(far, tensor_axis, 1)
    blocks = []
    for index in range(4):
        same_pair = jnp.where(rank == index, piece, near)
        other_pair = jnp.where(rank == index ^ 2, far, cross)
        blocks.append(jnp.where(rank // 2 == index // 2, same_pair, other_pair))
    return blocks


def tensor_columns(piece):
    return jnp.concatenate(tensor_blocks(piece), axis=1)


def sum_everywhere(value, axes):
    for axis in axes:
        step = 1
        while step < lax.axis_size(axis):
            value = value + swap(value, axis, step)
            step = 2 * step
    return value


def pick(blocks, index):
    return lax.dynamic_index_in_dim(blocks, index, 0, keepdims=False)


def bound_level(pairs):
    bounds = [
        left.shape[0]
        * jnp.max(jnp.abs(left.astype(jnp.float32)))
        * jnp.max(jnp.abs(right.astype(jnp.float32)))
        for left, right in pairs
    ]
    return jnp.ceil(jnp.log2(jnp.maximum(functools.reduce(jnp.maximum, bounds), 2.0**-100)))


def coded(values, level):
    rows = values.shape[0]
    padded = jnp.pad(values * jnp.exp2(13.0 - level), ((0, 16), (0, 0)))
    is_value = lax.broadcasted_iota(jnp.int32, padded.shape, 0) < rows
    return jnp.where(is_value, padded, level).astype(jnp.float16)


class Scattered:
    def __init__(self, pairs, first=0):
        self.pairs, self.first = pairs, max(first, 0)
        self.count = 4 - first if first >= 0 else -first
        self.got, self.parts = None, None
        self.level = bound_level(pairs)
        self.product = None

    def grad(self):
        if self.product is None:
            self.product = jnp.concatenate(
                [product_left(left, right) for left, right in self.pairs], axis=0
            )
        return self.product

    def slab(self):
        return self.grad().shape[0] // (2 * self.count)

    def near_message(self):
        grad, slab = self.grad(), self.slab()
        low = lax.axis_index(dp_axis) % 2
        blocks = grad.reshape(self.count, 2 * slab, grad.shape[1])
        give = lax.dynamic_slice_in_dim(blocks, (1 - low) * slab, slab, 1)
        return coded(give.reshape(-1, grad.shape[1]), self.level)

    def send_near(self, message):
        self.got = swap(message, dp_axis, 1)

    def got_level(self):
        return self.got[self.count * self.slab(), 0].astype(jnp.float32)

    def share(self, place):
        grad, slab = self.grad(), self.slab()
        low = lax.axis_index(dp_axis) % 2
        place = jnp.clip(place - self.first, 0, self.count - 1)
        kept = lax.dynamic_slice_in_dim(grad, (2 * place + low) * slab, slab, 0)
        arrived = lax.dynamic_slice_in_dim(self.got, place * slab, slab, 0)
        return kept + arrived.astype(jnp.float32) * jnp.exp2(self.got_level() - 13.0)

    def far_messages(self):
        high = lax.axis_index(dp_axis) // 2
        level = jnp.maximum(self.level, self.got_level()) + 1.0
        return [coded(self.share(high ^ step), level) for step in (1, 2, 3)]

    def send_far(self, messages):
        self.parts = []
        for step, message in zip((1, 2, 3), messages):
            pairs = [
                (2 * source + side, 2 * (source ^ step) + side)
                for source in range(4)
                for side in range(2)
                if self.first <= source ^ step < self.first + self.count
            ]
            self.parts.append(lax.ppermute(message, dp_axis, pairs))

    def total(self):
        if lax.axis_size(dp_axis) != 8:
            return lax.psum_scatter(self.grad(), dp_axis, scatter_dimension=0, tiled=True)
        slab = self.slab()
        total = self.share(lax.axis_index(dp_axis) // 2)
        for part in self.parts:
            level = part[slab, 0].astype(jnp.float32)
            total = total + part[:slab].astype(jnp.float32) * jnp.exp2(level - 13.0)
        return total


class Traffic:
    def __init__(self, plan):
        self.plan, self.groups = plan, {}

    def add(self, name, group):
        self.groups[name] = group
        return group

    def tie(self, value, near, far, arrived):
        near_messages = [group.near_message() for group in near]
        far_messages = [group.far_messages() for group in far]
        parts = [group.parts for group in arrived]
        value, near_messages, far_messages, parts = lax.optimization_barrier(
            (value, near_messages, far_messages, parts)
        )
        for group, message in zip(near, near_messages):
            group.send_near(message)
        for group, messages in zip(far, far_messages):
            group.send_far(messages)
        for group, part in zip(arrived, parts):
            group.parts = part
        return value

    def input_sum(self, partial_term, kernel):
        if lax.axis_size(dp_axis) != 8:
            return tensor_sum(partial_term, jnp.bfloat16, kernel)[0]
        near, far, arrived = [[self.groups[group] for group in part] for part in self.plan[kernel]]
        partial_term = self.tie(partial_term, near, [], [])
        total = tensor_sum(partial_term, jnp.bfloat16, kernel)[0]
        return self.tie(total, [], far, arrived)

    def finish(self, value, names):
        if lax.axis_size(dp_axis) != 8:
            return value
        return self.tie(value, [], [self.groups[name] for name in names], [])


def first_kernel(count, images, *refs):
    notes, class_table, shares = refs[0], refs[1], refs[2 : 2 + count]
    all_notes, classes, wholes = refs[2 + count], refs[3 + count], refs[4 + count : 4 + 2 * count]
    found, note_send, note_recv, class_send, class_recv, own_sem = refs[
        4 + 2 * count : 10 + 2 * count
    ]
    greet(pltpu.get_barrier_semaphore(), (dp_axis,))
    rank = lax.axis_index(dp_axis)
    ring = RingGather(shares, wholes, *refs[10 + 2 * count :])
    note_copies = spread(notes, all_notes, dp_axis, note_send, note_recv)
    all_notes[rank] = notes[...]
    ring.begin()
    for copy in note_copies:
        copy.wait()
    place = lax.broadcasted_iota(jnp.int32, class_table.shape, 1).astype(jnp.float32)
    lane = lax.broadcasted_iota(jnp.int32, found.shape, 1)
    columns = jnp.zeros(found.shape, jnp.float32)
    for image in range(8 * images):
        label = all_notes[image // images, 0:1, image % images : image % images + 1]
        value = jnp.sum(
            jnp.where(place == label, class_table[...], 0.0), axis=1, keepdims=True
        )
        columns = jnp.where(lane == image, value, columns)
    found[...] = columns
    own = pltpu.make_async_copy(found, classes.at[rank], own_sem.at[0])
    own.start()
    class_copies = spread(found, classes, dp_axis, class_send, class_recv)
    for step in (1, 2, 3):
        ring.advance(step)
    ring.finish()
    for copy in class_copies:
        copy.wait()
    own.wait()


def gather_first(notes, class_table, images, shares):
    count = len(shares)
    rows = class_table.shape[0]
    vmem, anywhere = pl.BlockSpec(memory_space=pltpu.VMEM), pl.BlockSpec(memory_space=pl.ANY)
    outs = pl.pallas_call(
        functools.partial(first_kernel, count, images),
        out_shape=[
            jax.ShapeDtypeStruct((8, 8, 128), jnp.float32),
            jax.ShapeDtypeStruct((8, rows, 128), jnp.float32),
        ]
        + [jax.ShapeDtypeStruct((8,) + share.shape, share.dtype) for share in shares],
        in_specs=[vmem, vmem] + [anywhere] * count,
        out_specs=[vmem, vmem] + [anywhere] * count,
        scratch_shapes=[pltpu.VMEM((rows, 128), jnp.float32)]
        + [pltpu.SemaphoreType.DMA((7,))] * 4
        + [pltpu.SemaphoreType.DMA((1,))]
        + ring_scratch(count),
        compiler_params=pltpu.CompilerParams(
            collective_id=first_gather, has_side_effects=True, vmem_limit_bytes=16 << 20
        ),
    )(notes, class_table, *shares)
    return outs[0], outs[1], outs[2:]


def scatter_small(grad):
    if lax.axis_size(dp_axis) != 8:
        return lax.psum_scatter(grad, dp_axis, scatter_dimension=0, tiled=True)
    rank = lax.axis_index(dp_axis)
    low, high = rank % 2, rank // 2
    slab, columns = grad.shape[0] // 8, grad.shape[1]
    blocks = grad.reshape(4, 2 * slab, columns)
    keep = lax.dynamic_slice_in_dim(blocks, low * slab, slab, 1)
    give = lax.dynamic_slice_in_dim(blocks, (1 - low) * slab, slab, 1)
    pairs = keep + swap(give, dp_axis, 1)
    total = pick(pairs, high)
    for step in (1, 2, 3):
        total = total + swap(pick(pairs, high ^ step), dp_axis, 2 * step)
    return total


def take_pieces(vector, starts, counts):
    return jnp.concatenate(
        [lax.dynamic_slice_in_dim(vector, start, count) for start, count in zip(starts, counts)]
    )


def place_pieces(total, pieces, starts):
    full = jnp.zeros((total,), jnp.float32)
    for piece, start in zip(pieces, starts):
        full = lax.dynamic_update_slice_in_dim(full, piece, start, 0)
    return full


def score_block(queries, key_rows, visible):
    scores = jnp.einsum(
        "bqhd,bkhd->bhqk", queries, key_rows, preferred_element_type=jnp.float32
    ) * HEAD ** (-0.5)
    return scores + (visible[:, None, None, :] - 1.0) * 1000000000.0


def attention(queries, key_rows, value_rows, visible):
    scores = score_block(queries, key_rows, visible)
    largest = jnp.max(scores, axis=-1, keepdims=True)
    exponent = jnp.exp(scores - largest)
    normaliser = jnp.sum(exponent, axis=-1, keepdims=True)
    chance = narrow(exponent / normaliser)
    attended = narrow(
        jnp.einsum("bhqk,bkhd->bqhd", chance, value_rows, preferred_element_type=jnp.float32)
    )
    return (attended, largest + jnp.log(normaliser))


def attention_back(queries, key_rows, value_rows, visible, log_total, grad_attended):
    chance = jnp.exp(score_block(queries, key_rows, visible) - log_total)
    grad_values = jnp.einsum(
        "bhqk,bqhd->bkhd", narrow(chance), grad_attended, preferred_element_type=jnp.float32
    )
    grad_chance = jnp.einsum(
        "bqhd,bkhd->bhqk", grad_attended, value_rows, preferred_element_type=jnp.float32
    )
    grad_scores = narrow(
        chance * (grad_chance - jnp.sum(chance * grad_chance, axis=-1, keepdims=True))
    )
    grad_queries = jnp.einsum(
        "bhqk,bkhd->bqhd", grad_scores, key_rows, preferred_element_type=jnp.float32
    ) * HEAD ** (-0.5)
    grad_keys = jnp.einsum(
        "bhqk,bqhd->bkhd", grad_scores, queries, preferred_element_type=jnp.float32
    ) * HEAD ** (-0.5)
    return (grad_queries, grad_keys, grad_values)


def block_forward(
    stream, visible, layer_rows, layer_bias, vectors, kernel, first_shares, last_shares
):
    images = visible.shape[0]
    local_width = D // lax.axis_size(tensor_axis)
    local_ff = FF // lax.axis_size(tensor_axis)
    heads_here = local_width // HEAD
    flat = stream.reshape(-1, D)
    normed = narrow(layer_norm(flat, vectors[0], vectors[1]))
    mixed = narrow(
        product_right(normed, layer_rows[: 3 * local_width]) + layer_bias[: 3 * local_width]
    )
    parts = [
        mixed[:, slot * local_width : (slot + 1) * local_width].reshape(
            images, -1, heads_here, HEAD
        )
        for slot in range(3)
    ]
    attended, log_total = attention(parts[0], parts[1], parts[2], visible)
    attended = attended.reshape(-1, local_width)
    branch, first_wholes = branch_sum(
        product(attended, layer_rows[3 * local_width + local_ff : 4 * local_width + local_ff]),
        kernel,
        first_shares,
    )
    middle = flat + branch + vectors[4]
    second = narrow(layer_norm(middle, vectors[2], vectors[3]))
    inner = (
        product_right(second, layer_rows[3 * local_width : 3 * local_width + local_ff])
        + layer_bias[3 * local_width :]
    )
    active = narrow(exact_gelu(inner))
    branch, last_wholes = branch_sum(
        product(active, layer_rows[4 * local_width + local_ff :]), kernel + 1, last_shares
    )
    result = middle + branch + vectors[5]
    return (
        result.reshape(stream.shape),
        (flat, normed, parts, log_total, attended, middle, second, inner, active),
        first_wholes,
        last_wholes,
    )


def block_back(incoming, visible, layer_rows, vectors, stored, kernel, traffic):
    flat, normed, parts, log_total, attended, middle, second, inner, active = stored
    local_width = D // lax.axis_size(tensor_axis)
    local_ff = FF // lax.axis_size(tensor_axis)
    mix_rows = layer_rows[: 3 * local_width]
    up_rows = layer_rows[3 * local_width : 3 * local_width + local_ff]
    proj_rows = layer_rows[3 * local_width + local_ff : 4 * local_width + local_ff]
    down_rows = layer_rows[4 * local_width + local_ff :]
    flow = incoming.reshape(-1, D)
    grad_branch = narrow(flow)
    grad_active = product_right(grad_branch, down_rows)
    grad_inner = narrow(local_back(exact_gelu, inner, grad_active))
    grad_second = traffic.input_sum(product(grad_inner, up_rows), kernel)
    grad_middle, grad_gain_two, grad_shift_two = jax.vjp(
        layer_norm, middle, vectors[2], vectors[3]
    )[1](grad_second)
    grad_middle = flow + grad_middle
    grad_attn = narrow(grad_middle)
    grad_attended = narrow(product_right(grad_attn, proj_rows)).reshape(parts[0].shape)
    grads_mixed = attention_back(parts[0], parts[1], parts[2], visible, log_total, grad_attended)
    grad_mixed = narrow(
        jnp.concatenate([piece.reshape(-1, local_width) for piece in grads_mixed], axis=1)
    )
    mix = [(grad_mixed, normed)]
    later = [(grad_inner, second), (attended, grad_attn), (active, grad_branch)]
    if kernel == back_encoder and lax.axis_size(dp_axis) == 8:
        owned_rows = [
            traffic.add(mix_group, Scattered(mix, -1)),
            traffic.add(kernel, Scattered(later, 1)),
        ]
    else:
        owned_rows = [traffic.add(kernel, Scattered(mix + later))]
    grad_normed = traffic.input_sum(product(grad_mixed, mix_rows), kernel + 1)
    grad_flat, grad_gain_one, grad_shift_one = jax.vjp(layer_norm, flat, vectors[0], vectors[1])[1](
        grad_normed
    )
    grad_bias = jnp.concatenate([column_sum(grad_mixed), column_sum(grad_inner)])
    grad_vectors = jnp.stack(
        [
            grad_gain_one,
            grad_shift_one,
            grad_gain_two,
            grad_shift_two,
            column_sum(grad_attn),
            column_sum(grad_branch),
        ]
    )
    return ((grad_middle + grad_flat).reshape(incoming.shape), owned_rows, grad_bias, grad_vectors)


def gathered_parts(columns, count):
    width = columns.shape[1] // count
    blocks = [block.astype(jnp.float32) for block in tensor_blocks(narrow(columns))]
    return [
        jnp.concatenate([block[:, slot * width : (slot + 1) * width] for block in blocks], axis=1)
        for slot in range(count)
    ]


def adaptive_vectors(cond_act, segment_rows, segment_bias):
    local_hidden = HW // lax.axis_size(tensor_axis)
    adaptive = (
        product_right(cond_act, segment_rows[: 3 * local_hidden]) + segment_bias[: 3 * local_hidden]
    )
    return gathered_parts(adaptive, 3)


def head_block(hidden_state, vectors, segment_rows, segment_bias, last_bias, kernel):
    local_hidden = HW // lax.axis_size(tensor_axis)
    shift_vec, scale_vec, gate_vec = vectors
    modulated = narrow(modulate(hidden_state, shift_vec, scale_vec))
    inner = (
        product_right(modulated, segment_rows[3 * local_hidden : 4 * local_hidden])
        + segment_bias[3 * local_hidden :]
    )
    active = narrow(jax.nn.silu(inner))
    branch = branch_sum(product(active, segment_rows[4 * local_hidden :]), kernel)[0] + last_bias
    return (
        hidden_state + gate_vec * branch,
        (hidden_state, shift_vec, scale_vec, gate_vec, modulated, inner, active, branch),
    )


def head_block_back(incoming, cond_act, segment_rows, offset, stored, kernel, traffic):
    hidden_state, shift_vec, scale_vec, gate_vec, modulated, inner, active, branch = stored
    local_hidden = HW // lax.axis_size(tensor_axis)
    grad_gate = incoming * branch
    grad_branch = narrow(incoming * gate_vec)
    grad_active = product_right(grad_branch, segment_rows[4 * local_hidden :])
    grad_inner = narrow(local_back(jax.nn.silu, inner, grad_active))
    grad_modulated = traffic.input_sum(
        product(grad_inner, segment_rows[3 * local_hidden : 4 * local_hidden]), kernel
    )
    grad_hidden, grad_shift, grad_scale = jax.vjp(modulate, hidden_state, shift_vec, scale_vec)[1](
        grad_modulated
    )
    grad_adaptive = narrow(
        jnp.concatenate(
            [
                lax.dynamic_slice_in_dim(piece, offset, local_hidden, 1)
                for piece in (grad_shift, grad_scale, grad_gate)
            ],
            axis=1,
        )
    )
    grad_cond = product(grad_adaptive, segment_rows[: 3 * local_hidden])
    owned_rows = traffic.add(
        kernel,
        Scattered([(grad_adaptive, cond_act), (grad_inner, modulated), (active, grad_branch)]),
    )
    grad_bias = jnp.concatenate([column_sum(grad_adaptive), column_sum(grad_inner)])
    return (incoming + grad_hidden, grad_cond, owned_rows, grad_bias, column_sum(grad_branch))


def adam_update(weight, moment_one, moment_two, gradient, factor, step_num):
    gradient = gradient * factor
    moment_one = beta_first * moment_one + (1.0 - beta_first) * gradient
    moment_two = beta_second * moment_two + (1.0 - beta_second) * gradient * gradient
    fixed_one = moment_one / (1.0 - beta_first**step_num)
    fixed_two = moment_two / (1.0 - beta_second**step_num)
    weight = weight - learn_rate * (
        fixed_one / (jnp.sqrt(fixed_two) + adam_eps) + decay_rate * weight
    )
    return (weight, moment_one, moment_two)


def local(
    block_weights,
    head_weights,
    head_rest,
    embed_tables,
    bias_rows,
    first_blocks,
    second_blocks,
    first_head,
    second_head,
    first_rest,
    second_rest,
    first_tables,
    second_tables,
    first_bias,
    second_bias,
    patches,
    noise,
    token_mask,
    labels,
    drop_marks,
    timesteps,
    step_weights,
    step_count,
):
    tensor_size = lax.axis_size(tensor_axis)
    tensor_index = lax.axis_index(tensor_axis)
    local_width = D // tensor_size
    local_ff = FF // tensor_size
    local_hidden = HW // tensor_size
    offset = tensor_index * local_hidden
    column_starts = [slot * D + tensor_index * local_width for slot in range(3)] + [
        3 * D + tensor_index * local_ff
    ]
    column_counts = [local_width] * 3 + [local_ff]
    head_starts = [slot * HW + offset for slot in range(4)]
    dp_size = lax.axis_size(dp_axis)
    dp_index = lax.axis_index(dp_axis)
    images = patches.shape[0]
    all_images = dp_size * images
    mask_float = token_mask.astype(jnp.float32)
    matches = timesteps[..., None] == jnp.arange(T_STEPS)
    row_weight = (
        jnp.sum(jnp.where(matches, step_weights, 0.0), axis=-1) * mask_float[None]
    ).reshape(-1)
    chosen = jnp.where(drop_marks == 1, CLASSES, labels)
    class_at = TOKD + 1
    class_end = class_at + CLASSES + 1
    weight_here = jnp.sum(row_weight)
    table_share = jnp.concatenate(
        [embed_tables[:, :class_at], embed_tables[:, class_end:]], axis=1
    )
    class_share = embed_tables[:, class_at:class_end]
    block_share = narrow(block_weights)
    if dp_size == 8:
        notes = jnp.zeros((8, 128), jnp.float32)
        notes = lax.dynamic_update_slice(notes, chosen.astype(jnp.float32)[None], (0, 0))
        notes = lax.dynamic_update_slice(notes, weight_here[None, None], (1, 0))
        all_notes, classes, (table_cols, first_block) = gather_first(
            notes, class_share, images, [table_share, block_share[0]]
        )
        all_chosen = all_notes[:, 0, :images].reshape(-1)
        weight_total = jnp.sum(all_notes[:, 1, 0])
        class_rows = lax.dynamic_slice_in_dim(
            classes.reshape(-1, classes.shape[-1]), dp_index * images, images, 1
        ).T
    else:
        all_chosen = lax.all_gather(chosen, dp_axis, axis=0, tiled=True).astype(jnp.float32)
        weight_total = lax.psum(weight_here, dp_axis)
        table_cols = lax.all_gather(table_share, dp_axis)
        first_block = lax.all_gather(block_share[0], dp_axis)
    picker = (all_chosen[:, None] == jnp.arange(CLASSES + 1)[None, :]).astype(jnp.float32)
    if dp_size != 8:
        found = lax.dot_general(
            class_share, picker, (((1,), (1,)), ((), ())), precision=highest
        )
        class_rows = lax.dynamic_slice_in_dim(
            lax.all_gather(found, dp_axis, axis=0, tiled=True), dp_index * images, images, 1
        ).T
    table_cols = table_cols.reshape(-1, table_cols.shape[-1])
    first_block = first_block.reshape(-1, D)
    share_rows = block_share[1].shape[0] // 2
    rest_share = narrow(head_rest)
    rest_rows_here = rest_share.shape[0] // 2
    flat_bias = bias_rows.reshape(-1)
    rest_bias = flat_bias[: 6 * HW].reshape(6, HW)
    head_bias = flat_bias[6 * HW : 6 * HW + 5 * HB * HW].reshape(HB, 5 * HW)
    column_bias = flat_bias[6 * HW + 5 * HB * HW :].reshape(LAYERS, 3 * D + FF)
    table_parts = cut_rows(table_cols.T, (TOKD, 1, TOK + BUF, TOK + BUF, 1, 6 * LAYERS, 4))
    layer_vectors = table_parts[5].reshape(LAYERS, 6, D)
    final_norms = table_parts[6]
    patch_flat = patches.reshape(-1, TOKD)
    tokens = product(patch_flat, narrow(table_parts[0])) + table_parts[1][0]
    stream = (
        jnp.concatenate(
            [
                jnp.broadcast_to(class_rows[:, None, :], (images, BUF, D)),
                tokens.reshape(images, TOK, D),
            ],
            axis=1,
        )
        + table_parts[2]
    )
    buffer_ones = jnp.ones((images, BUF), jnp.float32)
    visible_enc = jnp.concatenate([buffer_ones, 1.0 - mask_float], axis=1)
    visible_all = jnp.ones((images, TOK + BUF), jnp.float32)
    hidden_rows = jnp.concatenate([0.0 * buffer_ones, mask_float], axis=1)[..., None]
    layer_bias = [
        take_pieces(column_bias[layer], column_starts, column_counts) for layer in range(LAYERS)
    ]
    encoded, stored_enc, first_half, last_half = block_forward(
        stream,
        visible_enc,
        first_block,
        layer_bias[0],
        layer_vectors[0],
        encoder_forward,
        [block_share[1][:share_rows]],
        [block_share[1][share_rows:]],
    )
    encoded, head_share = lax.optimization_barrier((encoded, narrow(head_weights)))
    head_all = lax.all_gather(head_share, dp_axis, axis=1, tiled=True)
    second_block = jnp.concatenate([first_half[0], last_half[0]], axis=1).reshape(-1, D)
    block_all = [first_block, second_block]
    enc_normed = layer_norm(encoded, final_norms[0], final_norms[1])
    decoder_in = enc_normed * (1.0 - hidden_rows) + table_parts[4][0] * hidden_rows + table_parts[3]
    decoded, stored_dec, first_half, last_half = block_forward(
        decoder_in,
        visible_all,
        second_block,
        layer_bias[1],
        layer_vectors[1],
        decoder_forward,
        [rest_share[:rest_rows_here]],
        [rest_share[rest_rows_here:]],
    )
    rest_rows = jnp.concatenate([first_half[0], last_half[0]], axis=1)
    rest_rows = rest_rows.reshape(-1, rest_rows.shape[-1])
    cond_mine, input_mine, output_mine, time_first, second_mine, final_shift, final_scale = cut_rows(
        rest_rows, (D, TOKD, TOKD, HW, HW, HW, HW)
    )
    cond_weight, input_weight, output_weight, time_second = cut_rows(
        tensor_columns(jnp.concatenate([cond_mine, input_mine, output_mine, second_mine], axis=0)),
        (D, TOKD, TOKD, HW),
    )
    latent = narrow(layer_norm(decoded, final_norms[2], final_norms[3])[:, BUF:].reshape(-1, D))
    condition = product(latent, cond_weight) + rest_bias[0]
    step_rows = timesteps.reshape(COPIES, -1)
    time_feat = narrow(sinusoid(step_rows).reshape(-1, HW))
    time_pre = product(time_feat, time_first) + lax.dynamic_slice_in_dim(
        rest_bias[2], offset, local_hidden
    )
    time_act = tensor_columns(narrow(jax.nn.silu(time_pre)))
    time_embed = product(time_act, time_second) + rest_bias[3]
    cond_vec = (condition[None] + time_embed.reshape(COPIES, -1, HW)).reshape(-1, HW)
    cond_act = narrow(jax.nn.silu(cond_vec))
    phase = step_rows.astype(jnp.float32)[..., None] * (math.pi / (2 * T_STEPS))
    signal_coef = jnp.cos(phase)
    noise_coef = jnp.sin(phase)
    clean = patch_flat.astype(jnp.float32)[None]
    noise_rows = noise.reshape(COPIES, -1, TOKD).astype(jnp.float32)
    noisy_rows = narrow((signal_coef * clean + noise_coef * noise_rows).reshape(-1, TOKD))
    target = (signal_coef * noise_rows - noise_coef * clean).reshape(-1, TOKD)
    hidden_state = product(noisy_rows, input_weight) + rest_bias[1]
    stored_head = []
    segment_biases = [
        take_pieces(head_bias[segment], head_starts, [local_hidden] * 4) for segment in range(HB)
    ]
    head_vectors = [
        adaptive_vectors(cond_act, head_all[segment], segment_biases[segment])
        for segment in range(HB)
    ]
    last_pair = jnp.concatenate(
        [product(cond_act, final_shift), product(cond_act, final_scale)], axis=1
    ) + take_pieces(flat_bias, [4 * HW + offset, 5 * HW + offset], [local_hidden] * 2)
    shift_last, scale_last = gathered_parts(last_pair, 2)
    for segment in range(HB):
        hidden_state, stored = head_block(
            hidden_state,
            head_vectors[segment],
            head_all[segment],
            segment_biases[segment],
            head_bias[segment, 4 * HW :],
            head_forward + segment,
        )
        stored_head.append(stored)
    final_in = narrow(modulate(hidden_state, shift_last, scale_last))
    predicted = product_right(final_in, output_weight)
    sq_error = jnp.mean((predicted - target) ** 2, axis=-1)
    numerator = jnp.sum(row_weight * sq_error)
    grad_pred = narrow(2.0 / (TOKD * weight_total) * row_weight[:, None] * (predicted - target))
    grad_final = product(grad_pred, output_weight)
    grad_hidden, grad_shift_last, grad_scale_last = jax.vjp(
        modulate, hidden_state, shift_last, scale_last
    )[1](grad_final)

    def own_columns(value):
        return lax.dynamic_slice_in_dim(value, offset, local_hidden, 1)

    grad_shift_last = narrow(own_columns(grad_shift_last))
    grad_scale_last = narrow(own_columns(grad_scale_last))
    traffic = Traffic(
        {
            back_head + 1: ([], [], []),
            back_head: ([back_head + 1], [], []),
            back_cond: ([back_head], [back_head + 1], []),
            back_decoder: ([rest_group], [back_head], [back_head + 1]),
            back_decoder + 1: ([back_decoder], [rest_group], [back_head]),
            back_encoder: ([], [back_decoder], [rest_group]),
            back_encoder + 1: ([back_encoder, mix_group], [back_encoder], [back_decoder]),
        }
    )
    cond_split = product_right(grad_shift_last, final_shift) + product_right(
        grad_scale_last, final_scale
    )
    head_grads = []
    head_bias_grads = []
    for segment in reversed(range(HB)):
        grad_hidden, grad_cond, grad_segment, grad_segment_bias, grad_last_bias = head_block_back(
            grad_hidden,
            cond_act,
            head_all[segment],
            offset,
            stored_head[segment],
            back_head + segment,
            traffic,
        )
        cond_split = cond_split + grad_cond
        head_grads.insert(0, grad_segment)
        pieces = [
            grad_segment_bias[slot * local_hidden : (slot + 1) * local_hidden] for slot in range(4)
        ] + [grad_last_bias / tensor_size]
        head_bias_grads.insert(0, place_pieces(5 * HW, pieces, head_starts + [4 * HW]))
    grad_input = narrow(grad_hidden)
    grad_cond_vec = narrow(local_back(jax.nn.silu, cond_vec, traffic.input_sum(cond_split, back_cond)))
    cond_bias_grad = column_sum(grad_cond_vec)
    grad_time_act = product_right(
        grad_cond_vec, lax.dynamic_slice_in_dim(time_second, offset, local_hidden, 0)
    )
    grad_time_pre = narrow(local_back(jax.nn.silu, time_pre, grad_time_act))
    grad_latent = jnp.sum(product(grad_cond_vec, cond_weight.T).reshape(COPIES, -1, D), axis=0)
    grad_cond_mine = own_columns(grad_cond_vec)
    owned_rest = Scattered(
        [
            (jnp.tile(latent, (COPIES, 1)), grad_cond_mine),
            (noisy_rows, own_columns(grad_input)),
            (grad_pred, own_columns(final_in)),
            (time_feat, grad_time_pre),
            (time_act, grad_cond_mine),
            (cond_act, grad_shift_last),
            (cond_act, grad_scale_last),
        ]
    )
    traffic.add(rest_group, owned_rest)
    rest_bias_grad = place_pieces(
        6 * HW,
        [
            cond_bias_grad / tensor_size,
            column_sum(grad_input) / tensor_size,
            column_sum(grad_time_pre),
            cond_bias_grad / tensor_size,
            column_sum(grad_shift_last),
            column_sum(grad_scale_last),
        ],
        [0, HW, 2 * HW + offset, 3 * HW, 4 * HW + offset, 5 * HW + offset],
    )
    grad_top = jnp.concatenate(
        [jnp.zeros((images, BUF, D), jnp.float32), grad_latent.reshape(images, TOK, D)], axis=1
    )
    grad_decoded, grad_gain_dec, grad_shift_dec = jax.vjp(
        layer_norm, decoded, final_norms[2], final_norms[3]
    )[1](grad_top)
    grad_dec_in, grad_rows_dec, grad_bias_dec, grad_vec_dec = block_back(
        grad_decoded, visible_all, block_all[1], layer_vectors[1], stored_dec, back_decoder, traffic
    )
    grad_encoded, grad_gain_enc, grad_shift_enc = jax.vjp(
        layer_norm, encoded, final_norms[0], final_norms[1]
    )[1](grad_dec_in * (1.0 - hidden_rows))
    grad_stream, grad_rows_enc, grad_bias_enc, grad_vec_enc = block_back(
        grad_encoded, visible_enc, block_all[0], layer_vectors[0], stored_enc, back_encoder, traffic
    )
    grad_stream, bias_parts = traffic.finish(
        (grad_stream, [rest_bias_grad] + head_bias_grads),
        [mix_group],
    )
    grad_tokens = narrow(grad_stream[:, BUF:].reshape(-1, D))
    grad_class = lax.dynamic_update_slice_in_dim(
        jnp.zeros((all_images, D), jnp.float32),
        jnp.sum(grad_stream[:, :BUF], axis=1),
        dp_index * images,
        0,
    )
    small_rows = jnp.concatenate(
        [
            column_sum(grad_tokens)[None],
            jnp.sum(grad_dec_in * hidden_rows, axis=(0, 1))[None],
            grad_vec_enc,
            grad_vec_dec,
            jnp.stack([grad_gain_enc, grad_shift_enc, grad_gain_dec, grad_shift_dec]),
            grad_class,
        ],
        axis=0,
    )
    seq_rows = TOK + BUF
    small_at = 2 * seq_rows + TOKD
    table_count = small_at + small_rows.shape[0]
    quarter = -(-table_count // (8 * tensor_size)) * 8
    small_rows = jnp.pad(small_rows, ((0, quarter * tensor_size - table_count), (0, 0)))
    grad_tables = jnp.concatenate(
        [
            jnp.sum(grad_stream, axis=0),
            jnp.sum(grad_dec_in, axis=0),
            product_left(patch_flat, grad_tokens),
            small_rows,
        ],
        axis=0,
    )
    grad_tables = lax.dynamic_slice_in_dim(grad_tables, tensor_index * quarter, quarter, 0)
    owned_cols = tensor_columns(scatter_small(grad_tables.T))
    class_cols = small_at + 6 * LAYERS + 6
    owned_tables = jnp.concatenate(
        [
            owned_cols[:, 2 * seq_rows : small_at + 1],
            jnp.dot(
                owned_cols[:, class_cols : class_cols + all_images], picker, precision=highest
            ),
            owned_cols[:, : 2 * seq_rows],
            owned_cols[:, small_at + 1 : class_cols],
        ],
        axis=1,
    )
    encoder_shares = [group.total() for group in grad_rows_enc]
    if len(encoder_shares) == 2:
        encoder_shares = [jnp.where(dp_index < 2, encoder_shares[0], encoder_shares[1])]
    owned_blocks = jnp.stack(encoder_shares + [grad_rows_dec[0].total()])
    owned_head = jnp.stack([group.total() for group in head_grads])
    owned_rest = owned_rest.total()
    column_grads = []
    for grad_local in (grad_bias_enc, grad_bias_dec):
        pieces = [
            grad_local[slot * local_width : (slot + 1) * local_width] for slot in range(3)
        ] + [grad_local[3 * local_width :]]
        column_grads.append(place_pieces(3 * D + FF, pieces, column_starts))
    lanes = bias_rows.shape[1]
    bias_grad = sum_everywhere(
        jnp.concatenate(bias_parts + column_grads).reshape(-1, lanes), (tensor_axis, dp_axis)
    )
    split_squares = (
        jnp.sum(owned_blocks * owned_blocks)
        + jnp.sum(owned_head * owned_head)
        + jnp.sum(owned_rest * owned_rest)
    )
    shared_squares = jnp.sum(owned_tables * owned_tables) / tensor_size
    every_squares = jnp.sum(bias_grad * bias_grad) / (tensor_size * lax.axis_size(dp_axis))
    last_sums = small_sums(
        [split_squares + shared_squares + every_squares, numerator / tensor_size]
    )
    norm_square = last_sums[0]
    loss_value = last_sums[1] / weight_total
    grad_norm = jnp.sqrt(norm_square)
    factor = jnp.minimum(1.0, clip_limit / (grad_norm + 1e-06))
    step_num = step_count[0].astype(jnp.float32)
    blocks_new, blocks_first, blocks_second = adam_update(
        block_weights, first_blocks, second_blocks, owned_blocks, factor, step_num
    )
    head_new, head_first, head_second = adam_update(
        head_weights, first_head, second_head, owned_head, factor, step_num
    )
    rest_new, rest_first, rest_second = adam_update(
        head_rest, first_rest, second_rest, owned_rest, factor, step_num
    )
    tables_new, tables_first, tables_second = adam_update(
        embed_tables, first_tables, second_tables, owned_tables, factor, step_num
    )
    bias_new, bias_first, bias_second = adam_update(
        bias_rows, first_bias, second_bias, bias_grad, factor, step_num
    )
    return (
        loss_value,
        grad_norm,
        blocks_new,
        blocks_first,
        blocks_second,
        narrow(blocks_new),
        head_new,
        head_first,
        head_second,
        narrow(head_new),
        rest_new,
        rest_first,
        rest_second,
        narrow(rest_new),
        tables_new,
        tables_first,
        tables_second,
        narrow(tables_new),
        bias_new,
        bias_first,
        bias_second,
        narrow(bias_new),
    )


def solution(mesh):
    in_specs = (
        P(None, (dp_axis, tensor_axis), None),
        P(None, (dp_axis, tensor_axis), None),
        P(dp_axis, tensor_axis),
        P(dp_axis, None),
        P(),
        P(None, (dp_axis, tensor_axis), None),
        P(None, (dp_axis, tensor_axis), None),
        P(None, (dp_axis, tensor_axis), None),
        P(None, (dp_axis, tensor_axis), None),
        P(dp_axis, tensor_axis),
        P(dp_axis, tensor_axis),
        P(dp_axis, None),
        P(dp_axis, None),
        P(),
        P(),
        P(dp_axis, None, None),
        P(None, dp_axis, None, None),
        P(dp_axis, None),
        P(dp_axis),
        P(dp_axis),
        P(None, dp_axis, None),
        P(),
        P(),
    )
    out_specs = (
        P(),
        P(),
        P(None, (dp_axis, tensor_axis), None),
        P(None, (dp_axis, tensor_axis), None),
        P(None, (dp_axis, tensor_axis), None),
        P(None, (dp_axis, tensor_axis), None),
        P(None, (dp_axis, tensor_axis), None),
        P(None, (dp_axis, tensor_axis), None),
        P(None, (dp_axis, tensor_axis), None),
        P(None, (dp_axis, tensor_axis), None),
        P(dp_axis, tensor_axis),
        P(dp_axis, tensor_axis),
        P(dp_axis, tensor_axis),
        P(dp_axis, tensor_axis),
        P(dp_axis, None),
        P(dp_axis, None),
        P(dp_axis, None),
        P(dp_axis, None),
        P(),
        P(),
        P(),
        P(),
    )
    return jax.shard_map(local, mesh=mesh, in_specs=in_specs, out_specs=out_specs, check_vma=False)
```

```python
import functools
import math

import jax
import jax.numpy as jnp
from jax import lax
from jax.experimental import pallas as pl
from jax.experimental.pallas import tpu as pltpu
from jax.sharding import PartitionSpec as P

D = 768
HEAD = 64
FF = 3072
HW = 1024
TOKD = 64
CLASSES = 1000
BUF = 64
TOK = 256
T_STEPS = 1000
COPIES = 1
LAYERS = 2
HB = 2


highest = lax.Precision.HIGHEST
norm_eps = 1e-06
beta_first = 0.9
beta_second = 0.95
adam_eps = 1e-08
learn_rate = 0.02
decay_rate = 0.05
clip_limit = 0.002
dp_axis, tensor_axis = "dp", "tensor"


def layer_norm(inputs, gain_vec, offset_vec):
    average = jnp.mean(inputs, axis=-1, keepdims=True)
    centred = inputs - average
    spread = jnp.mean(centred * centred, axis=-1, keepdims=True)
    return centred * lax.rsqrt(spread + norm_eps) * gain_vec + offset_vec


def modulate(inputs, shift_vec, scale_vec):
    return layer_norm(inputs, 1.0, 0.0) * (1.0 + scale_vec) + shift_vec


def exact_gelu(inputs):
    return jax.nn.gelu(inputs, approximate=False)


def local_back(function, inputs, incoming):
    return jax.vjp(function, inputs)[1](incoming)[0]


def sinusoid(step_ids):
    half_width = HW // 2
    frequency = jnp.exp(-math.log(10000.0) * jnp.arange(half_width, dtype=jnp.float32) / half_width)
    angles = step_ids.astype(jnp.float32)[..., None] * frequency
    return jnp.concatenate([jnp.cos(angles), jnp.sin(angles)], axis=-1)


def cut_rows(packed, counts):
    pieces = []
    begin_at = 0
    for count in counts:
        pieces.append(packed[begin_at : begin_at + count])
        begin_at = begin_at + count
    return pieces


def narrow(inputs):
    return inputs.astype(jnp.bfloat16)


def product(left, right):
    return jnp.dot(left, right, preferred_element_type=jnp.float32)


def product_left(left, right):
    return lax.dot_general(
        left, right, (((0,), (0,)), ((), ())), preferred_element_type=jnp.float32
    )


def product_right(left, right):
    return lax.dot_general(
        left, right, (((1,), (1,)), ((), ())), preferred_element_type=jnp.float32
    )


def column_sum(inputs):
    return jnp.sum(inputs.astype(jnp.float32), axis=0)


def swap(value, axis, step):
    return lax.ppermute(value, axis, [(i, i ^ step) for i in range(lax.axis_size(axis))])


MESH = pl.DeviceIdType.MESH
(
    first_gather,
    last_sums_kernel,
    encoder_forward,
    decoder_forward,
    head_forward,
    back_head,
    back_cond,
    back_decoder,
    back_encoder,
    last_exchange,
) = (0, 1, 2, 4, 6, 8, 10, 11, 13, 15)
rest_group, mix_group = 100, 101


class RingGather:
    def __init__(self, shares, wholes, local_sem, send_sem, recv_sem):
        rank = lax.axis_index(dp_axis)
        self.rank, self.low, self.high = rank, lax.rem(rank, 2), lax.div(rank, 2)
        self.beside = rank + 1 - 2 * self.low
        self.ahead = 2 * lax.rem(self.high + 1, 4) + self.low
        self.behind = 2 * lax.rem(self.high + 3, 4) + self.low
        self.shares, self.wholes = shares, wholes
        self.send_sem, self.recv_sem = send_sem, recv_sem
        self.items = range(len(shares))
        self.sent = []
        self.own = [
            pltpu.make_async_copy(shares[item], wholes[item].at[rank], local_sem.at[item])
            for item in self.items
        ]

    def copy(self, item, source, place, peer, slot):
        return pltpu.make_async_remote_copy(
            src_ref=source,
            dst_ref=self.wholes[item].at[place],
            send_sem=self.send_sem.at[item, slot],
            recv_sem=self.recv_sem.at[item, slot],
            device_id={dp_axis: peer},
            device_id_type=MESH,
        )

    def send(self, *arguments):
        self.sent.append(self.copy(*arguments))
        self.sent[-1].start()

    def begin(self):
        for item in self.items:
            self.send(item, self.shares[item], self.rank, self.ahead, 0)
            self.send(item, self.shares[item], self.rank, self.beside, 4)
            self.own[item].start()

    def advance(self, step):
        place = 2 * lax.rem(self.high + 4 - step, 4) + self.low
        for item in self.items:
            source = self.wholes[item].at[place]
            self.copy(item, source, place, self.ahead, step - 1).wait_recv()
            if step < 3:
                self.send(item, source, place, self.ahead, step)
            self.send(item, source, place, self.beside, 4 + step)

    def finish(self):
        for step in range(4):
            place = 2 * lax.rem(self.high + 4 - step, 4) + 1 - self.low
            for item in self.items:
                source = self.wholes[item].at[place]
                self.copy(item, source, place, self.beside, 4 + step).wait_recv()
        for sent in self.sent:
            sent.wait_send()
        for kept in self.own:
            kept.wait()


def ring_scratch(count):
    return [
        pltpu.SemaphoreType.DMA((count,)),
        pltpu.SemaphoreType.DMA((count, 8)),
        pltpu.SemaphoreType.DMA((count, 8)),
    ]


def sum_kernel(count, cross_type, *refs):
    partial, shares = refs[0], refs[1 : 1 + count]
    total, wholes = refs[1 + count], refs[2 + count : 2 + 2 * count]
    near, pair, far, send_sem, recv_sem = refs[2 + 2 * count : 7 + 2 * count]
    rank = lax.axis_index(tensor_axis)
    low = lax.rem(rank, 2)
    partner, across = rank + 1 - 2 * low, lax.rem(rank + 2, 4)
    ring = RingGather(shares, wholes, *refs[7 + 2 * count :]) if count else None
    barrier = pltpu.get_barrier_semaphore()
    for peer in (partner, across):
        pl.semaphore_signal(barrier, inc=1, device_id={tensor_axis: peer}, device_id_type=MESH)
    if ring:
        for peer in (ring.beside, ring.behind):
            pl.semaphore_signal(barrier, inc=1, device_id={dp_axis: peer}, device_id_type=MESH)
    pl.semaphore_wait(barrier, 4 if ring else 2)
    half = partial.shape[0] // 2
    mine = pl.ds(pl.multiple_of(low * half, 8), half)
    others = pl.ds(pl.multiple_of((1 - low) * half, 8), half)

    def copy(source, target, peer, slot):
        return pltpu.make_async_remote_copy(
            src_ref=source,
            dst_ref=target,
            send_sem=send_sem.at[slot],
            recv_sem=recv_sem.at[slot],
            device_id={tensor_axis: peer},
            device_id_type=MESH,
        )

    give = copy(partial.at[others], near, partner, 0)
    cross = copy(pair, far, across, 1)
    back = copy(total.at[mine], total.at[mine], partner, 2)
    give.start()
    if ring:
        ring.begin()
    give.wait()
    pair[...] = (partial[mine, :] + near[...]).astype(cross_type)
    cross.start()
    if ring:
        ring.advance(1)
        ring.advance(2)
    cross.wait()
    total[mine, :] = pair[...].astype(jnp.float32) + far[...].astype(jnp.float32)
    back.start()
    if ring:
        ring.advance(3)
    back.wait()
    if ring:
        ring.finish()


def tensor_sum(partial_term, cross_type, kernel, shares=()):
    ring_here = lax.axis_size(dp_axis) == 8
    wholes = [] if ring_here else [lax.all_gather(share, dp_axis) for share in shares]
    shares = shares if ring_here else ()
    if lax.axis_size(tensor_axis) != 4:
        return lax.psum(partial_term, tensor_axis), wholes
    rows, columns = partial_term.shape
    count = len(shares)
    vmem, anywhere = pl.BlockSpec(memory_space=pltpu.VMEM), pl.BlockSpec(memory_space=pl.ANY)
    outs = pl.pallas_call(
        functools.partial(sum_kernel, count, cross_type),
        out_shape=[jax.ShapeDtypeStruct(partial_term.shape, jnp.float32)]
        + [jax.ShapeDtypeStruct((8,) + share.shape, share.dtype) for share in shares],
        in_specs=[vmem] + [anywhere] * count,
        out_specs=[vmem] + [anywhere] * count,
        scratch_shapes=[
            pltpu.VMEM((rows // 2, columns), jnp.float32),
            pltpu.VMEM((rows // 2, columns), cross_type),
            pltpu.VMEM((rows // 2, columns), cross_type),
            pltpu.SemaphoreType.DMA((3,)),
            pltpu.SemaphoreType.DMA((3,)),
        ]
        + (ring_scratch(count) if count else []),
        compiler_params=pltpu.CompilerParams(
            collective_id=kernel, has_side_effects=True, vmem_limit_bytes=16 << 20
        ),
        cost_estimate=pl.CostEstimate(flops=0, bytes_accessed=2_000_000, transcendentals=0),
    )(partial_term, *shares)
    return outs[0], outs[1:] if ring_here else wholes


def branch_sum(partial_term, kernel, shares=()):
    return tensor_sum(partial_term, jnp.bfloat16, kernel, shares)


def spread(block, slots, axis, send_sem, recv_sem):
    rank, size = lax.axis_index(axis), lax.axis_size(axis)
    copies = []
    for step in range(1, size):
        peer = lax.rem(rank + step, size)
        copies.append(
            pltpu.make_async_remote_copy(
                src_ref=block,
                dst_ref=slots.at[rank],
                send_sem=send_sem.at[step - 1],
                recv_sem=recv_sem.at[step - 1],
                device_id={axis: peer},
                device_id_type=MESH,
            )
        )
        copies[-1].start()
    return copies


def greet(barrier, axes, others=()):
    count = len(others)
    for peer in others:
        pl.semaphore_signal(barrier, inc=1, device_id=peer, device_id_type=MESH)
    for axis in axes:
        rank, size = lax.axis_index(axis), lax.axis_size(axis)
        for step in range(1, size):
            peer = lax.rem(rank + step, size)
            pl.semaphore_signal(barrier, inc=1, device_id={axis: peer}, device_id_type=MESH)
            count += 1
    pl.semaphore_wait(barrier, count)


def small_sum_kernel(value, total, middle, near, far, near_send, near_recv, far_send, far_recv):
    greet(pltpu.get_barrier_semaphore(), (tensor_axis, dp_axis))
    near[lax.axis_index(tensor_axis)] = value[...]
    for copy in spread(value, near, tensor_axis, near_send, near_recv):
        copy.wait()
    middle[...] = functools.reduce(jnp.add, [near[slot] for slot in range(near.shape[0])])
    far[lax.axis_index(dp_axis)] = middle[...]
    for copy in spread(middle, far, dp_axis, far_send, far_recv):
        copy.wait()
    total[...] = functools.reduce(jnp.add, [far[slot] for slot in range(far.shape[0])])


def small_sums(values):
    sizes = [lax.axis_size(tensor_axis), lax.axis_size(dp_axis)]
    if max(sizes) > 8:
        return sum_everywhere(jnp.stack(values), (tensor_axis, dp_axis))
    rows = lax.broadcasted_iota(jnp.int32, (8, 128), 0)
    block = jnp.zeros((8, 128), jnp.float32)
    for row, value in enumerate(values):
        block = jnp.where(rows == row, value, block)
    scratch = [pltpu.VMEM((8, 128), jnp.float32)]
    scratch += [pltpu.VMEM((size, 8, 128), jnp.float32) for size in sizes]
    for size in sizes:
        scratch += [pltpu.SemaphoreType.DMA((size - 1,))] * 2
    total = pl.pallas_call(
        small_sum_kernel,
        out_shape=jax.ShapeDtypeStruct((8, 128), jnp.float32),
        in_specs=[pl.BlockSpec(memory_space=pltpu.VMEM)],
        out_specs=pl.BlockSpec(memory_space=pltpu.VMEM),
        scratch_shapes=scratch,
        compiler_params=pltpu.CompilerParams(
            collective_id=last_sums_kernel, has_side_effects=True
        ),
    )(block)
    return total[:, 0]


def tensor_blocks(piece):
    if lax.axis_size(tensor_axis) != 4:
        return list(lax.all_gather(piece, tensor_axis))
    rank = lax.axis_index(tensor_axis)
    near = swap(piece, tensor_axis, 1)
    far = swap(piece, tensor_axis, 2)
    cross = swap(far, tensor_axis, 1)
    blocks = []
    for index in range(4):
        same_pair = jnp.where(rank == index, piece, near)
        other_pair = jnp.where(rank == index ^ 2, far, cross)
        blocks.append(jnp.where(rank // 2 == index // 2, same_pair, other_pair))
    return blocks


def tensor_columns(piece):
    return jnp.concatenate(tensor_blocks(piece), axis=1)


def sum_everywhere(value, axes):
    for axis in axes:
        step = 1
        while step < lax.axis_size(axis):
            value = value + swap(value, axis, step)
            step = 2 * step
    return value


def pick(blocks, index):
    return lax.dynamic_index_in_dim(blocks, index, 0, keepdims=False)


def bound_level(pairs):
    bounds = [
        left.shape[0]
        * jnp.max(jnp.abs(left.astype(jnp.float32)))
        * jnp.max(jnp.abs(right.astype(jnp.float32)))
        for left, right in pairs
    ]
    return jnp.ceil(jnp.log2(jnp.maximum(functools.reduce(jnp.maximum, bounds), 2.0**-100)))


def coded(values, level):
    rows = values.shape[0]
    padded = jnp.pad(values * jnp.exp2(13.0 - level), ((0, 16), (0, 0)))
    is_value = lax.broadcasted_iota(jnp.int32, padded.shape, 0) < rows
    return jnp.where(is_value, padded, level).astype(jnp.float16)


def decoded(message, rows):
    level = message[rows : rows + 1].astype(jnp.float32)
    return message[:rows].astype(jnp.float32) * jnp.exp2(level - 13.0)


class Scattered:
    def __init__(self, pairs, first=0):
        self.pairs, self.first = pairs, max(first, 0)
        self.count = 4 - first if first >= 0 else -first
        self.got, self.parts, self.owned, self.owned_square = None, None, None, None
        self.level = bound_level(pairs)
        self.product = None

    def grad(self):
        if self.product is None:
            self.product = jnp.concatenate(
                [product_left(left, right) for left, right in self.pairs], axis=0
            )
        return self.product

    def slab(self):
        return self.grad().shape[0] // (2 * self.count)

    def near_message(self):
        grad, slab = self.grad(), self.slab()
        low = lax.axis_index(dp_axis) % 2
        blocks = grad.reshape(self.count, 2 * slab, grad.shape[1])
        give = lax.dynamic_slice_in_dim(blocks, (1 - low) * slab, slab, 1)
        return coded(give.reshape(-1, grad.shape[1]), self.level)

    def send_near(self, message):
        self.got = swap(message, dp_axis, 1)

    def got_level(self):
        at = self.count * self.slab()
        return self.got[at : at + 1].astype(jnp.float32)

    def share(self, place):
        grad, slab = self.grad(), self.slab()
        low = lax.axis_index(dp_axis) % 2
        place = jnp.clip(place - self.first, 0, self.count - 1)
        kept = lax.dynamic_slice_in_dim(grad, (2 * place + low) * slab, slab, 0)
        arrived = lax.dynamic_slice_in_dim(self.got, place * slab, slab, 0)
        return kept + arrived.astype(jnp.float32) * jnp.exp2(self.got_level() - 13.0)

    def far_messages(self):
        high = lax.axis_index(dp_axis) // 2
        level = jnp.maximum(self.level, self.got_level()) + 1.0
        return [coded(self.share(high ^ step), level) for step in (1, 2, 3)]

    def send_far(self, messages):
        self.parts = []
        for step, message in zip((1, 2, 3), messages):
            pairs = [
                (2 * source + side, 2 * (source ^ step) + side)
                for source in range(4)
                for side in range(2)
                if self.first <= source ^ step < self.first + self.count
            ]
            self.parts.append(lax.ppermute(message, dp_axis, pairs))

    def square(self):
        if self.owned_square is None:
            self.owned_square = jnp.sum(self.total() ** 2)
        return self.owned_square

    def total(self):
        if self.owned is None:
            self.owned = self.summed()
        return self.owned

    def summed(self):
        if lax.axis_size(dp_axis) != 8:
            return lax.psum_scatter(self.grad(), dp_axis, scatter_dimension=0, tiled=True)
        slab = self.slab()
        total = self.share(lax.axis_index(dp_axis) // 2)
        for part in self.parts:
            total = total + decoded(part, slab)
        return total


def tail_kernel(*refs):
    give, keep, bias, tables, bias_total = refs[:5]
    got, pairs, far, own, near, middle, beside_sum, pair_sum, far_sum, send_sem, recv_sem = refs[5:]
    rank, across = lax.axis_index(dp_axis), lax.axis_index(tensor_axis)
    low, high = lax.rem(rank, 2), lax.div(rank, 2)
    beside = {dp_axis: rank + 1 - 2 * low}
    pair_peers = [{dp_axis: 2 * lax.rem(high + step, 4) + low} for step in (1, 2, 3)]
    tensor_peers = [{tensor_axis: lax.rem(across + step, 4)} for step in (1, 2, 3)]
    barrier = pltpu.get_barrier_semaphore()
    peers = [beside] + pair_peers + tensor_peers
    for peer in peers:
        pl.semaphore_signal(barrier, inc=1, device_id=peer, device_id_type=MESH)
    pl.semaphore_wait(barrier, len(peers))
    slots = iter(range(14))

    def send(source, target, peer):
        slot = next(slots)
        copy = pltpu.make_async_remote_copy(
            src_ref=source,
            dst_ref=target,
            send_sem=send_sem.at[slot],
            recv_sem=recv_sem.at[slot],
            device_id=peer,
            device_id_type=MESH,
        )
        copy.start()
        return copy

    tables_near = send(give, got, beside)
    bias_near = [send(bias, near.at[across], peer) for peer in tensor_peers]
    near[across] = bias[...]
    tables_near.wait()
    pairs[...] = keep[...] + got[...]
    tables_far = [
        send(pairs.at[lax.rem(high + step, 4)], far.at[step - 1], pair_peers[step - 1])
        for step in (1, 2, 3)
    ]
    for copy in bias_near:
        copy.wait()
    middle[...] = near[0] + near[1] + near[2] + near[3]
    send(middle, beside_sum, beside).wait()
    pair_sum[...] = middle[...] + beside_sum[...]
    far_sum[high] = pair_sum[...]
    bias_far = [send(pair_sum, far_sum.at[high], peer) for peer in pair_peers]
    for copy in tables_far:
        copy.wait()
    own[...] = pairs[high] + far[0] + far[1] + far[2]
    tables[across] = own[...]
    tables_all = [send(own, tables.at[across], peer) for peer in tensor_peers]
    for copy in bias_far:
        copy.wait()
    bias_total[...] = far_sum[0] + far_sum[1] + far_sum[2] + far_sum[3]
    for copy in tables_all:
        copy.wait()


def tail_exchange(tables, bias):
    low = lax.axis_index(dp_axis) % 2
    slab, columns = tables.shape[0] // 8, tables.shape[1]
    blocks = tables.reshape(4, 2 * slab, columns)
    keep = lax.dynamic_slice_in_dim(blocks, low * slab, slab, 1)
    give = lax.dynamic_slice_in_dim(blocks, (1 - low) * slab, slab, 1)
    four, one = keep.shape, (slab, columns)
    vmem = pl.BlockSpec(memory_space=pltpu.VMEM)
    return pl.pallas_call(
        tail_kernel,
        out_shape=[
            jax.ShapeDtypeStruct(four, jnp.float32),
            jax.ShapeDtypeStruct(bias.shape, jnp.float32),
        ],
        in_specs=[vmem] * 3,
        out_specs=[vmem] * 2,
        scratch_shapes=[
            pltpu.VMEM(four, jnp.float32),
            pltpu.VMEM(four, jnp.float32),
            pltpu.VMEM((3,) + one, jnp.float32),
            pltpu.VMEM(one, jnp.float32),
            pltpu.VMEM((4,) + bias.shape, jnp.float32),
            pltpu.VMEM(bias.shape, jnp.float32),
            pltpu.VMEM(bias.shape, jnp.float32),
            pltpu.VMEM(bias.shape, jnp.float32),
            pltpu.VMEM((4,) + bias.shape, jnp.float32),
            pltpu.SemaphoreType.DMA((14,)),
            pltpu.SemaphoreType.DMA((14,)),
        ],
        compiler_params=pltpu.CompilerParams(
            collective_id=last_exchange, has_side_effects=True, vmem_limit_bytes=24 << 20
        ),
    )(give, keep, bias)


class Traffic:
    def __init__(self, plan):
        self.plan, self.groups = plan, {}

    def add(self, name, group):
        self.groups[name] = group
        return group

    def tie(self, value, near, far, arrived):
        near_messages = [group.near_message() for group in near]
        parts = [group.parts for group in arrived]
        if far:
            value, gots = lax.optimization_barrier((value, [group.got for group in far]))
            for group, got in zip(far, gots):
                group.got = got
        far_messages = [group.far_messages() for group in far]
        value, near_messages, far_messages, parts = lax.optimization_barrier(
            (value, near_messages, far_messages, parts)
        )
        for group, message in zip(near, near_messages):
            group.send_near(message)
        for group, messages in zip(far, far_messages):
            group.send_far(messages)
        for group, part in zip(arrived, parts):
            group.parts = part
        return value

    def input_sum(self, partial_term, kernel):
        if lax.axis_size(dp_axis) != 8:
            return tensor_sum(partial_term, jnp.bfloat16, kernel)[0]
        near, far, arrived = [[self.groups[group] for group in part] for part in self.plan[kernel]]
        partial_term = self.tie(partial_term, near, [], [])
        if kernel == back_encoder + 1:
            group = self.groups[back_encoder]
            done = [self.groups[key] for key in (back_head, back_head + 1, rest_group)]
            totals = [(item.total(), item.square()) for item in done]
            partial_term, group.got, totals = lax.optimization_barrier(
                (partial_term, group.got, totals)
            )
            for item, (total, square) in zip(done, totals):
                item.owned, item.owned_square = total, square
        total = tensor_sum(partial_term, jnp.bfloat16, kernel)[0]
        total = self.tie(total, [], far, arrived)
        if kernel == back_encoder + 1:
            mix = self.groups[mix_group]
            total, mix.got = lax.optimization_barrier((total, mix.got))
            total, messages = lax.optimization_barrier((total, self.encoder_messages()))
            self.encoder_parts = [
                swap(message, dp_axis, 2 * step) for step, message in zip((1, 2, 3), messages)
            ]
        return total

    def arrive(self, value, index):
        if lax.axis_size(dp_axis) != 8:
            return value
        value, self.encoder_parts[index] = lax.optimization_barrier(
            (value, self.encoder_parts[index])
        )
        return value

    def encoder_share(self, place):
        mix, rest = self.groups[mix_group], self.groups[back_encoder]
        return jnp.where(place == 0, mix.share(place), rest.share(place))

    def encoder_messages(self):
        mix, rest = self.groups[mix_group], self.groups[back_encoder]
        high = lax.axis_index(dp_axis) // 2
        level = jnp.maximum(
            jnp.maximum(mix.level, mix.got_level()), jnp.maximum(rest.level, rest.got_level())
        )
        return [
            coded(self.encoder_share(high ^ step), level + 1.0) for step in (1, 2, 3)
        ]

    def encoder_total(self, ahead):
        parts, ahead = lax.optimization_barrier((self.encoder_parts, ahead))
        slab = self.groups[mix_group].slab()
        total = self.encoder_share(lax.axis_index(dp_axis) // 2)
        for part in parts:
            total = total + decoded(part, slab)
        return total, ahead


def first_kernel(
    images,
    notes,
    class_table,
    table_share,
    block_share,
    all_notes,
    classes,
    tables,
    blocks,
    found,
    note_send,
    note_recv,
    class_send,
    class_recv,
    own_sem,
    across_send,
    across_recv,
    *ring_sems,
):
    rank, place_across = lax.axis_index(dp_axis), lax.axis_index(tensor_axis)
    low = lax.rem(place_across, 2)
    partner, across = place_across + 1 - 2 * low, lax.rem(place_across + 2, 4)
    others = [{tensor_axis: partner}, {tensor_axis: across}]
    greet(pltpu.get_barrier_semaphore(), (dp_axis,), others)
    table_ring = RingGather([table_share], [tables.at[place_across]], *ring_sems[:3])
    block_ring = RingGather([block_share], [blocks], *ring_sems[3:])
    note_copies = spread(notes, all_notes, dp_axis, note_send, note_recv)
    all_notes[rank] = notes[...]
    table_ring.begin()
    block_ring.begin()
    for copy in note_copies:
        copy.wait()
    for step in (1, 2, 3):
        table_ring.advance(step)
    block_ring.advance(1)
    table_ring.finish()

    def cross(owner, peer, slot):
        return pltpu.make_async_remote_copy(
            src_ref=tables.at[owner],
            dst_ref=tables.at[owner],
            send_sem=across_send.at[slot],
            recv_sem=across_recv.at[slot],
            device_id={tensor_axis: peer},
            device_id_type=MESH,
        )

    near = cross(place_across, partner, 0)
    far = cross(place_across, across, 1)
    near.start()
    far.start()
    place = lax.broadcasted_iota(jnp.int32, class_table.shape, 1).astype(jnp.float32)
    lane = lax.broadcasted_iota(jnp.int32, found.shape, 1)
    columns = jnp.zeros(found.shape, jnp.float32)
    for image in range(8 * images):
        label = all_notes[image // images, 0:1, image % images : image % images + 1]
        value = jnp.sum(
            jnp.where(place == label, class_table[...], 0.0), axis=1, keepdims=True
        )
        columns = jnp.where(lane == image, value, columns)
    found[...] = columns
    block_ring.advance(2)
    own = pltpu.make_async_copy(found, classes.at[rank], own_sem.at[0])
    own.start()
    class_copies = spread(found, classes, dp_axis, class_send, class_recv)
    near.wait()
    far.wait()
    forward = cross(across, partner, 2)
    forward.start()
    block_ring.advance(3)
    block_ring.finish()
    forward.wait()
    for copy in class_copies:
        copy.wait()
    own.wait()


def gather_first(notes, class_table, images, table_share, block_share):
    rows = class_table.shape[0]
    vmem, anywhere = pl.BlockSpec(memory_space=pltpu.VMEM), pl.BlockSpec(memory_space=pl.ANY)
    return pl.pallas_call(
        functools.partial(first_kernel, images),
        out_shape=[
            jax.ShapeDtypeStruct((8, 8, 128), jnp.float32),
            jax.ShapeDtypeStruct((8, rows, 128), jnp.float32),
            jax.ShapeDtypeStruct((4, 8) + table_share.shape, table_share.dtype),
            jax.ShapeDtypeStruct((8,) + block_share.shape, block_share.dtype),
        ],
        in_specs=[vmem, vmem, anywhere, anywhere],
        out_specs=[vmem, vmem, anywhere, anywhere],
        scratch_shapes=[pltpu.VMEM((rows, 128), jnp.float32)]
        + [pltpu.SemaphoreType.DMA((7,))] * 4
        + [pltpu.SemaphoreType.DMA((1,))]
        + [pltpu.SemaphoreType.DMA((3,))] * 2
        + ring_scratch(1)
        + ring_scratch(1),
        compiler_params=pltpu.CompilerParams(
            collective_id=first_gather, has_side_effects=True, vmem_limit_bytes=16 << 20
        ),
    )(notes, class_table, table_share, block_share)


def take_pieces(vector, starts, counts):
    return jnp.concatenate(
        [lax.dynamic_slice_in_dim(vector, start, count) for start, count in zip(starts, counts)]
    )


def place_pieces(total, pieces, starts):
    full = jnp.zeros((total,), jnp.float32)
    for piece, start in zip(pieces, starts):
        full = lax.dynamic_update_slice_in_dim(full, piece, start, 0)
    return full


def score_block(queries, key_rows, visible):
    scores = jnp.einsum(
        "bqhd,bkhd->bhqk", queries, key_rows, preferred_element_type=jnp.float32
    ) * HEAD ** (-0.5)
    return scores + (visible[:, None, None, :] - 1.0) * 1000000000.0


def attention(queries, key_rows, value_rows, visible):
    scores = score_block(queries, key_rows, visible)
    largest = jnp.max(scores, axis=-1, keepdims=True)
    exponent = jnp.exp(scores - largest)
    normaliser = jnp.sum(exponent, axis=-1, keepdims=True)
    chance = narrow(exponent / normaliser)
    attended = narrow(
        jnp.einsum("bhqk,bkhd->bqhd", chance, value_rows, preferred_element_type=jnp.float32)
    )
    return (attended, largest + jnp.log(normaliser))


def attention_back(queries, key_rows, value_rows, visible, log_total, grad_attended):
    chance = jnp.exp(score_block(queries, key_rows, visible) - log_total)
    grad_values = jnp.einsum(
        "bhqk,bqhd->bkhd", narrow(chance), grad_attended, preferred_element_type=jnp.float32
    )
    grad_chance = jnp.einsum(
        "bqhd,bkhd->bhqk", grad_attended, value_rows, preferred_element_type=jnp.float32
    )
    grad_scores = narrow(
        chance * (grad_chance - jnp.sum(chance * grad_chance, axis=-1, keepdims=True))
    )
    grad_queries = jnp.einsum(
        "bhqk,bkhd->bqhd", grad_scores, key_rows, preferred_element_type=jnp.float32
    ) * HEAD ** (-0.5)
    grad_keys = jnp.einsum(
        "bhqk,bqhd->bkhd", grad_scores, queries, preferred_element_type=jnp.float32
    ) * HEAD ** (-0.5)
    return (grad_queries, grad_keys, grad_values)


def block_forward(
    stream, visible, layer_rows, layer_bias, vectors, kernel, first_shares, last_shares
):
    images = visible.shape[0]
    local_width = D // lax.axis_size(tensor_axis)
    local_ff = FF // lax.axis_size(tensor_axis)
    heads_here = local_width // HEAD
    flat = stream.reshape(-1, D)
    normed = narrow(layer_norm(flat, vectors[0], vectors[1]))
    mixed = narrow(
        product_right(normed, layer_rows[: 3 * local_width]) + layer_bias[: 3 * local_width]
    )
    parts = [
        mixed[:, slot * local_width : (slot + 1) * local_width].reshape(
            images, -1, heads_here, HEAD
        )
        for slot in range(3)
    ]
    attended, log_total = attention(parts[0], parts[1], parts[2], visible)
    attended = attended.reshape(-1, local_width)
    branch, first_wholes = branch_sum(
        product(attended, layer_rows[3 * local_width + local_ff : 4 * local_width + local_ff]),
        kernel,
        first_shares,
    )
    middle = flat + branch + vectors[4]
    second = narrow(layer_norm(middle, vectors[2], vectors[3]))
    inner = (
        product_right(second, layer_rows[3 * local_width : 3 * local_width + local_ff])
        + layer_bias[3 * local_width :]
    )
    active = narrow(exact_gelu(inner))
    branch, last_wholes = branch_sum(
        product(active, layer_rows[4 * local_width + local_ff :]), kernel + 1, last_shares
    )
    result = middle + branch + vectors[5]
    return (
        result.reshape(stream.shape),
        (flat, normed, parts, log_total, attended, middle, second, inner, active),
        first_wholes,
        last_wholes,
    )


def block_back(incoming, visible, layer_rows, vectors, stored, kernel, traffic):
    flat, normed, parts, log_total, attended, middle, second, inner, active = stored
    local_width = D // lax.axis_size(tensor_axis)
    local_ff = FF // lax.axis_size(tensor_axis)
    mix_rows = layer_rows[: 3 * local_width]
    up_rows = layer_rows[3 * local_width : 3 * local_width + local_ff]
    proj_rows = layer_rows[3 * local_width + local_ff : 4 * local_width + local_ff]
    down_rows = layer_rows[4 * local_width + local_ff :]
    flow = incoming.reshape(-1, D)
    grad_branch = narrow(flow)
    grad_active = product_right(grad_branch, down_rows)
    grad_inner = narrow(local_back(exact_gelu, inner, grad_active))
    grad_second = traffic.input_sum(product(grad_inner, up_rows), kernel)
    grad_middle, grad_gain_two, grad_shift_two = jax.vjp(
        layer_norm, middle, vectors[2], vectors[3]
    )[1](grad_second)
    grad_middle = flow + grad_middle
    grad_attn = narrow(grad_middle)
    grad_attended = narrow(product_right(grad_attn, proj_rows)).reshape(parts[0].shape)
    grads_mixed = attention_back(parts[0], parts[1], parts[2], visible, log_total, grad_attended)
    grad_mixed = narrow(
        jnp.concatenate([piece.reshape(-1, local_width) for piece in grads_mixed], axis=1)
    )
    mix = [(grad_mixed, normed)]
    later = [(grad_inner, second), (attended, grad_attn), (active, grad_branch)]
    if kernel == back_encoder and lax.axis_size(dp_axis) == 8:
        owned_rows = [
            traffic.add(mix_group, Scattered(mix, -1)),
            traffic.add(kernel, Scattered(later, 1)),
        ]
    else:
        owned_rows = [traffic.add(kernel, Scattered(mix + later))]
    grad_normed = traffic.input_sum(product(grad_mixed, mix_rows), kernel + 1)
    grad_flat, grad_gain_one, grad_shift_one = jax.vjp(layer_norm, flat, vectors[0], vectors[1])[1](
        grad_normed
    )
    grad_bias = jnp.concatenate([column_sum(grad_mixed), column_sum(grad_inner)])
    grad_vectors = jnp.stack(
        [
            grad_gain_one,
            grad_shift_one,
            grad_gain_two,
            grad_shift_two,
            column_sum(grad_attn),
            column_sum(grad_branch),
        ]
    )
    return ((grad_middle + grad_flat).reshape(incoming.shape), owned_rows, grad_bias, grad_vectors)


def gathered_parts(columns, count):
    width = columns.shape[1] // count
    blocks = [block.astype(jnp.float32) for block in tensor_blocks(narrow(columns))]
    return [
        jnp.concatenate([block[:, slot * width : (slot + 1) * width] for block in blocks], axis=1)
        for slot in range(count)
    ]


def adaptive_vectors(cond_act, segment_rows, segment_bias):
    local_hidden = HW // lax.axis_size(tensor_axis)
    adaptive = (
        product_right(cond_act, segment_rows[: 3 * local_hidden]) + segment_bias[: 3 * local_hidden]
    )
    return gathered_parts(adaptive, 3)


def head_block(hidden_state, vectors, segment_rows, segment_bias, last_bias, kernel):
    local_hidden = HW // lax.axis_size(tensor_axis)
    shift_vec, scale_vec, gate_vec = vectors
    modulated = narrow(modulate(hidden_state, shift_vec, scale_vec))
    inner = (
        product_right(modulated, segment_rows[3 * local_hidden : 4 * local_hidden])
        + segment_bias[3 * local_hidden :]
    )
    active = narrow(jax.nn.silu(inner))
    branch = branch_sum(product(active, segment_rows[4 * local_hidden :]), kernel)[0] + last_bias
    return (
        hidden_state + gate_vec * branch,
        (hidden_state, shift_vec, scale_vec, gate_vec, modulated, inner, active, branch),
    )


def head_block_back(incoming, cond_act, segment_rows, offset, stored, kernel, traffic):
    hidden_state, shift_vec, scale_vec, gate_vec, modulated, inner, active, branch = stored
    local_hidden = HW // lax.axis_size(tensor_axis)
    grad_gate = incoming * branch
    grad_branch = narrow(incoming * gate_vec)
    grad_active = product_right(grad_branch, segment_rows[4 * local_hidden :])
    grad_inner = narrow(local_back(jax.nn.silu, inner, grad_active))
    grad_modulated = traffic.input_sum(
        product(grad_inner, segment_rows[3 * local_hidden : 4 * local_hidden]), kernel
    )
    grad_hidden, grad_shift, grad_scale = jax.vjp(modulate, hidden_state, shift_vec, scale_vec)[1](
        grad_modulated
    )
    grad_adaptive = narrow(
        jnp.concatenate(
            [
                lax.dynamic_slice_in_dim(piece, offset, local_hidden, 1)
                for piece in (grad_shift, grad_scale, grad_gate)
            ],
            axis=1,
        )
    )
    grad_cond = product(grad_adaptive, segment_rows[: 3 * local_hidden])
    owned_rows = traffic.add(
        kernel,
        Scattered([(grad_adaptive, cond_act), (grad_inner, modulated), (active, grad_branch)]),
    )
    grad_bias = jnp.concatenate([column_sum(grad_adaptive), column_sum(grad_inner)])
    return (incoming + grad_hidden, grad_cond, owned_rows, grad_bias, column_sum(grad_branch))


def adam_update(weight, moment_one, moment_two, gradient, factor, step_num):
    gradient = gradient * factor
    moment_one = beta_first * moment_one + (1.0 - beta_first) * gradient
    moment_two = beta_second * moment_two + (1.0 - beta_second) * gradient * gradient
    fixed_one = moment_one / (1.0 - beta_first**step_num)
    fixed_two = moment_two / (1.0 - beta_second**step_num)
    weight = weight - learn_rate * (
        fixed_one / (jnp.sqrt(fixed_two) + adam_eps) + decay_rate * weight
    )
    return (weight, moment_one, moment_two)


def local(
    block_weights,
    head_weights,
    head_rest,
    embed_tables,
    bias_rows,
    first_blocks,
    second_blocks,
    first_head,
    second_head,
    first_rest,
    second_rest,
    first_tables,
    second_tables,
    first_bias,
    second_bias,
    patches,
    noise,
    token_mask,
    labels,
    drop_marks,
    timesteps,
    step_weights,
    step_count,
):
    tensor_size = lax.axis_size(tensor_axis)
    tensor_index = lax.axis_index(tensor_axis)
    local_width = D // tensor_size
    local_ff = FF // tensor_size
    local_hidden = HW // tensor_size
    offset = tensor_index * local_hidden
    column_starts = [slot * D + tensor_index * local_width for slot in range(3)] + [
        3 * D + tensor_index * local_ff
    ]
    column_counts = [local_width] * 3 + [local_ff]
    head_starts = [slot * HW + offset for slot in range(4)]
    dp_size = lax.axis_size(dp_axis)
    dp_index = lax.axis_index(dp_axis)
    images = patches.shape[0]
    all_images = dp_size * images
    mask_float = token_mask.astype(jnp.float32)
    matches = timesteps[..., None] == jnp.arange(T_STEPS)
    row_weight = (
        jnp.sum(jnp.where(matches, step_weights, 0.0), axis=-1) * mask_float[None]
    ).reshape(-1)
    chosen = jnp.where(drop_marks == 1, CLASSES, labels)
    class_at = TOKD + 1
    class_end = class_at + CLASSES + 1
    weight_here = jnp.sum(row_weight)
    table_share = jnp.concatenate(
        [embed_tables[:, :class_at], embed_tables[:, class_end:]], axis=1
    )
    class_share = embed_tables[:, class_at:class_end]
    block_share = narrow(block_weights)
    whole_here = dp_size == 8 and tensor_size == 4
    if whole_here:
        part = -(-table_share.shape[1] // 32) * 8
        table_share = jnp.pad(table_share, ((0, 0), (0, 4 * part - table_share.shape[1])))
        table_share = lax.dynamic_slice_in_dim(table_share, tensor_index * part, part, 1)
        notes = jnp.zeros((8, 128), jnp.float32)
        notes = lax.dynamic_update_slice(notes, chosen.astype(jnp.float32)[None], (0, 0))
        notes = lax.dynamic_update_slice(notes, weight_here[None, None], (1, 0))
        all_notes, classes, table_parts, first_block = gather_first(
            notes, class_share, images, table_share.T, block_share[0]
        )
        table_rows = table_parts.transpose(0, 2, 1, 3).reshape(4 * part, -1)
        all_chosen = all_notes[:, 0, :images].reshape(-1)
        weight_total = jnp.sum(all_notes[:, 1, 0])
        class_rows = lax.dynamic_slice_in_dim(
            classes.reshape(-1, classes.shape[-1]), dp_index * images, images, 1
        ).T
    else:
        all_chosen = lax.all_gather(chosen, dp_axis, axis=0, tiled=True).astype(jnp.float32)
        weight_total = lax.psum(weight_here, dp_axis)
        table_rows = lax.all_gather(table_share, dp_axis, axis=0, tiled=True).T
        first_block = lax.all_gather(block_share[0], dp_axis)
    picker = (all_chosen[:, None] == jnp.arange(CLASSES + 1)[None, :]).astype(jnp.float32)
    if not whole_here:
        found = lax.dot_general(
            class_share, picker, (((1,), (1,)), ((), ())), precision=highest
        )
        class_rows = lax.dynamic_slice_in_dim(
            lax.all_gather(found, dp_axis, axis=0, tiled=True), dp_index * images, images, 1
        ).T
    first_block = first_block.reshape(-1, D)
    share_rows = block_share[1].shape[0] // 2
    rest_share = narrow(head_rest)
    flat_bias = bias_rows.reshape(-1)
    rest_bias = flat_bias[: 6 * HW].reshape(6, HW)
    head_bias = flat_bias[6 * HW : 6 * HW + 5 * HB * HW].reshape(HB, 5 * HW)
    column_bias = flat_bias[6 * HW + 5 * HB * HW :].reshape(LAYERS, 3 * D + FF)
    table_parts = cut_rows(table_rows, (TOKD, 1, TOK + BUF, TOK + BUF, 1, 6 * LAYERS, 4))
    layer_vectors = table_parts[5].reshape(LAYERS, 6, D)
    final_norms = table_parts[6]
    patch_flat = patches.reshape(-1, TOKD)
    tokens = product(patch_flat, narrow(table_parts[0])) + table_parts[1][0]
    stream = (
        jnp.concatenate(
            [
                jnp.broadcast_to(class_rows[:, None, :], (images, BUF, D)),
                tokens.reshape(images, TOK, D),
            ],
            axis=1,
        )
        + table_parts[2]
    )
    buffer_ones = jnp.ones((images, BUF), jnp.float32)
    visible_enc = jnp.concatenate([buffer_ones, 1.0 - mask_float], axis=1)
    visible_all = jnp.ones((images, TOK + BUF), jnp.float32)
    hidden_rows = jnp.concatenate([0.0 * buffer_ones, mask_float], axis=1)[..., None]
    layer_bias = [
        take_pieces(column_bias[layer], column_starts, column_counts) for layer in range(LAYERS)
    ]
    encoded, stored_enc, first_half, last_half = block_forward(
        stream,
        visible_enc,
        first_block,
        layer_bias[0],
        layer_vectors[0],
        encoder_forward,
        [block_share[1][:share_rows]],
        [block_share[1][share_rows:]],
    )
    encoded, head_share = lax.optimization_barrier((encoded, narrow(head_weights)))
    head_all = lax.all_gather(head_share, dp_axis, axis=1, tiled=True)
    second_block = jnp.concatenate([first_half[0], last_half[0]], axis=1).reshape(-1, D)
    block_all = [first_block, second_block]
    enc_normed = layer_norm(encoded, final_norms[0], final_norms[1])
    decoder_in = enc_normed * (1.0 - hidden_rows) + table_parts[4][0] * hidden_rows + table_parts[3]
    decoded, stored_dec, first_half, last_half = block_forward(
        decoder_in,
        visible_all,
        second_block,
        layer_bias[1],
        layer_vectors[1],
        decoder_forward,
        [rest_share],
        [],
    )
    rest_rows = first_half[0].reshape(-1, rest_share.shape[-1])
    cond_mine, input_mine, output_mine, time_first, second_mine, final_shift, final_scale = cut_rows(
        rest_rows, (D, TOKD, TOKD, HW, HW, HW, HW)
    )
    cond_weight, input_weight, output_weight, time_second = cut_rows(
        tensor_columns(jnp.concatenate([cond_mine, input_mine, output_mine, second_mine], axis=0)),
        (D, TOKD, TOKD, HW),
    )
    latent = narrow(layer_norm(decoded, final_norms[2], final_norms[3])[:, BUF:].reshape(-1, D))
    condition = product(latent, cond_weight) + rest_bias[0]
    step_rows = timesteps.reshape(COPIES, -1)
    time_feat = narrow(sinusoid(step_rows).reshape(-1, HW))
    time_pre = product(time_feat, time_first) + lax.dynamic_slice_in_dim(
        rest_bias[2], offset, local_hidden
    )
    time_act = tensor_columns(narrow(jax.nn.silu(time_pre)))
    time_embed = product(time_act, time_second) + rest_bias[3]
    cond_vec = (condition[None] + time_embed.reshape(COPIES, -1, HW)).reshape(-1, HW)
    cond_vec, head_all = lax.optimization_barrier((cond_vec, head_all))
    cond_act = narrow(jax.nn.silu(cond_vec))
    phase = step_rows.astype(jnp.float32)[..., None] * (math.pi / (2 * T_STEPS))
    signal_coef = jnp.cos(phase)
    noise_coef = jnp.sin(phase)
    clean = patch_flat.astype(jnp.float32)[None]
    noise_rows = noise.reshape(COPIES, -1, TOKD).astype(jnp.float32)
    noisy_rows = narrow((signal_coef * clean + noise_coef * noise_rows).reshape(-1, TOKD))
    target = (signal_coef * noise_rows - noise_coef * clean).reshape(-1, TOKD)
    hidden_state = product(noisy_rows, input_weight) + rest_bias[1]
    stored_head = []
    segment_biases = [
        take_pieces(head_bias[segment], head_starts, [local_hidden] * 4) for segment in range(HB)
    ]
    head_vectors = [
        adaptive_vectors(cond_act, head_all[segment], segment_biases[segment])
        for segment in range(HB)
    ]
    last_pair = jnp.concatenate(
        [product(cond_act, final_shift), product(cond_act, final_scale)], axis=1
    ) + take_pieces(flat_bias, [4 * HW + offset, 5 * HW + offset], [local_hidden] * 2)
    shift_last, scale_last = gathered_parts(last_pair, 2)
    for segment in range(HB):
        hidden_state, stored = head_block(
            hidden_state,
            head_vectors[segment],
            head_all[segment],
            segment_biases[segment],
            head_bias[segment, 4 * HW :],
            head_forward + segment,
        )
        stored_head.append(stored)
    final_in = narrow(modulate(hidden_state, shift_last, scale_last))
    predicted = product_right(final_in, output_weight)
    sq_error = jnp.mean((predicted - target) ** 2, axis=-1)
    numerator = jnp.sum(row_weight * sq_error)
    grad_pred = narrow(2.0 / (TOKD * weight_total) * row_weight[:, None] * (predicted - target))
    grad_final = product(grad_pred, output_weight)
    grad_hidden, grad_shift_last, grad_scale_last = jax.vjp(
        modulate, hidden_state, shift_last, scale_last
    )[1](grad_final)

    def own_columns(value):
        return lax.dynamic_slice_in_dim(value, offset, local_hidden, 1)

    grad_shift_last = narrow(own_columns(grad_shift_last))
    grad_scale_last = narrow(own_columns(grad_scale_last))
    traffic = Traffic(
        {
            back_head + 1: ([], [], []),
            back_head: ([back_head + 1], [], []),
            back_cond: ([back_head], [back_head + 1], []),
            back_decoder: ([rest_group], [back_head], [back_head + 1]),
            back_decoder + 1: ([back_decoder], [rest_group], [back_head]),
            back_encoder: ([], [back_decoder], [rest_group]),
            back_encoder + 1: ([back_encoder, mix_group], [], [back_decoder]),
        }
    )
    cond_split = product_right(grad_shift_last, final_shift) + product_right(
        grad_scale_last, final_scale
    )
    head_grads = []
    head_bias_grads = []
    for segment in reversed(range(HB)):
        grad_hidden, grad_cond, grad_segment, grad_segment_bias, grad_last_bias = head_block_back(
            grad_hidden,
            cond_act,
            head_all[segment],
            offset,
            stored_head[segment],
            back_head + segment,
            traffic,
        )
        cond_split = cond_split + grad_cond
        head_grads.insert(0, grad_segment)
        pieces = [
            grad_segment_bias[slot * local_hidden : (slot + 1) * local_hidden] for slot in range(4)
        ] + [grad_last_bias / tensor_size]
        head_bias_grads.insert(0, place_pieces(5 * HW, pieces, head_starts + [4 * HW]))
    grad_input = narrow(grad_hidden)
    grad_cond_vec = narrow(local_back(jax.nn.silu, cond_vec, traffic.input_sum(cond_split, back_cond)))
    cond_bias_grad = column_sum(grad_cond_vec)
    grad_time_act = product_right(
        grad_cond_vec, lax.dynamic_slice_in_dim(time_second, offset, local_hidden, 0)
    )
    grad_time_pre = narrow(local_back(jax.nn.silu, time_pre, grad_time_act))
    grad_latent = jnp.sum(product(grad_cond_vec, cond_weight.T).reshape(COPIES, -1, D), axis=0)
    grad_cond_mine = own_columns(grad_cond_vec)
    rest_scattered = Scattered(
        [
            (jnp.tile(latent, (COPIES, 1)), grad_cond_mine),
            (noisy_rows, own_columns(grad_input)),
            (grad_pred, own_columns(final_in)),
            (time_feat, grad_time_pre),
            (time_act, grad_cond_mine),
            (cond_act, grad_shift_last),
            (cond_act, grad_scale_last),
        ]
    )
    traffic.add(rest_group, rest_scattered)
    rest_bias_grad = place_pieces(
        6 * HW,
        [
            cond_bias_grad / tensor_size,
            column_sum(grad_input) / tensor_size,
            column_sum(grad_time_pre),
            cond_bias_grad / tensor_size,
            column_sum(grad_shift_last),
            column_sum(grad_scale_last),
        ],
        [0, HW, 2 * HW + offset, 3 * HW, 4 * HW + offset, 5 * HW + offset],
    )
    grad_top = jnp.concatenate(
        [jnp.zeros((images, BUF, D), jnp.float32), grad_latent.reshape(images, TOK, D)], axis=1
    )
    grad_decoded, grad_gain_dec, grad_shift_dec = jax.vjp(
        layer_norm, decoded, final_norms[2], final_norms[3]
    )[1](grad_top)
    grad_dec_in, grad_rows_dec, grad_bias_dec, grad_vec_dec = block_back(
        grad_decoded, visible_all, block_all[1], layer_vectors[1], stored_dec, back_decoder, traffic
    )
    grad_encoded, grad_gain_enc, grad_shift_enc = jax.vjp(
        layer_norm, encoded, final_norms[0], final_norms[1]
    )[1](grad_dec_in * (1.0 - hidden_rows))
    grad_stream, grad_rows_enc, grad_bias_enc, grad_vec_enc = block_back(
        grad_encoded, visible_enc, block_all[0], layer_vectors[0], stored_enc, back_encoder, traffic
    )
    grad_stream = traffic.arrive(grad_stream, 0)
    bias_parts = [rest_bias_grad] + head_bias_grads
    grad_tokens = narrow(grad_stream[:, BUF:].reshape(-1, D))
    grad_class = lax.dynamic_update_slice_in_dim(
        jnp.zeros((all_images, D), jnp.float32),
        jnp.sum(grad_stream[:, :BUF], axis=1),
        dp_index * images,
        0,
    )
    small_rows = jnp.concatenate(
        [
            column_sum(grad_tokens)[None],
            jnp.sum(grad_dec_in * hidden_rows, axis=(0, 1))[None],
            grad_vec_enc,
            grad_vec_dec,
            jnp.stack([grad_gain_enc, grad_shift_enc, grad_gain_dec, grad_shift_dec]),
            grad_class,
        ],
        axis=0,
    )
    seq_rows = TOK + BUF
    small_at = 2 * seq_rows + TOKD
    table_count = small_at + small_rows.shape[0]
    quarter = -(-table_count // (8 * tensor_size)) * 8
    small_rows = jnp.pad(small_rows, ((0, quarter * tensor_size - table_count), (0, 0)))
    grad_tables = jnp.concatenate(
        [
            jnp.sum(grad_stream, axis=0),
            jnp.sum(grad_dec_in, axis=0),
            product_left(patch_flat, grad_tokens),
            small_rows,
        ],
        axis=0,
    )
    grad_tables = lax.dynamic_slice_in_dim(grad_tables, tensor_index * quarter, quarter, 0)
    column_grads = []
    for grad_local in (grad_bias_enc, grad_bias_dec):
        pieces = [
            grad_local[slot * local_width : (slot + 1) * local_width] for slot in range(3)
        ] + [grad_local[3 * local_width :]]
        column_grads.append(place_pieces(3 * D + FF, pieces, column_starts))
    lanes = bias_rows.shape[1]
    bias_local = jnp.concatenate(bias_parts + column_grads).reshape(-1, lanes)
    if dp_size == 8 and tensor_size == 4:
        bias_count = bias_local.shape[0]
        bias_local = jnp.pad(bias_local, ((0, -bias_count % 8), (0, 0)))
        grad_tables = traffic.arrive(grad_tables, 1)
        owned_cols, bias_grad = tail_exchange(grad_tables.T, bias_local)
        encoder_owned, (owned_cols, bias_grad) = traffic.encoder_total((owned_cols, bias_grad))
        owned_cols = jnp.concatenate([owned_cols[index] for index in range(4)], axis=1)
        bias_grad = bias_grad[:bias_count]
    else:
        owned_cols = tensor_columns(
            lax.psum_scatter(grad_tables.T, dp_axis, scatter_dimension=0, tiled=True)
        )
        bias_grad = sum_everywhere(bias_local, (tensor_axis, dp_axis))
        encoder_owned = grad_rows_enc[0].total()
    class_cols = small_at + 6 * LAYERS + 6
    owned_tables = jnp.concatenate(
        [
            owned_cols[:, 2 * seq_rows : small_at + 1],
            jnp.dot(
                owned_cols[:, class_cols : class_cols + all_images], picker, precision=highest
            ),
            owned_cols[:, : 2 * seq_rows],
            owned_cols[:, small_at + 1 : class_cols],
        ],
        axis=1,
    )
    owned_blocks = jnp.stack([encoder_owned, grad_rows_dec[0].total()])
    owned_head = jnp.stack([group.total() for group in head_grads])
    owned_rest = rest_scattered.total()
    split_squares = (
        jnp.sum(encoder_owned * encoder_owned)
        + grad_rows_dec[0].square()
        + sum(group.square() for group in head_grads)
        + rest_scattered.square()
    )
    shared_squares = jnp.sum(owned_tables * owned_tables) / tensor_size
    every_squares = jnp.sum(bias_grad * bias_grad) / (tensor_size * lax.axis_size(dp_axis))
    last_sums = small_sums(
        [split_squares + shared_squares + every_squares, numerator / tensor_size]
    )
    norm_square = last_sums[0]
    loss_value = last_sums[1] / weight_total
    grad_norm = jnp.sqrt(norm_square)
    factor = jnp.minimum(1.0, clip_limit / (grad_norm + 1e-06))
    step_num = step_count[0].astype(jnp.float32)
    blocks_new, blocks_first, blocks_second = adam_update(
        block_weights, first_blocks, second_blocks, owned_blocks, factor, step_num
    )
    head_new, head_first, head_second = adam_update(
        head_weights, first_head, second_head, owned_head, factor, step_num
    )
    rest_new, rest_first, rest_second = adam_update(
        head_rest, first_rest, second_rest, owned_rest, factor, step_num
    )
    tables_new, tables_first, tables_second = adam_update(
        embed_tables, first_tables, second_tables, owned_tables, factor, step_num
    )
    bias_new, bias_first, bias_second = adam_update(
        bias_rows, first_bias, second_bias, bias_grad, factor, step_num
    )
    return (
        loss_value,
        grad_norm,
        blocks_new,
        blocks_first,
        blocks_second,
        narrow(blocks_new),
        head_new,
        head_first,
        head_second,
        narrow(head_new),
        rest_new,
        rest_first,
        rest_second,
        narrow(rest_new),
        tables_new,
        tables_first,
        tables_second,
        narrow(tables_new),
        bias_new,
        bias_first,
        bias_second,
        narrow(bias_new),
    )


def solution(mesh):
    in_specs = (
        P(None, (dp_axis, tensor_axis), None),
        P(None, (dp_axis, tensor_axis), None),
        P(dp_axis, tensor_axis),
        P(dp_axis, None),
        P(),
        P(None, (dp_axis, tensor_axis), None),
        P(None, (dp_axis, tensor_axis), None),
        P(None, (dp_axis, tensor_axis), None),
        P(None, (dp_axis, tensor_axis), None),
        P(dp_axis, tensor_axis),
        P(dp_axis, tensor_axis),
        P(dp_axis, None),
        P(dp_axis, None),
        P(),
        P(),
        P(dp_axis, None, None),
        P(None, dp_axis, None, None),
        P(dp_axis, None),
        P(dp_axis),
        P(dp_axis),
        P(None, dp_axis, None),
        P(),
        P(),
    )
    out_specs = (
        P(),
        P(),
        P(None, (dp_axis, tensor_axis), None),
        P(None, (dp_axis, tensor_axis), None),
        P(None, (dp_axis, tensor_axis), None),
        P(None, (dp_axis, tensor_axis), None),
        P(None, (dp_axis, tensor_axis), None),
        P(None, (dp_axis, tensor_axis), None),
        P(None, (dp_axis, tensor_axis), None),
        P(None, (dp_axis, tensor_axis), None),
        P(dp_axis, tensor_axis),
        P(dp_axis, tensor_axis),
        P(dp_axis, tensor_axis),
        P(dp_axis, tensor_axis),
        P(dp_axis, None),
        P(dp_axis, None),
        P(dp_axis, None),
        P(dp_axis, None),
        P(),
        P(),
        P(),
        P(),
    )
    return jax.shard_map(local, mesh=mesh, in_specs=in_specs, out_specs=out_specs, check_vma=False)
```

```python
import functools
import math

import jax
import jax.numpy as jnp
from jax import lax
from jax.experimental import pallas as pl
from jax.experimental.pallas import tpu as pltpu
from jax.sharding import PartitionSpec as P

D = 768
HEAD = 64
FF = 3072
HW = 1024
TOKD = 64
CLASSES = 1000
BUF = 64
TOK = 256
T_STEPS = 1000
COPIES = 1
LAYERS = 2
HB = 2


highest = lax.Precision.HIGHEST
norm_eps = 1e-06
beta_first = 0.9
beta_second = 0.95
adam_eps = 1e-08
learn_rate = 0.02
decay_rate = 0.05
clip_limit = 0.002
dp_axis, tensor_axis = "dp", "tensor"


def layer_norm(inputs, gain_vec, offset_vec):
    average = jnp.mean(inputs, axis=-1, keepdims=True)
    centred = inputs - average
    spread = jnp.mean(centred * centred, axis=-1, keepdims=True)
    return centred * lax.rsqrt(spread + norm_eps) * gain_vec + offset_vec


def modulate(inputs, shift_vec, scale_vec):
    return layer_norm(inputs, 1.0, 0.0) * (1.0 + scale_vec) + shift_vec


def exact_gelu(inputs):
    return jax.nn.gelu(inputs, approximate=False)


def local_back(function, inputs, incoming):
    return jax.vjp(function, inputs)[1](incoming)[0]


def sinusoid(step_ids):
    half_width = HW // 2
    frequency = jnp.exp(-math.log(10000.0) * jnp.arange(half_width, dtype=jnp.float32) / half_width)
    angles = step_ids.astype(jnp.float32)[..., None] * frequency
    return jnp.concatenate([jnp.cos(angles), jnp.sin(angles)], axis=-1)


def cut_rows(packed, counts):
    pieces = []
    begin_at = 0
    for count in counts:
        pieces.append(packed[begin_at : begin_at + count])
        begin_at = begin_at + count
    return pieces


def narrow(inputs):
    return inputs.astype(jnp.bfloat16)


def product(left, right):
    return jnp.dot(left, right, preferred_element_type=jnp.float32)


def product_left(left, right):
    return lax.dot_general(
        left, right, (((0,), (0,)), ((), ())), preferred_element_type=jnp.float32
    )


def product_right(left, right):
    return lax.dot_general(
        left, right, (((1,), (1,)), ((), ())), preferred_element_type=jnp.float32
    )


def column_sum(inputs):
    return jnp.sum(inputs.astype(jnp.float32), axis=0)


def swap(value, axis, step):
    return lax.ppermute(value, axis, [(i, i ^ step) for i in range(lax.axis_size(axis))])


MESH = pl.DeviceIdType.MESH
(
    first_gather,
    last_sums_kernel,
    encoder_forward,
    decoder_forward,
    head_forward,
    back_head,
    back_cond,
    back_decoder,
    back_encoder,
    last_exchange,
) = (0, 1, 2, 4, 6, 8, 10, 11, 13, 15)
rest_group, mix_group = 100, 101


class RingGather:
    def __init__(self, shares, wholes, local_sem, send_sem, recv_sem):
        rank = lax.axis_index(dp_axis)
        self.rank, self.low, self.high = rank, lax.rem(rank, 2), lax.div(rank, 2)
        self.beside = rank + 1 - 2 * self.low
        self.ahead = 2 * lax.rem(self.high + 1, 4) + self.low
        self.behind = 2 * lax.rem(self.high + 3, 4) + self.low
        self.shares, self.wholes = [], []
        for share, whole in zip(shares, wholes):
            rows = share.shape[0]
            cut = -(-rows // 32) * 16
            for start, size in ((0, cut), (cut, rows - cut)):
                self.shares.append(share.at[pl.ds(start, size)])
                self.wholes.append(whole.at[:, pl.ds(start, size)])
        shares, wholes = self.shares, self.wholes
        self.send_sem, self.recv_sem = send_sem, recv_sem
        self.items = range(len(shares))
        self.sent = []
        self.own = [
            pltpu.make_async_copy(shares[item], wholes[item].at[rank], local_sem.at[item])
            for item in self.items
        ]

    def copy(self, item, source, place, peer, slot):
        return pltpu.make_async_remote_copy(
            src_ref=source,
            dst_ref=self.wholes[item].at[place],
            send_sem=self.send_sem.at[item, slot],
            recv_sem=self.recv_sem.at[item, slot],
            device_id={dp_axis: peer},
            device_id_type=MESH,
        )

    def send(self, *arguments):
        self.sent.append(self.copy(*arguments))
        self.sent[-1].start()

    def begin(self):
        for item in self.items:
            self.send(item, self.shares[item], self.rank, self.ahead, 0)
            self.send(item, self.shares[item], self.rank, self.beside, 4)
            self.own[item].start()

    def advance(self, step):
        place = 2 * lax.rem(self.high + 4 - step, 4) + self.low
        for item in self.items:
            source = self.wholes[item].at[place]
            self.copy(item, source, place, self.ahead, step - 1).wait_recv()
            if step < 3:
                self.send(item, source, place, self.ahead, step)
            self.send(item, source, place, self.beside, 4 + step)

    def finish(self):
        for step in range(4):
            place = 2 * lax.rem(self.high + 4 - step, 4) + 1 - self.low
            for item in self.items:
                source = self.wholes[item].at[place]
                self.copy(item, source, place, self.beside, 4 + step).wait_recv()
        for sent in self.sent:
            sent.wait_send()
        for kept in self.own:
            kept.wait()


def ring_scratch(arrays):
    count = 2 * arrays
    return [
        pltpu.SemaphoreType.DMA((count,)),
        pltpu.SemaphoreType.DMA((count, 8)),
        pltpu.SemaphoreType.DMA((count, 8)),
    ]


def sum_kernel(count, cross_type, *refs):
    partial, shares = refs[0], refs[1 : 1 + count]
    total, wholes = refs[1 + count], refs[2 + count : 2 + 2 * count]
    near, pair, far, send_sem, recv_sem = refs[2 + 2 * count : 7 + 2 * count]
    rank = lax.axis_index(tensor_axis)
    low = lax.rem(rank, 2)
    partner, across = rank + 1 - 2 * low, lax.rem(rank + 2, 4)
    ring = RingGather(shares, wholes, *refs[7 + 2 * count :]) if count else None
    barrier = pltpu.get_barrier_semaphore()
    for peer in (partner, across):
        pl.semaphore_signal(barrier, inc=1, device_id={tensor_axis: peer}, device_id_type=MESH)
    if ring:
        for peer in (ring.beside, ring.behind):
            pl.semaphore_signal(barrier, inc=1, device_id={dp_axis: peer}, device_id_type=MESH)
    pl.semaphore_wait(barrier, 4 if ring else 2)
    half = partial.shape[0] // 2
    mine = pl.ds(pl.multiple_of(low * half, 8), half)
    others = pl.ds(pl.multiple_of((1 - low) * half, 8), half)

    def copy(source, target, peer, slot):
        return pltpu.make_async_remote_copy(
            src_ref=source,
            dst_ref=target,
            send_sem=send_sem.at[slot],
            recv_sem=recv_sem.at[slot],
            device_id={tensor_axis: peer},
            device_id_type=MESH,
        )

    give = copy(partial.at[others], near, partner, 0)
    cross = copy(pair, far, across, 1)
    back = copy(total.at[mine], total.at[mine], partner, 2)
    give.start()
    if ring:
        ring.begin()
    give.wait()
    pair[...] = (partial[mine, :] + near[...]).astype(cross_type)
    cross.start()
    if ring:
        ring.advance(1)
        ring.advance(2)
    cross.wait()
    total[mine, :] = pair[...].astype(jnp.float32) + far[...].astype(jnp.float32)
    back.start()
    if ring:
        ring.advance(3)
    back.wait()
    if ring:
        ring.finish()


def tensor_sum(partial_term, cross_type, kernel, shares=()):
    ring_here = lax.axis_size(dp_axis) == 8
    wholes = [] if ring_here else [lax.all_gather(share, dp_axis) for share in shares]
    shares = shares if ring_here else ()
    if lax.axis_size(tensor_axis) != 4:
        return lax.psum(partial_term, tensor_axis), wholes
    rows, columns = partial_term.shape
    count = len(shares)
    vmem, anywhere = pl.BlockSpec(memory_space=pltpu.VMEM), pl.BlockSpec(memory_space=pl.ANY)
    outs = pl.pallas_call(
        functools.partial(sum_kernel, count, cross_type),
        out_shape=[jax.ShapeDtypeStruct(partial_term.shape, jnp.float32)]
        + [jax.ShapeDtypeStruct((8,) + share.shape, share.dtype) for share in shares],
        in_specs=[vmem] + [anywhere] * count,
        out_specs=[vmem] + [anywhere] * count,
        scratch_shapes=[
            pltpu.VMEM((rows // 2, columns), jnp.float32),
            pltpu.VMEM((rows // 2, columns), cross_type),
            pltpu.VMEM((rows // 2, columns), cross_type),
            pltpu.SemaphoreType.DMA((3,)),
            pltpu.SemaphoreType.DMA((3,)),
        ]
        + (ring_scratch(count) if count else []),
        compiler_params=pltpu.CompilerParams(
            collective_id=kernel, has_side_effects=True, vmem_limit_bytes=16 << 20
        ),
        cost_estimate=pl.CostEstimate(flops=0, bytes_accessed=2_000_000, transcendentals=0),
    )(partial_term, *shares)
    return outs[0], outs[1:] if ring_here else wholes


def branch_sum(partial_term, kernel, shares=()):
    return tensor_sum(partial_term, jnp.bfloat16, kernel, shares)


def spread(block, slots, axis, send_sem, recv_sem):
    rank, size = lax.axis_index(axis), lax.axis_size(axis)
    copies = []
    for step in range(1, size):
        peer = lax.rem(rank + step, size)
        copies.append(
            pltpu.make_async_remote_copy(
                src_ref=block,
                dst_ref=slots.at[rank],
                send_sem=send_sem.at[step - 1],
                recv_sem=recv_sem.at[step - 1],
                device_id={axis: peer},
                device_id_type=MESH,
            )
        )
        copies[-1].start()
    return copies


def greet(barrier, axes, others=()):
    count = len(others)
    for peer in others:
        pl.semaphore_signal(barrier, inc=1, device_id=peer, device_id_type=MESH)
    for axis in axes:
        rank, size = lax.axis_index(axis), lax.axis_size(axis)
        for step in range(1, size):
            peer = lax.rem(rank + step, size)
            pl.semaphore_signal(barrier, inc=1, device_id={axis: peer}, device_id_type=MESH)
            count += 1
    pl.semaphore_wait(barrier, count)


def small_sum_kernel(value, total, middle, near, far, near_send, near_recv, far_send, far_recv):
    greet(pltpu.get_barrier_semaphore(), (tensor_axis, dp_axis))
    near[lax.axis_index(tensor_axis)] = value[...]
    for copy in spread(value, near, tensor_axis, near_send, near_recv):
        copy.wait()
    middle[...] = functools.reduce(jnp.add, [near[slot] for slot in range(near.shape[0])])
    far[lax.axis_index(dp_axis)] = middle[...]
    for copy in spread(middle, far, dp_axis, far_send, far_recv):
        copy.wait()
    total[...] = functools.reduce(jnp.add, [far[slot] for slot in range(far.shape[0])])


def small_sums(values):
    sizes = [lax.axis_size(tensor_axis), lax.axis_size(dp_axis)]
    if max(sizes) > 8:
        return sum_everywhere(jnp.stack(values), (tensor_axis, dp_axis))
    rows = lax.broadcasted_iota(jnp.int32, (8, 128), 0)
    block = jnp.zeros((8, 128), jnp.float32)
    for row, value in enumerate(values):
        block = jnp.where(rows == row, value, block)
    scratch = [pltpu.VMEM((8, 128), jnp.float32)]
    scratch += [pltpu.VMEM((size, 8, 128), jnp.float32) for size in sizes]
    for size in sizes:
        scratch += [pltpu.SemaphoreType.DMA((size - 1,))] * 2
    total = pl.pallas_call(
        small_sum_kernel,
        out_shape=jax.ShapeDtypeStruct((8, 128), jnp.float32),
        in_specs=[pl.BlockSpec(memory_space=pltpu.VMEM)],
        out_specs=pl.BlockSpec(memory_space=pltpu.VMEM),
        scratch_shapes=scratch,
        compiler_params=pltpu.CompilerParams(
            collective_id=last_sums_kernel, has_side_effects=True
        ),
    )(block)
    return total[:, 0]


def tensor_blocks(piece):
    if lax.axis_size(tensor_axis) != 4:
        return list(lax.all_gather(piece, tensor_axis))
    rank = lax.axis_index(tensor_axis)
    near = swap(piece, tensor_axis, 1)
    far = swap(piece, tensor_axis, 2)
    cross = swap(far, tensor_axis, 1)
    blocks = []
    for index in range(4):
        same_pair = jnp.where(rank == index, piece, near)
        other_pair = jnp.where(rank == index ^ 2, far, cross)
        blocks.append(jnp.where(rank // 2 == index // 2, same_pair, other_pair))
    return blocks


def tensor_columns(piece):
    return jnp.concatenate(tensor_blocks(piece), axis=1)


def sum_everywhere(value, axes):
    for axis in axes:
        step = 1
        while step < lax.axis_size(axis):
            value = value + swap(value, axis, step)
            step = 2 * step
    return value


def pick(blocks, index):
    return lax.dynamic_index_in_dim(blocks, index, 0, keepdims=False)


def bound_level(pairs):
    bounds = [
        left.shape[0]
        * jnp.max(jnp.abs(left.astype(jnp.float32)))
        * jnp.max(jnp.abs(right.astype(jnp.float32)))
        for left, right in pairs
    ]
    return jnp.ceil(jnp.log2(jnp.maximum(functools.reduce(jnp.maximum, bounds), 2.0**-100)))


def coded(values, level):
    rows = values.shape[0]
    padded = jnp.pad(values * jnp.exp2(13.0 - level), ((0, 16), (0, 0)))
    is_value = lax.broadcasted_iota(jnp.int32, padded.shape, 0) < rows
    return jnp.where(is_value, padded, level).astype(jnp.float16)


def decoded(message, rows):
    level = message[rows : rows + 1].astype(jnp.float32)
    return message[:rows].astype(jnp.float32) * jnp.exp2(level - 13.0)


class Scattered:
    def __init__(self, pairs, first=0, split=False):
        self.pairs, self.first, self.split = pairs, max(first, 0), split
        self.count = 4 - first if first >= 0 else -first
        self.got, self.parts, self.owned, self.owned_square = None, None, None, None
        self.level = bound_level(pairs)
        self.product = None

    def grad(self):
        if self.product is None:
            self.product = jnp.concatenate(
                [product_left(left, right) for left, right in self.pairs], axis=0
            )
        return self.product

    def slab(self):
        return self.grad().shape[0] // (2 * self.count)

    def near_message(self):
        grad, slab = self.grad(), self.slab()
        low = lax.axis_index(dp_axis) % 2
        blocks = grad.reshape(self.count, 2 * slab, grad.shape[1])
        give = lax.dynamic_slice_in_dim(blocks, (1 - low) * slab, slab, 1)
        if self.split:
            return [coded(give[place], self.level) for place in range(self.count)]
        return coded(give.reshape(-1, grad.shape[1]), self.level)

    def send_near(self, message):
        parts = [swap(part, dp_axis, 1) for part in (message if self.split else [message])]
        self.got = parts if self.split else parts[0]

    def got_level(self):
        slab = self.slab()
        got, at = (self.got[0], slab) if self.split else (self.got, self.count * slab)
        return got[at : at + 1].astype(jnp.float32)

    def share(self, place):
        grad, slab = self.grad(), self.slab()
        low = lax.axis_index(dp_axis) % 2
        place = jnp.clip(place - self.first, 0, self.count - 1)
        kept = lax.dynamic_slice_in_dim(grad, (2 * place + low) * slab, slab, 0)
        if self.split:
            arrived = self.got[0][:slab]
            for index in range(1, self.count):
                arrived = jnp.where(place == index, self.got[index][:slab], arrived)
        else:
            arrived = lax.dynamic_slice_in_dim(self.got, place * slab, slab, 0)
        return kept + arrived.astype(jnp.float32) * jnp.exp2(self.got_level() - 13.0)

    def far_messages(self):
        high = lax.axis_index(dp_axis) // 2
        level = jnp.maximum(self.level, self.got_level()) + 1.0
        return [coded(self.share(high ^ step), level) for step in (1, 2, 3)]

    def send_far(self, messages):
        self.parts = []
        for step, message in zip((1, 2, 3), messages):
            pairs = [
                (2 * source + side, 2 * (source ^ step) + side)
                for source in range(4)
                for side in range(2)
                if self.first <= source ^ step < self.first + self.count
            ]
            self.parts.append(lax.ppermute(message, dp_axis, pairs))

    def square(self):
        if self.owned_square is None:
            self.owned_square = jnp.sum(self.total() ** 2)
        return self.owned_square

    def total(self):
        if self.owned is None:
            self.owned = self.summed()
        return self.owned

    def summed(self):
        if lax.axis_size(dp_axis) != 8:
            return lax.psum_scatter(self.grad(), dp_axis, scatter_dimension=0, tiled=True)
        slab = self.slab()
        total = self.share(lax.axis_index(dp_axis) // 2)
        for part in self.parts:
            total = total + decoded(part, slab)
        return total


def tail_kernel(*refs):
    give, keep, bias, tables, bias_total = refs[:5]
    got, pairs, far, own, near, middle, beside_sum, pair_sum, far_sum, send_sem, recv_sem = refs[5:]
    rank, across = lax.axis_index(dp_axis), lax.axis_index(tensor_axis)
    low, high = lax.rem(rank, 2), lax.div(rank, 2)
    beside = {dp_axis: rank + 1 - 2 * low}
    pair_peers = [{dp_axis: 2 * lax.rem(high + step, 4) + low} for step in (1, 2, 3)]
    tensor_peers = [{tensor_axis: lax.rem(across + step, 4)} for step in (1, 2, 3)]
    barrier = pltpu.get_barrier_semaphore()
    peers = [beside] + pair_peers + tensor_peers
    for peer in peers:
        pl.semaphore_signal(barrier, inc=1, device_id=peer, device_id_type=MESH)
    pl.semaphore_wait(barrier, len(peers))
    slots = iter(range(17))

    def send(source, target, peer):
        slot = next(slots)
        copy = pltpu.make_async_remote_copy(
            src_ref=source,
            dst_ref=target,
            send_sem=send_sem.at[slot],
            recv_sem=recv_sem.at[slot],
            device_id=peer,
            device_id_type=MESH,
        )
        copy.start()
        return copy

    tables_near = send(give, got, beside)
    bias_near = [send(bias, near.at[across], peer) for peer in tensor_peers]
    near[across] = bias[...]
    tables_near.wait()
    pairs[...] = keep[...] + got[...]
    tables_far = [
        send(pairs.at[lax.rem(high + step, 4)], far.at[step - 1], pair_peers[step - 1])
        for step in (1, 2, 3)
    ]
    for copy in bias_near:
        copy.wait()
    middle[...] = near[0] + near[1] + near[2] + near[3]
    send(middle, beside_sum, beside).wait()
    pair_sum[...] = middle[...] + beside_sum[...]
    rows = bias_total.shape[0] // 4
    mine = pl.ds(pl.multiple_of(across * rows, 8), rows)
    far_sum[high] = pair_sum[mine, :]
    bias_far = [send(pair_sum.at[mine], far_sum.at[high], peer) for peer in pair_peers]
    for copy in tables_far:
        copy.wait()
    own[...] = pairs[high] + far[0] + far[1] + far[2]
    tables[across] = own[...]
    tables_all = [send(own, tables.at[across], peer) for peer in tensor_peers]
    for copy in bias_far:
        copy.wait()
    bias_total[mine, :] = far_sum[0] + far_sum[1] + far_sum[2] + far_sum[3]
    bias_all = [send(bias_total.at[mine], bias_total.at[mine], peer) for peer in tensor_peers]
    for copy in tables_all + bias_all:
        copy.wait()


def tail_exchange(tables, bias):
    low = lax.axis_index(dp_axis) % 2
    slab, columns = tables.shape[0] // 8, tables.shape[1]
    blocks = tables.reshape(4, 2 * slab, columns)
    keep = lax.dynamic_slice_in_dim(blocks, low * slab, slab, 1)
    give = lax.dynamic_slice_in_dim(blocks, (1 - low) * slab, slab, 1)
    four, one = keep.shape, (slab, columns)
    vmem = pl.BlockSpec(memory_space=pltpu.VMEM)
    return pl.pallas_call(
        tail_kernel,
        out_shape=[
            jax.ShapeDtypeStruct(four, jnp.float32),
            jax.ShapeDtypeStruct(bias.shape, jnp.float32),
        ],
        in_specs=[vmem] * 3,
        out_specs=[vmem] * 2,
        scratch_shapes=[
            pltpu.VMEM(four, jnp.float32),
            pltpu.VMEM(four, jnp.float32),
            pltpu.VMEM((3,) + one, jnp.float32),
            pltpu.VMEM(one, jnp.float32),
            pltpu.VMEM((4,) + bias.shape, jnp.float32),
            pltpu.VMEM(bias.shape, jnp.float32),
            pltpu.VMEM(bias.shape, jnp.float32),
            pltpu.VMEM(bias.shape, jnp.float32),
            pltpu.VMEM((4, bias.shape[0] // 4, bias.shape[1]), jnp.float32),
            pltpu.SemaphoreType.DMA((17,)),
            pltpu.SemaphoreType.DMA((17,)),
        ],
        compiler_params=pltpu.CompilerParams(
            collective_id=last_exchange, has_side_effects=True, vmem_limit_bytes=24 << 20
        ),
    )(give, keep, bias)


class Traffic:
    def __init__(self, plan):
        self.plan, self.groups = plan, {}

    def add(self, name, group):
        self.groups[name] = group
        return group

    def tie(self, value, near, far, arrived):
        near_messages = [group.near_message() for group in near]
        parts = [group.parts for group in arrived]
        if far:
            value, gots = lax.optimization_barrier((value, [group.got for group in far]))
            for group, got in zip(far, gots):
                group.got = got
        far_messages = [group.far_messages() for group in far]
        value, near_messages, far_messages, parts = lax.optimization_barrier(
            (value, near_messages, far_messages, parts)
        )
        for group, message in zip(near, near_messages):
            group.send_near(message)
        for group, messages in zip(far, far_messages):
            group.send_far(messages)
        for group, part in zip(arrived, parts):
            group.parts = part
        return value

    def input_sum(self, partial_term, kernel):
        if lax.axis_size(dp_axis) != 8:
            return tensor_sum(partial_term, jnp.bfloat16, kernel)[0]
        near, far, arrived = [[self.groups[group] for group in part] for part in self.plan[kernel]]
        partial_term = self.tie(partial_term, near, [], [])
        if kernel == back_encoder + 1:
            group = self.groups[back_encoder]
            done = [self.groups[key] for key in (back_head, back_head + 1, rest_group)]
            totals = [(item.total(), item.square()) for item in done]
            partial_term, group.got[1], totals = lax.optimization_barrier(
                (partial_term, group.got[1], totals)
            )
            for item, (total, square) in zip(done, totals):
                item.owned, item.owned_square = total, square
        total = tensor_sum(partial_term, jnp.bfloat16, kernel)[0]
        total = self.tie(total, [], far, arrived)
        if kernel == back_encoder + 1:
            mix = self.groups[mix_group]
            rest = self.groups[back_encoder]
            total, mix.got, rest.got[2] = lax.optimization_barrier((total, mix.got, rest.got[2]))
            total, messages = lax.optimization_barrier((total, self.encoder_messages()))
            self.encoder_parts = [
                swap(message, dp_axis, 2 * step) for step, message in zip((1, 2, 3), messages)
            ]
        return total

    def arrive(self, value, index):
        if lax.axis_size(dp_axis) != 8:
            return value
        value, self.encoder_parts[index] = lax.optimization_barrier(
            (value, self.encoder_parts[index])
        )
        return value

    def encoder_share(self, place):
        mix, rest = self.groups[mix_group], self.groups[back_encoder]
        return jnp.where(place == 0, mix.share(place), rest.share(place))

    def encoder_messages(self):
        mix, rest = self.groups[mix_group], self.groups[back_encoder]
        high = lax.axis_index(dp_axis) // 2
        level = jnp.maximum(
            jnp.maximum(mix.level, mix.got_level()), jnp.maximum(rest.level, rest.got_level())
        )
        return [
            coded(self.encoder_share(high ^ step), level + 1.0) for step in (1, 2, 3)
        ]

    def encoder_total(self, ahead):
        parts, ahead = lax.optimization_barrier((self.encoder_parts, ahead))
        slab = self.groups[mix_group].slab()
        total = self.encoder_share(lax.axis_index(dp_axis) // 2)
        for part in parts:
            total = total + decoded(part, slab)
        return total, ahead


def first_kernel(
    images,
    notes,
    class_table,
    table_share,
    block_share,
    all_notes,
    classes,
    tables,
    blocks,
    found,
    note_send,
    note_recv,
    class_send,
    class_recv,
    own_sem,
    across_send,
    across_recv,
    *ring_sems,
):
    rank, place_across = lax.axis_index(dp_axis), lax.axis_index(tensor_axis)
    low = lax.rem(place_across, 2)
    partner, across = place_across + 1 - 2 * low, lax.rem(place_across + 2, 4)
    others = [{tensor_axis: partner}, {tensor_axis: across}]
    greet(pltpu.get_barrier_semaphore(), (dp_axis,), others)
    table_ring = RingGather([table_share], [tables.at[place_across]], *ring_sems[:3])
    block_ring = RingGather([block_share], [blocks], *ring_sems[3:])
    note_copies = spread(notes, all_notes, dp_axis, note_send, note_recv)
    all_notes[rank] = notes[...]
    table_ring.begin()
    block_ring.begin()
    for copy in note_copies:
        copy.wait()
    for step in (1, 2, 3):
        table_ring.advance(step)
    block_ring.advance(1)
    table_ring.finish()

    def cross(owner, peer, slot):
        return pltpu.make_async_remote_copy(
            src_ref=tables.at[owner],
            dst_ref=tables.at[owner],
            send_sem=across_send.at[slot],
            recv_sem=across_recv.at[slot],
            device_id={tensor_axis: peer},
            device_id_type=MESH,
        )

    near = cross(place_across, partner, 0)
    far = cross(place_across, across, 1)
    near.start()
    far.start()
    place = lax.broadcasted_iota(jnp.int32, class_table.shape, 1).astype(jnp.float32)
    lane = lax.broadcasted_iota(jnp.int32, found.shape, 1)
    columns = jnp.zeros(found.shape, jnp.float32)
    for image in range(8 * images):
        label = all_notes[image // images, 0:1, image % images : image % images + 1]
        value = jnp.sum(
            jnp.where(place == label, class_table[...], 0.0), axis=1, keepdims=True
        )
        columns = jnp.where(lane == image, value, columns)
    found[...] = columns
    block_ring.advance(2)
    own = pltpu.make_async_copy(found, classes.at[rank], own_sem.at[0])
    own.start()
    class_copies = spread(found, classes, dp_axis, class_send, class_recv)
    near.wait()
    far.wait()
    forward = cross(across, partner, 2)
    forward.start()
    block_ring.advance(3)
    block_ring.finish()
    forward.wait()
    for copy in class_copies:
        copy.wait()
    own.wait()


def gather_first(notes, class_table, images, table_share, block_share):
    rows = class_table.shape[0]
    vmem, anywhere = pl.BlockSpec(memory_space=pltpu.VMEM), pl.BlockSpec(memory_space=pl.ANY)
    return pl.pallas_call(
        functools.partial(first_kernel, images),
        out_shape=[
            jax.ShapeDtypeStruct((8, 8, 128), jnp.float32),
            jax.ShapeDtypeStruct((8, rows, 128), jnp.float32),
            jax.ShapeDtypeStruct((4, 8) + table_share.shape, table_share.dtype),
            jax.ShapeDtypeStruct((8,) + block_share.shape, block_share.dtype),
        ],
        in_specs=[vmem, vmem, anywhere, anywhere],
        out_specs=[vmem, vmem, anywhere, anywhere],
        scratch_shapes=[pltpu.VMEM((rows, 128), jnp.float32)]
        + [pltpu.SemaphoreType.DMA((7,))] * 4
        + [pltpu.SemaphoreType.DMA((1,))]
        + [pltpu.SemaphoreType.DMA((3,))] * 2
        + ring_scratch(1)
        + ring_scratch(1),
        compiler_params=pltpu.CompilerParams(
            collective_id=first_gather, has_side_effects=True, vmem_limit_bytes=16 << 20
        ),
    )(notes, class_table, table_share, block_share)


def take_pieces(vector, starts, counts):
    return jnp.concatenate(
        [lax.dynamic_slice_in_dim(vector, start, count) for start, count in zip(starts, counts)]
    )


def place_pieces(total, pieces, starts):
    full = jnp.zeros((total,), jnp.float32)
    for piece, start in zip(pieces, starts):
        full = lax.dynamic_update_slice_in_dim(full, piece, start, 0)
    return full


def score_block(queries, key_rows, visible):
    scores = jnp.einsum(
        "bqhd,bkhd->bhqk", queries, key_rows, preferred_element_type=jnp.float32
    ) * HEAD ** (-0.5)
    return scores + (visible[:, None, None, :] - 1.0) * 1000000000.0


def attention(queries, key_rows, value_rows, visible):
    scores = score_block(queries, key_rows, visible)
    largest = jnp.max(scores, axis=-1, keepdims=True)
    exponent = jnp.exp(scores - largest)
    normaliser = jnp.sum(exponent, axis=-1, keepdims=True)
    chance = narrow(exponent / normaliser)
    attended = narrow(
        jnp.einsum("bhqk,bkhd->bqhd", chance, value_rows, preferred_element_type=jnp.float32)
    )
    return (attended, largest + jnp.log(normaliser))


def attention_back(queries, key_rows, value_rows, visible, log_total, grad_attended):
    chance = jnp.exp(score_block(queries, key_rows, visible) - log_total)
    grad_values = jnp.einsum(
        "bhqk,bqhd->bkhd", narrow(chance), grad_attended, preferred_element_type=jnp.float32
    )
    grad_chance = jnp.einsum(
        "bqhd,bkhd->bhqk", grad_attended, value_rows, preferred_element_type=jnp.float32
    )
    grad_scores = narrow(
        chance * (grad_chance - jnp.sum(chance * grad_chance, axis=-1, keepdims=True))
    )
    grad_queries = jnp.einsum(
        "bhqk,bkhd->bqhd", grad_scores, key_rows, preferred_element_type=jnp.float32
    ) * HEAD ** (-0.5)
    grad_keys = jnp.einsum(
        "bhqk,bqhd->bkhd", grad_scores, queries, preferred_element_type=jnp.float32
    ) * HEAD ** (-0.5)
    return (grad_queries, grad_keys, grad_values)


def block_forward(
    stream, visible, layer_rows, layer_bias, vectors, kernel, first_shares, last_shares
):
    images = visible.shape[0]
    local_width = D // lax.axis_size(tensor_axis)
    local_ff = FF // lax.axis_size(tensor_axis)
    heads_here = local_width // HEAD
    flat = stream.reshape(-1, D)
    normed = narrow(layer_norm(flat, vectors[0], vectors[1]))
    mixed = narrow(
        product_right(normed, layer_rows[: 3 * local_width]) + layer_bias[: 3 * local_width]
    )
    parts = [
        mixed[:, slot * local_width : (slot + 1) * local_width].reshape(
            images, -1, heads_here, HEAD
        )
        for slot in range(3)
    ]
    attended, log_total = attention(parts[0], parts[1], parts[2], visible)
    attended = attended.reshape(-1, local_width)
    branch, first_wholes = branch_sum(
        product(attended, layer_rows[3 * local_width + local_ff : 4 * local_width + local_ff]),
        kernel,
        first_shares,
    )
    middle = flat + branch + vectors[4]
    second = narrow(layer_norm(middle, vectors[2], vectors[3]))
    inner = (
        product_right(second, layer_rows[3 * local_width : 3 * local_width + local_ff])
        + layer_bias[3 * local_width :]
    )
    active = narrow(exact_gelu(inner))
    branch, last_wholes = branch_sum(
        product(active, layer_rows[4 * local_width + local_ff :]), kernel + 1, last_shares
    )
    result = middle + branch + vectors[5]
    return (
        result.reshape(stream.shape),
        (flat, normed, parts, log_total, attended, middle, second, inner, active),
        first_wholes,
        last_wholes,
    )


def block_back(incoming, visible, layer_rows, vectors, stored, kernel, traffic):
    flat, normed, parts, log_total, attended, middle, second, inner, active = stored
    local_width = D // lax.axis_size(tensor_axis)
    local_ff = FF // lax.axis_size(tensor_axis)
    mix_rows = layer_rows[: 3 * local_width]
    up_rows = layer_rows[3 * local_width : 3 * local_width + local_ff]
    proj_rows = layer_rows[3 * local_width + local_ff : 4 * local_width + local_ff]
    down_rows = layer_rows[4 * local_width + local_ff :]
    flow = incoming.reshape(-1, D)
    grad_branch = narrow(flow)
    grad_active = product_right(grad_branch, down_rows)
    grad_inner = narrow(local_back(exact_gelu, inner, grad_active))
    grad_second = traffic.input_sum(product(grad_inner, up_rows), kernel)
    grad_middle, grad_gain_two, grad_shift_two = jax.vjp(
        layer_norm, middle, vectors[2], vectors[3]
    )[1](grad_second)
    grad_middle = flow + grad_middle
    grad_attn = narrow(grad_middle)
    grad_attended = narrow(product_right(grad_attn, proj_rows)).reshape(parts[0].shape)
    later = [(grad_inner, second), (attended, grad_attn), (active, grad_branch)]
    apart = kernel == back_encoder and lax.axis_size(dp_axis) == 8
    if apart:
        owned_rows = [traffic.add(kernel, Scattered(later, 1, True))]
        grad_attended = traffic.tie(grad_attended, owned_rows, [], [])
    grads_mixed = attention_back(parts[0], parts[1], parts[2], visible, log_total, grad_attended)
    grad_mixed = narrow(
        jnp.concatenate([piece.reshape(-1, local_width) for piece in grads_mixed], axis=1)
    )
    mix = [(grad_mixed, normed)]
    if apart:
        grad_mixed, owned_rows[0].got[0] = lax.optimization_barrier(
            (grad_mixed, owned_rows[0].got[0])
        )
        traffic.add(mix_group, Scattered(mix, -1))
    else:
        owned_rows = [traffic.add(kernel, Scattered(mix + later))]
    grad_normed = traffic.input_sum(product(grad_mixed, mix_rows), kernel + 1)
    grad_flat, grad_gain_one, grad_shift_one = jax.vjp(layer_norm, flat, vectors[0], vectors[1])[1](
        grad_normed
    )
    grad_bias = jnp.concatenate([column_sum(grad_mixed), column_sum(grad_inner)])
    grad_vectors = jnp.stack(
        [
            grad_gain_one,
            grad_shift_one,
            grad_gain_two,
            grad_shift_two,
            column_sum(grad_attn),
            column_sum(grad_branch),
        ]
    )
    return ((grad_middle + grad_flat).reshape(incoming.shape), owned_rows, grad_bias, grad_vectors)


def gathered_parts(columns, count):
    width = columns.shape[1] // count
    blocks = [block.astype(jnp.float32) for block in tensor_blocks(narrow(columns))]
    return [
        jnp.concatenate([block[:, slot * width : (slot + 1) * width] for block in blocks], axis=1)
        for slot in range(count)
    ]


def adaptive_vectors(cond_act, segment_rows, segment_bias):
    local_hidden = HW // lax.axis_size(tensor_axis)
    adaptive = (
        product_right(cond_act, segment_rows[: 3 * local_hidden]) + segment_bias[: 3 * local_hidden]
    )
    return gathered_parts(adaptive, 3)


def head_block(hidden_state, vectors, segment_rows, segment_bias, last_bias, kernel):
    local_hidden = HW // lax.axis_size(tensor_axis)
    shift_vec, scale_vec, gate_vec = vectors
    modulated = narrow(modulate(hidden_state, shift_vec, scale_vec))
    inner = (
        product_right(modulated, segment_rows[3 * local_hidden : 4 * local_hidden])
        + segment_bias[3 * local_hidden :]
    )
    active = narrow(jax.nn.silu(inner))
    branch = branch_sum(product(active, segment_rows[4 * local_hidden :]), kernel)[0] + last_bias
    return (
        hidden_state + gate_vec * branch,
        (hidden_state, shift_vec, scale_vec, gate_vec, modulated, inner, active, branch),
    )


def head_block_back(incoming, cond_act, segment_rows, offset, stored, kernel, traffic):
    hidden_state, shift_vec, scale_vec, gate_vec, modulated, inner, active, branch = stored
    local_hidden = HW // lax.axis_size(tensor_axis)
    grad_gate = incoming * branch
    grad_branch = narrow(incoming * gate_vec)
    grad_active = product_right(grad_branch, segment_rows[4 * local_hidden :])
    grad_inner = narrow(local_back(jax.nn.silu, inner, grad_active))
    grad_modulated = traffic.input_sum(
        product(grad_inner, segment_rows[3 * local_hidden : 4 * local_hidden]), kernel
    )
    grad_hidden, grad_shift, grad_scale = jax.vjp(modulate, hidden_state, shift_vec, scale_vec)[1](
        grad_modulated
    )
    grad_adaptive = narrow(
        jnp.concatenate(
            [
                lax.dynamic_slice_in_dim(piece, offset, local_hidden, 1)
                for piece in (grad_shift, grad_scale, grad_gate)
            ],
            axis=1,
        )
    )
    grad_cond = product(grad_adaptive, segment_rows[: 3 * local_hidden])
    owned_rows = traffic.add(
        kernel,
        Scattered([(grad_adaptive, cond_act), (grad_inner, modulated), (active, grad_branch)]),
    )
    grad_bias = jnp.concatenate([column_sum(grad_adaptive), column_sum(grad_inner)])
    return (incoming + grad_hidden, grad_cond, owned_rows, grad_bias, column_sum(grad_branch))


def adam_update(weight, moment_one, moment_two, gradient, factor, step_num):
    gradient = gradient * factor
    moment_one = beta_first * moment_one + (1.0 - beta_first) * gradient
    moment_two = beta_second * moment_two + (1.0 - beta_second) * gradient * gradient
    fixed_one = moment_one / (1.0 - beta_first**step_num)
    fixed_two = moment_two / (1.0 - beta_second**step_num)
    weight = weight - learn_rate * (
        fixed_one / (jnp.sqrt(fixed_two) + adam_eps) + decay_rate * weight
    )
    return (weight, moment_one, moment_two)


def local(
    block_weights,
    head_weights,
    head_rest,
    embed_tables,
    bias_rows,
    first_blocks,
    second_blocks,
    first_head,
    second_head,
    first_rest,
    second_rest,
    first_tables,
    second_tables,
    first_bias,
    second_bias,
    patches,
    noise,
    token_mask,
    labels,
    drop_marks,
    timesteps,
    step_weights,
    step_count,
):
    tensor_size = lax.axis_size(tensor_axis)
    tensor_index = lax.axis_index(tensor_axis)
    local_width = D // tensor_size
    local_ff = FF // tensor_size
    local_hidden = HW // tensor_size
    offset = tensor_index * local_hidden
    column_starts = [slot * D + tensor_index * local_width for slot in range(3)] + [
        3 * D + tensor_index * local_ff
    ]
    column_counts = [local_width] * 3 + [local_ff]
    head_starts = [slot * HW + offset for slot in range(4)]
    dp_size = lax.axis_size(dp_axis)
    dp_index = lax.axis_index(dp_axis)
    images = patches.shape[0]
    all_images = dp_size * images
    mask_float = token_mask.astype(jnp.float32)
    matches = timesteps[..., None] == jnp.arange(T_STEPS)
    row_weight = (
        jnp.sum(jnp.where(matches, step_weights, 0.0), axis=-1) * mask_float[None]
    ).reshape(-1)
    chosen = jnp.where(drop_marks == 1, CLASSES, labels)
    class_at = TOKD + 1
    class_end = class_at + CLASSES + 1
    weight_here = jnp.sum(row_weight)
    table_share = jnp.concatenate(
        [embed_tables[:, :class_at], embed_tables[:, class_end:]], axis=1
    )
    class_share = embed_tables[:, class_at:class_end]
    block_share = narrow(block_weights)
    whole_here = dp_size == 8 and tensor_size == 4
    if whole_here:
        part = -(-table_share.shape[1] // 32) * 8
        table_share = jnp.pad(table_share, ((0, 0), (0, 4 * part - table_share.shape[1])))
        table_share = lax.dynamic_slice_in_dim(table_share, tensor_index * part, part, 1)
        notes = jnp.zeros((8, 128), jnp.float32)
        notes = lax.dynamic_update_slice(notes, chosen.astype(jnp.float32)[None], (0, 0))
        notes = lax.dynamic_update_slice(notes, weight_here[None, None], (1, 0))
        all_notes, classes, table_parts, first_block = gather_first(
            notes, class_share, images, table_share.T, block_share[0]
        )
        table_rows = table_parts.transpose(0, 2, 1, 3).reshape(4 * part, -1)
        all_chosen = all_notes[:, 0, :images].reshape(-1)
        weight_total = jnp.sum(all_notes[:, 1, 0])
        class_rows = lax.dynamic_slice_in_dim(
            classes.reshape(-1, classes.shape[-1]), dp_index * images, images, 1
        ).T
    else:
        all_chosen = lax.all_gather(chosen, dp_axis, axis=0, tiled=True).astype(jnp.float32)
        weight_total = lax.psum(weight_here, dp_axis)
        table_rows = lax.all_gather(table_share, dp_axis, axis=0, tiled=True).T
        first_block = lax.all_gather(block_share[0], dp_axis)
    picker = (all_chosen[:, None] == jnp.arange(CLASSES + 1)[None, :]).astype(jnp.float32)
    if not whole_here:
        found = lax.dot_general(
            class_share, picker, (((1,), (1,)), ((), ())), precision=highest
        )
        class_rows = lax.dynamic_slice_in_dim(
            lax.all_gather(found, dp_axis, axis=0, tiled=True), dp_index * images, images, 1
        ).T
    first_block = first_block.reshape(-1, D)
    share_rows = block_share[1].shape[0] // 2
    rest_share = narrow(head_rest)
    flat_bias = bias_rows.reshape(-1)
    rest_bias = flat_bias[: 6 * HW].reshape(6, HW)
    head_bias = flat_bias[6 * HW : 6 * HW + 5 * HB * HW].reshape(HB, 5 * HW)
    column_bias = flat_bias[6 * HW + 5 * HB * HW :].reshape(LAYERS, 3 * D + FF)
    table_parts = cut_rows(table_rows, (TOKD, 1, TOK + BUF, TOK + BUF, 1, 6 * LAYERS, 4))
    layer_vectors = table_parts[5].reshape(LAYERS, 6, D)
    final_norms = table_parts[6]
    patch_flat = patches.reshape(-1, TOKD)
    tokens = product(patch_flat, narrow(table_parts[0])) + table_parts[1][0]
    stream = (
        jnp.concatenate(
            [
                jnp.broadcast_to(class_rows[:, None, :], (images, BUF, D)),
                tokens.reshape(images, TOK, D),
            ],
            axis=1,
        )
        + table_parts[2]
    )
    buffer_ones = jnp.ones((images, BUF), jnp.float32)
    visible_enc = jnp.concatenate([buffer_ones, 1.0 - mask_float], axis=1)
    visible_all = jnp.ones((images, TOK + BUF), jnp.float32)
    hidden_rows = jnp.concatenate([0.0 * buffer_ones, mask_float], axis=1)[..., None]
    layer_bias = [
        take_pieces(column_bias[layer], column_starts, column_counts) for layer in range(LAYERS)
    ]
    encoded, stored_enc, first_half, last_half = block_forward(
        stream,
        visible_enc,
        first_block,
        layer_bias[0],
        layer_vectors[0],
        encoder_forward,
        [block_share[1][:share_rows]],
        [block_share[1][share_rows:]],
    )
    encoded, head_share = lax.optimization_barrier((encoded, narrow(head_weights)))
    head_all = lax.all_gather(head_share, dp_axis, axis=1, tiled=True)
    second_block = jnp.concatenate([first_half[0], last_half[0]], axis=1).reshape(-1, D)
    block_all = [first_block, second_block]
    enc_normed = layer_norm(encoded, final_norms[0], final_norms[1])
    decoder_in = enc_normed * (1.0 - hidden_rows) + table_parts[4][0] * hidden_rows + table_parts[3]
    decoded, stored_dec, first_half, last_half = block_forward(
        decoder_in,
        visible_all,
        second_block,
        layer_bias[1],
        layer_vectors[1],
        decoder_forward,
        [rest_share],
        [],
    )
    rest_rows = first_half[0].reshape(-1, rest_share.shape[-1])
    cond_mine, input_mine, output_mine, time_first, second_mine, final_shift, final_scale = cut_rows(
        rest_rows, (D, TOKD, TOKD, HW, HW, HW, HW)
    )
    cond_weight, input_weight, output_weight, time_second = cut_rows(
        tensor_columns(jnp.concatenate([cond_mine, input_mine, output_mine, second_mine], axis=0)),
        (D, TOKD, TOKD, HW),
    )
    latent = narrow(layer_norm(decoded, final_norms[2], final_norms[3])[:, BUF:].reshape(-1, D))
    condition = product(latent, cond_weight) + rest_bias[0]
    decoded, timesteps, noise, clean = lax.optimization_barrier(
        (decoded, timesteps, noise, patch_flat)
    )
    step_rows = timesteps.reshape(COPIES, -1)
    time_feat = narrow(sinusoid(step_rows).reshape(-1, HW))
    time_pre = product(time_feat, time_first) + lax.dynamic_slice_in_dim(
        rest_bias[2], offset, local_hidden
    )
    time_act = tensor_columns(narrow(jax.nn.silu(time_pre)))
    time_embed = product(time_act, time_second) + rest_bias[3]
    cond_vec = (condition[None] + time_embed.reshape(COPIES, -1, HW)).reshape(-1, HW)
    cond_vec, head_all = lax.optimization_barrier((cond_vec, head_all))
    cond_act = narrow(jax.nn.silu(cond_vec))
    phase = step_rows.astype(jnp.float32)[..., None] * (math.pi / (2 * T_STEPS))
    signal_coef = jnp.cos(phase)
    noise_coef = jnp.sin(phase)
    clean = clean.astype(jnp.float32)[None]
    noise_rows = noise.reshape(COPIES, -1, TOKD).astype(jnp.float32)
    noisy_rows = narrow((signal_coef * clean + noise_coef * noise_rows).reshape(-1, TOKD))
    target = (signal_coef * noise_rows - noise_coef * clean).reshape(-1, TOKD)
    hidden_state = product(noisy_rows, input_weight) + rest_bias[1]
    stored_head = []
    segment_biases = [
        take_pieces(head_bias[segment], head_starts, [local_hidden] * 4) for segment in range(HB)
    ]
    head_vectors = [
        adaptive_vectors(cond_act, head_all[segment], segment_biases[segment])
        for segment in range(HB)
    ]
    last_pair = jnp.concatenate(
        [product(cond_act, final_shift), product(cond_act, final_scale)], axis=1
    ) + take_pieces(flat_bias, [4 * HW + offset, 5 * HW + offset], [local_hidden] * 2)
    shift_last, scale_last = gathered_parts(last_pair, 2)
    for segment in range(HB):
        hidden_state, stored = head_block(
            hidden_state,
            head_vectors[segment],
            head_all[segment],
            segment_biases[segment],
            head_bias[segment, 4 * HW :],
            head_forward + segment,
        )
        stored_head.append(stored)
    final_in = narrow(modulate(hidden_state, shift_last, scale_last))
    predicted = product_right(final_in, output_weight)
    sq_error = jnp.mean((predicted - target) ** 2, axis=-1)
    numerator = jnp.sum(row_weight * sq_error)
    grad_pred = narrow(2.0 / (TOKD * weight_total) * row_weight[:, None] * (predicted - target))
    grad_final = product(grad_pred, output_weight)
    grad_hidden, grad_shift_last, grad_scale_last = jax.vjp(
        modulate, hidden_state, shift_last, scale_last
    )[1](grad_final)

    def own_columns(value):
        return lax.dynamic_slice_in_dim(value, offset, local_hidden, 1)

    grad_shift_last = narrow(own_columns(grad_shift_last))
    grad_scale_last = narrow(own_columns(grad_scale_last))
    traffic = Traffic(
        {
            back_head + 1: ([], [], []),
            back_head: ([back_head + 1], [], []),
            back_cond: ([back_head], [back_head + 1], []),
            back_decoder: ([rest_group], [back_head], [back_head + 1]),
            back_decoder + 1: ([back_decoder], [rest_group], [back_head]),
            back_encoder: ([], [back_decoder], [rest_group]),
            back_encoder + 1: ([mix_group], [], [back_decoder]),
        }
    )
    cond_split = product_right(grad_shift_last, final_shift) + product_right(
        grad_scale_last, final_scale
    )
    head_grads = []
    head_bias_grads = []
    for segment in reversed(range(HB)):
        grad_hidden, grad_cond, grad_segment, grad_segment_bias, grad_last_bias = head_block_back(
            grad_hidden,
            cond_act,
            head_all[segment],
            offset,
            stored_head[segment],
            back_head + segment,
            traffic,
        )
        cond_split = cond_split + grad_cond
        head_grads.insert(0, grad_segment)
        pieces = [
            grad_segment_bias[slot * local_hidden : (slot + 1) * local_hidden] for slot in range(4)
        ] + [grad_last_bias / tensor_size]
        head_bias_grads.insert(0, place_pieces(5 * HW, pieces, head_starts + [4 * HW]))
    grad_input = narrow(grad_hidden)
    grad_cond_vec = narrow(local_back(jax.nn.silu, cond_vec, traffic.input_sum(cond_split, back_cond)))
    cond_bias_grad = column_sum(grad_cond_vec)
    grad_time_act = product_right(
        grad_cond_vec, lax.dynamic_slice_in_dim(time_second, offset, local_hidden, 0)
    )
    grad_time_pre = narrow(local_back(jax.nn.silu, time_pre, grad_time_act))
    grad_latent = jnp.sum(product(grad_cond_vec, cond_weight.T).reshape(COPIES, -1, D), axis=0)
    grad_cond_mine = own_columns(grad_cond_vec)
    rest_scattered = Scattered(
        [
            (jnp.tile(latent, (COPIES, 1)), grad_cond_mine),
            (noisy_rows, own_columns(grad_input)),
            (grad_pred, own_columns(final_in)),
            (time_feat, grad_time_pre),
            (time_act, grad_cond_mine),
            (cond_act, grad_shift_last),
            (cond_act, grad_scale_last),
        ]
    )
    traffic.add(rest_group, rest_scattered)
    rest_bias_grad = place_pieces(
        6 * HW,
        [
            cond_bias_grad / tensor_size,
            column_sum(grad_input) / tensor_size,
            column_sum(grad_time_pre),
            cond_bias_grad / tensor_size,
            column_sum(grad_shift_last),
            column_sum(grad_scale_last),
        ],
        [0, HW, 2 * HW + offset, 3 * HW, 4 * HW + offset, 5 * HW + offset],
    )
    grad_top = jnp.concatenate(
        [jnp.zeros((images, BUF, D), jnp.float32), grad_latent.reshape(images, TOK, D)], axis=1
    )
    grad_decoded, grad_gain_dec, grad_shift_dec = jax.vjp(
        layer_norm, decoded, final_norms[2], final_norms[3]
    )[1](grad_top)
    grad_dec_in, grad_rows_dec, grad_bias_dec, grad_vec_dec = block_back(
        grad_decoded, visible_all, block_all[1], layer_vectors[1], stored_dec, back_decoder, traffic
    )
    grad_encoded, grad_gain_enc, grad_shift_enc = jax.vjp(
        layer_norm, encoded, final_norms[0], final_norms[1]
    )[1](grad_dec_in * (1.0 - hidden_rows))
    grad_stream, grad_rows_enc, grad_bias_enc, grad_vec_enc = block_back(
        grad_encoded, visible_enc, block_all[0], layer_vectors[0], stored_enc, back_encoder, traffic
    )
    grad_stream = traffic.arrive(grad_stream, 0)
    bias_parts = [rest_bias_grad] + head_bias_grads
    grad_tokens = narrow(grad_stream[:, BUF:].reshape(-1, D))
    grad_class = lax.dynamic_update_slice_in_dim(
        jnp.zeros((all_images, D), jnp.float32),
        jnp.sum(grad_stream[:, :BUF], axis=1),
        dp_index * images,
        0,
    )
    small_rows = jnp.concatenate(
        [
            column_sum(grad_tokens)[None],
            jnp.sum(grad_dec_in * hidden_rows, axis=(0, 1))[None],
            grad_vec_enc,
            grad_vec_dec,
            jnp.stack([grad_gain_enc, grad_shift_enc, grad_gain_dec, grad_shift_dec]),
            grad_class,
        ],
        axis=0,
    )
    seq_rows = TOK + BUF
    small_at = 2 * seq_rows + TOKD
    table_count = small_at + small_rows.shape[0]
    quarter = -(-table_count // (8 * tensor_size)) * 8
    small_rows = jnp.pad(small_rows, ((0, quarter * tensor_size - table_count), (0, 0)))
    grad_tables = jnp.concatenate(
        [
            jnp.sum(grad_stream, axis=0),
            jnp.sum(grad_dec_in, axis=0),
            product_left(patch_flat, grad_tokens),
            small_rows,
        ],
        axis=0,
    )
    grad_tables = lax.dynamic_slice_in_dim(grad_tables, tensor_index * quarter, quarter, 0)
    column_grads = []
    for grad_local in (grad_bias_enc, grad_bias_dec):
        pieces = [
            grad_local[slot * local_width : (slot + 1) * local_width] for slot in range(3)
        ] + [grad_local[3 * local_width :]]
        column_grads.append(place_pieces(3 * D + FF, pieces, column_starts))
    lanes = bias_rows.shape[1]
    bias_local = jnp.concatenate(bias_parts + column_grads).reshape(-1, lanes)
    if dp_size == 8 and tensor_size == 4:
        bias_count = bias_local.shape[0]
        bias_local = jnp.pad(bias_local, ((0, -bias_count % 32), (0, 0)))
        grad_tables = traffic.arrive(grad_tables, 1)
        owned_cols, bias_grad = tail_exchange(grad_tables.T, bias_local)
        encoder_owned, (owned_cols, bias_grad) = traffic.encoder_total((owned_cols, bias_grad))
        owned_cols = jnp.concatenate([owned_cols[index] for index in range(4)], axis=1)
        bias_grad = bias_grad[:bias_count]
    else:
        owned_cols = tensor_columns(
            lax.psum_scatter(grad_tables.T, dp_axis, scatter_dimension=0, tiled=True)
        )
        bias_grad = sum_everywhere(bias_local, (tensor_axis, dp_axis))
        encoder_owned = grad_rows_enc[0].total()
    class_cols = small_at + 6 * LAYERS + 6
    owned_tables = jnp.concatenate(
        [
            owned_cols[:, 2 * seq_rows : small_at + 1],
            jnp.dot(
                owned_cols[:, class_cols : class_cols + all_images], picker, precision=highest
            ),
            owned_cols[:, : 2 * seq_rows],
            owned_cols[:, small_at + 1 : class_cols],
        ],
        axis=1,
    )
    owned_blocks = jnp.stack([encoder_owned, grad_rows_dec[0].total()])
    owned_head = jnp.stack([group.total() for group in head_grads])
    owned_rest = rest_scattered.total()
    split_squares = (
        jnp.sum(encoder_owned * encoder_owned)
        + grad_rows_dec[0].square()
        + sum(group.square() for group in head_grads)
        + rest_scattered.square()
    )
    shared_squares = jnp.sum(owned_tables * owned_tables) / tensor_size
    every_squares = jnp.sum(bias_grad * bias_grad) / (tensor_size * lax.axis_size(dp_axis))
    last_sums = small_sums(
        [split_squares + shared_squares + every_squares, numerator / tensor_size]
    )
    norm_square = last_sums[0]
    loss_value = last_sums[1] / weight_total
    grad_norm = jnp.sqrt(norm_square)
    factor = jnp.minimum(1.0, clip_limit / (grad_norm + 1e-06))
    step_num = step_count[0].astype(jnp.float32)
    blocks_new, blocks_first, blocks_second = adam_update(
        block_weights, first_blocks, second_blocks, owned_blocks, factor, step_num
    )
    head_new, head_first, head_second = adam_update(
        head_weights, first_head, second_head, owned_head, factor, step_num
    )
    rest_new, rest_first, rest_second = adam_update(
        head_rest, first_rest, second_rest, owned_rest, factor, step_num
    )
    tables_new, tables_first, tables_second = adam_update(
        embed_tables, first_tables, second_tables, owned_tables, factor, step_num
    )
    bias_new, bias_first, bias_second = adam_update(
        bias_rows, first_bias, second_bias, bias_grad, factor, step_num
    )
    return (
        loss_value,
        grad_norm,
        blocks_new,
        blocks_first,
        blocks_second,
        narrow(blocks_new),
        head_new,
        head_first,
        head_second,
        narrow(head_new),
        rest_new,
        rest_first,
        rest_second,
        narrow(rest_new),
        tables_new,
        tables_first,
        tables_second,
        narrow(tables_new),
        bias_new,
        bias_first,
        bias_second,
        narrow(bias_new),
    )


def solution(mesh):
    in_specs = (
        P(None, (dp_axis, tensor_axis), None),
        P(None, (dp_axis, tensor_axis), None),
        P(dp_axis, tensor_axis),
        P(dp_axis, None),
        P(),
        P(None, (dp_axis, tensor_axis), None),
        P(None, (dp_axis, tensor_axis), None),
        P(None, (dp_axis, tensor_axis), None),
        P(None, (dp_axis, tensor_axis), None),
        P(dp_axis, tensor_axis),
        P(dp_axis, tensor_axis),
        P(dp_axis, None),
        P(dp_axis, None),
        P(),
        P(),
        P(dp_axis, None, None),
        P(None, dp_axis, None, None),
        P(dp_axis, None),
        P(dp_axis),
        P(dp_axis),
        P(None, dp_axis, None),
        P(),
        P(),
    )
    out_specs = (
        P(),
        P(),
        P(None, (dp_axis, tensor_axis), None),
        P(None, (dp_axis, tensor_axis), None),
        P(None, (dp_axis, tensor_axis), None),
        P(None, (dp_axis, tensor_axis), None),
        P(None, (dp_axis, tensor_axis), None),
        P(None, (dp_axis, tensor_axis), None),
        P(None, (dp_axis, tensor_axis), None),
        P(None, (dp_axis, tensor_axis), None),
        P(dp_axis, tensor_axis),
        P(dp_axis, tensor_axis),
        P(dp_axis, tensor_axis),
        P(dp_axis, tensor_axis),
        P(dp_axis, None),
        P(dp_axis, None),
        P(dp_axis, None),
        P(dp_axis, None),
        P(),
        P(),
        P(),
        P(),
    )
    return jax.shard_map(local, mesh=mesh, in_specs=in_specs, out_specs=out_specs, check_vma=False)
```

```python
import functools
import math

import jax
import jax.numpy as jnp
from jax import lax
from jax.experimental import pallas as pl
from jax.experimental.pallas import tpu as pltpu
from jax.sharding import PartitionSpec as P

D = 768
HEAD = 64
FF = 3072
HW = 1024
TOKD = 64
CLASSES = 1000
BUF = 64
TOK = 256
T_STEPS = 1000
COPIES = 1
LAYERS = 2
HB = 2


highest = lax.Precision.HIGHEST
norm_eps = 1e-06
beta_first = 0.9
beta_second = 0.95
adam_eps = 1e-08
learn_rate = 0.02
decay_rate = 0.05
clip_limit = 0.002
dp_axis, tensor_axis = "dp", "tensor"


def layer_norm(inputs, gain_vec, offset_vec):
    average = jnp.mean(inputs, axis=-1, keepdims=True)
    centred = inputs - average
    spread = jnp.mean(centred * centred, axis=-1, keepdims=True)
    return centred * lax.rsqrt(spread + norm_eps) * gain_vec + offset_vec


def modulate(inputs, shift_vec, scale_vec):
    return layer_norm(inputs, 1.0, 0.0) * (1.0 + scale_vec) + shift_vec


def exact_gelu(inputs):
    return jax.nn.gelu(inputs, approximate=False)


def local_back(function, inputs, incoming):
    return jax.vjp(function, inputs)[1](incoming)[0]


def sinusoid(step_ids):
    half_width = HW // 2
    frequency = jnp.exp(-math.log(10000.0) * jnp.arange(half_width, dtype=jnp.float32) / half_width)
    angles = step_ids.astype(jnp.float32)[..., None] * frequency
    return jnp.concatenate([jnp.cos(angles), jnp.sin(angles)], axis=-1)


def cut_rows(packed, counts):
    pieces = []
    begin_at = 0
    for count in counts:
        pieces.append(packed[begin_at : begin_at + count])
        begin_at = begin_at + count
    return pieces


def narrow(inputs):
    return inputs.astype(jnp.bfloat16)


def product(left, right):
    return jnp.dot(left, right, preferred_element_type=jnp.float32)


def product_left(left, right):
    return lax.dot_general(
        left, right, (((0,), (0,)), ((), ())), preferred_element_type=jnp.float32
    )


def product_right(left, right):
    return lax.dot_general(
        left, right, (((1,), (1,)), ((), ())), preferred_element_type=jnp.float32
    )


def column_sum(inputs):
    return jnp.sum(inputs.astype(jnp.float32), axis=0)


def swap(value, axis, step):
    return lax.ppermute(value, axis, [(i, i ^ step) for i in range(lax.axis_size(axis))])


MESH = pl.DeviceIdType.MESH
(
    first_gather,
    last_sums_kernel,
    encoder_forward,
    decoder_forward,
    head_forward,
    back_head,
    back_cond,
    back_decoder,
    back_encoder,
    last_exchange,
) = (0, 1, 2, 4, 6, 8, 10, 11, 13, 15)
rest_group, mix_group = 100, 101


class RingGather:
    def __init__(self, shares, wholes, local_sem, send_sem, recv_sem):
        rank = lax.axis_index(dp_axis)
        self.rank, self.low, self.high = rank, lax.rem(rank, 2), lax.div(rank, 2)
        self.beside = rank + 1 - 2 * self.low
        self.ahead = 2 * lax.rem(self.high + 1, 4) + self.low
        self.behind = 2 * lax.rem(self.high + 3, 4) + self.low
        self.shares, self.wholes = [], []
        for share, whole in zip(shares, wholes):
            rows = share.shape[0]
            cut = -(-rows // 32) * 16
            for start, size in ((0, cut), (cut, rows - cut)):
                self.shares.append(share.at[pl.ds(start, size)])
                self.wholes.append(whole.at[:, pl.ds(start, size)])
        shares, wholes = self.shares, self.wholes
        self.send_sem, self.recv_sem = send_sem, recv_sem
        self.items = range(len(shares))
        self.sent = []
        self.own = [
            pltpu.make_async_copy(shares[item], wholes[item].at[rank], local_sem.at[item])
            for item in self.items
        ]

    def copy(self, item, source, place, peer, slot):
        return pltpu.make_async_remote_copy(
            src_ref=source,
            dst_ref=self.wholes[item].at[place],
            send_sem=self.send_sem.at[item, slot],
            recv_sem=self.recv_sem.at[item, slot],
            device_id={dp_axis: peer},
            device_id_type=MESH,
        )

    def send(self, *arguments):
        self.sent.append(self.copy(*arguments))
        self.sent[-1].start()

    def begin(self):
        for item in self.items:
            self.send(item, self.shares[item], self.rank, self.ahead, 0)
            self.send(item, self.shares[item], self.rank, self.beside, 4)
            self.own[item].start()

    def advance(self, step):
        place = 2 * lax.rem(self.high + 4 - step, 4) + self.low
        for item in self.items:
            source = self.wholes[item].at[place]
            self.copy(item, source, place, self.ahead, step - 1).wait_recv()
            if step < 3:
                self.send(item, source, place, self.ahead, step)
            self.send(item, source, place, self.beside, 4 + step)

    def finish(self):
        for step in range(4):
            place = 2 * lax.rem(self.high + 4 - step, 4) + 1 - self.low
            for item in self.items:
                source = self.wholes[item].at[place]
                self.copy(item, source, place, self.beside, 4 + step).wait_recv()
        for sent in self.sent:
            sent.wait_send()
        for kept in self.own:
            kept.wait()


def ring_scratch(arrays):
    count = 2 * arrays
    return [
        pltpu.SemaphoreType.DMA((count,)),
        pltpu.SemaphoreType.DMA((count, 8)),
        pltpu.SemaphoreType.DMA((count, 8)),
    ]


def sum_kernel(count, cross_type, *refs):
    partial, shares = refs[0], refs[1 : 1 + count]
    total, wholes = refs[1 + count], refs[2 + count : 2 + 2 * count]
    near, pair, far, send_sem, recv_sem = refs[2 + 2 * count : 7 + 2 * count]
    rank = lax.axis_index(tensor_axis)
    low = lax.rem(rank, 2)
    partner, across = rank + 1 - 2 * low, lax.rem(rank + 2, 4)
    ring = RingGather(shares, wholes, *refs[7 + 2 * count :]) if count else None
    barrier = pltpu.get_barrier_semaphore()
    for peer in (partner, across):
        pl.semaphore_signal(barrier, inc=1, device_id={tensor_axis: peer}, device_id_type=MESH)
    if ring:
        for peer in (ring.beside, ring.behind):
            pl.semaphore_signal(barrier, inc=1, device_id={dp_axis: peer}, device_id_type=MESH)
    pl.semaphore_wait(barrier, 4 if ring else 2)
    half = partial.shape[0] // 2
    mine = pl.ds(pl.multiple_of(low * half, 8), half)
    others = pl.ds(pl.multiple_of((1 - low) * half, 8), half)

    def copy(source, target, peer, slot):
        return pltpu.make_async_remote_copy(
            src_ref=source,
            dst_ref=target,
            send_sem=send_sem.at[slot],
            recv_sem=recv_sem.at[slot],
            device_id={tensor_axis: peer},
            device_id_type=MESH,
        )

    give = copy(partial.at[others], near, partner, 0)
    cross = copy(pair, far, across, 1)
    back = copy(total.at[mine], total.at[mine], partner, 2)
    give.start()
    if ring:
        ring.begin()
    give.wait()
    pair[...] = (partial[mine, :] + near[...]).astype(cross_type)
    cross.start()
    if ring:
        ring.advance(1)
        ring.advance(2)
    cross.wait()
    total[mine, :] = pair[...].astype(jnp.float32) + far[...].astype(jnp.float32)
    back.start()
    if ring:
        ring.advance(3)
    back.wait()
    if ring:
        ring.finish()


def tensor_sum(partial_term, cross_type, kernel, shares=()):
    ring_here = lax.axis_size(dp_axis) == 8
    wholes = [] if ring_here else [lax.all_gather(share, dp_axis) for share in shares]
    shares = shares if ring_here else ()
    if lax.axis_size(tensor_axis) != 4:
        return lax.psum(partial_term, tensor_axis), wholes
    rows, columns = partial_term.shape
    count = len(shares)
    vmem, anywhere = pl.BlockSpec(memory_space=pltpu.VMEM), pl.BlockSpec(memory_space=pl.ANY)
    outs = pl.pallas_call(
        functools.partial(sum_kernel, count, cross_type),
        out_shape=[jax.ShapeDtypeStruct(partial_term.shape, jnp.float32)]
        + [jax.ShapeDtypeStruct((8,) + share.shape, share.dtype) for share in shares],
        in_specs=[vmem] + [anywhere] * count,
        out_specs=[vmem] + [anywhere] * count,
        scratch_shapes=[
            pltpu.VMEM((rows // 2, columns), jnp.float32),
            pltpu.VMEM((rows // 2, columns), cross_type),
            pltpu.VMEM((rows // 2, columns), cross_type),
            pltpu.SemaphoreType.DMA((3,)),
            pltpu.SemaphoreType.DMA((3,)),
        ]
        + (ring_scratch(count) if count else []),
        compiler_params=pltpu.CompilerParams(
            collective_id=kernel, has_side_effects=True, vmem_limit_bytes=16 << 20
        ),
        cost_estimate=pl.CostEstimate(flops=0, bytes_accessed=2_000_000, transcendentals=0),
    )(partial_term, *shares)
    return outs[0], outs[1:] if ring_here else wholes


def branch_sum(partial_term, kernel, shares=()):
    return tensor_sum(partial_term, jnp.bfloat16, kernel, shares)


def spread(block, slots, axis, send_sem, recv_sem):
    rank, size = lax.axis_index(axis), lax.axis_size(axis)
    copies = []
    for step in range(1, size):
        peer = lax.rem(rank + step, size)
        copies.append(
            pltpu.make_async_remote_copy(
                src_ref=block,
                dst_ref=slots.at[rank],
                send_sem=send_sem.at[step - 1],
                recv_sem=recv_sem.at[step - 1],
                device_id={axis: peer},
                device_id_type=MESH,
            )
        )
        copies[-1].start()
    return copies


def greet(barrier, axes, others=()):
    count = len(others)
    for peer in others:
        pl.semaphore_signal(barrier, inc=1, device_id=peer, device_id_type=MESH)
    for axis in axes:
        rank, size = lax.axis_index(axis), lax.axis_size(axis)
        for step in range(1, size):
            peer = lax.rem(rank + step, size)
            pl.semaphore_signal(barrier, inc=1, device_id={axis: peer}, device_id_type=MESH)
            count += 1
    pl.semaphore_wait(barrier, count)


def small_sum_kernel(value, total, middle, near, far, near_send, near_recv, far_send, far_recv):
    greet(pltpu.get_barrier_semaphore(), (tensor_axis, dp_axis))
    near[lax.axis_index(tensor_axis)] = value[...]
    for copy in spread(value, near, tensor_axis, near_send, near_recv):
        copy.wait()
    middle[...] = functools.reduce(jnp.add, [near[slot] for slot in range(near.shape[0])])
    far[lax.axis_index(dp_axis)] = middle[...]
    for copy in spread(middle, far, dp_axis, far_send, far_recv):
        copy.wait()
    total[...] = functools.reduce(jnp.add, [far[slot] for slot in range(far.shape[0])])


def small_sums(values):
    sizes = [lax.axis_size(tensor_axis), lax.axis_size(dp_axis)]
    if max(sizes) > 8:
        return sum_everywhere(jnp.stack(values), (tensor_axis, dp_axis))
    rows = lax.broadcasted_iota(jnp.int32, (8, 128), 0)
    block = jnp.zeros((8, 128), jnp.float32)
    for row, value in enumerate(values):
        block = jnp.where(rows == row, value, block)
    scratch = [pltpu.VMEM((8, 128), jnp.float32)]
    scratch += [pltpu.VMEM((size, 8, 128), jnp.float32) for size in sizes]
    for size in sizes:
        scratch += [pltpu.SemaphoreType.DMA((size - 1,))] * 2
    total = pl.pallas_call(
        small_sum_kernel,
        out_shape=jax.ShapeDtypeStruct((8, 128), jnp.float32),
        in_specs=[pl.BlockSpec(memory_space=pltpu.VMEM)],
        out_specs=pl.BlockSpec(memory_space=pltpu.VMEM),
        scratch_shapes=scratch,
        compiler_params=pltpu.CompilerParams(
            collective_id=last_sums_kernel, has_side_effects=True
        ),
    )(block)
    return total[:, 0]


def tensor_blocks(piece):
    if lax.axis_size(tensor_axis) != 4:
        return list(lax.all_gather(piece, tensor_axis))
    rank = lax.axis_index(tensor_axis)
    near = swap(piece, tensor_axis, 1)
    far = swap(piece, tensor_axis, 2)
    cross = swap(far, tensor_axis, 1)
    blocks = []
    for index in range(4):
        same_pair = jnp.where(rank == index, piece, near)
        other_pair = jnp.where(rank == index ^ 2, far, cross)
        blocks.append(jnp.where(rank // 2 == index // 2, same_pair, other_pair))
    return blocks


def tensor_columns(piece):
    return jnp.concatenate(tensor_blocks(piece), axis=1)


def sum_everywhere(value, axes):
    for axis in axes:
        step = 1
        while step < lax.axis_size(axis):
            value = value + swap(value, axis, step)
            step = 2 * step
    return value


def pick(blocks, index):
    return lax.dynamic_index_in_dim(blocks, index, 0, keepdims=False)


def bound_level(pairs):
    bounds = [
        left.shape[0]
        * jnp.max(jnp.abs(left.astype(jnp.float32)))
        * jnp.max(jnp.abs(right.astype(jnp.float32)))
        for left, right in pairs
    ]
    return jnp.ceil(jnp.log2(jnp.maximum(functools.reduce(jnp.maximum, bounds), 2.0**-100)))


def coded(values, level):
    rows = values.shape[0]
    padded = jnp.pad(values * jnp.exp2(13.0 - level), ((0, 16), (0, 0)))
    is_value = lax.broadcasted_iota(jnp.int32, padded.shape, 0) < rows
    return jnp.where(is_value, padded, level).astype(jnp.float16)


def decoded(message, rows):
    level = message[rows : rows + 1].astype(jnp.float32)
    return message[:rows].astype(jnp.float32) * jnp.exp2(level - 13.0)


class Scattered:
    def __init__(self, pairs, first=0, split=False):
        self.pairs, self.first, self.split = pairs, max(first, 0), split
        self.count = 4 - first if first >= 0 else -first
        self.got, self.parts, self.owned, self.owned_square = None, None, None, None
        self.level = bound_level(pairs)
        self.product = None

    def grad(self):
        if self.product is None:
            self.product = jnp.concatenate(
                [product_left(left, right) for left, right in self.pairs], axis=0
            )
        return self.product

    def slab(self):
        return self.grad().shape[0] // (2 * self.count)

    def near_message(self):
        grad, slab = self.grad(), self.slab()
        low = lax.axis_index(dp_axis) % 2
        blocks = grad.reshape(self.count, 2 * slab, grad.shape[1])
        give = lax.dynamic_slice_in_dim(blocks, (1 - low) * slab, slab, 1)
        if self.split:
            return [coded(give[place], self.level) for place in range(self.count)]
        return coded(give.reshape(-1, grad.shape[1]), self.level)

    def send_near(self, message):
        parts = [swap(part, dp_axis, 1) for part in (message if self.split else [message])]
        self.got = parts if self.split else parts[0]

    def got_level(self):
        slab = self.slab()
        got, at = (self.got[0], slab) if self.split else (self.got, self.count * slab)
        return got[at : at + 1].astype(jnp.float32)

    def share(self, place):
        grad, slab = self.grad(), self.slab()
        low = lax.axis_index(dp_axis) % 2
        place = jnp.clip(place - self.first, 0, self.count - 1)
        kept = lax.dynamic_slice_in_dim(grad, (2 * place + low) * slab, slab, 0)
        if self.split:
            arrived = self.got[0][:slab]
            for index in range(1, self.count):
                arrived = jnp.where(place == index, self.got[index][:slab], arrived)
        else:
            arrived = lax.dynamic_slice_in_dim(self.got, place * slab, slab, 0)
        return kept + arrived.astype(jnp.float32) * jnp.exp2(self.got_level() - 13.0)

    def far_messages(self):
        high = lax.axis_index(dp_axis) // 2
        level = jnp.maximum(self.level, self.got_level()) + 1.0
        return [coded(self.share(high ^ step), level) for step in (1, 2, 3)]

    def send_far(self, messages):
        self.parts = []
        for step, message in zip((1, 2, 3), messages):
            pairs = [
                (2 * source + side, 2 * (source ^ step) + side)
                for source in range(4)
                for side in range(2)
                if self.first <= source ^ step < self.first + self.count
            ]
            self.parts.append(lax.ppermute(message, dp_axis, pairs))

    def square(self):
        if self.owned_square is None:
            self.owned_square = jnp.sum(self.total() ** 2)
        return self.owned_square

    def total(self):
        if self.owned is None:
            self.owned = self.summed()
        return self.owned

    def summed(self):
        if lax.axis_size(dp_axis) != 8:
            return lax.psum_scatter(self.grad(), dp_axis, scatter_dimension=0, tiled=True)
        slab = self.slab()
        total = self.share(lax.axis_index(dp_axis) // 2)
        for part in self.parts:
            total = total + decoded(part, slab)
        return total


def tail_kernel(*refs):
    give, keep, bias, tables, bias_total = refs[:5]
    got, pairs, far, own, near, middle, beside_sum, pair_sum, far_sum, send_sem, recv_sem = refs[5:]
    rank, across = lax.axis_index(dp_axis), lax.axis_index(tensor_axis)
    low, high = lax.rem(rank, 2), lax.div(rank, 2)
    beside = {dp_axis: rank + 1 - 2 * low}
    pair_peers = [{dp_axis: 2 * lax.rem(high + step, 4) + low} for step in (1, 2, 3)]
    tensor_peers = [{tensor_axis: lax.rem(across + step, 4)} for step in (1, 2, 3)]
    barrier = pltpu.get_barrier_semaphore()
    peers = [beside] + pair_peers + tensor_peers
    for peer in peers:
        pl.semaphore_signal(barrier, inc=1, device_id=peer, device_id_type=MESH)
    pl.semaphore_wait(barrier, len(peers))
    slots = iter(range(17))

    def send(source, target, peer):
        slot = next(slots)
        copy = pltpu.make_async_remote_copy(
            src_ref=source,
            dst_ref=target,
            send_sem=send_sem.at[slot],
            recv_sem=recv_sem.at[slot],
            device_id=peer,
            device_id_type=MESH,
        )
        copy.start()
        return copy

    tables_near = send(give, got, beside)
    bias_near = [send(bias, near.at[across], peer) for peer in tensor_peers]
    near[across] = bias[...]
    tables_near.wait()
    pairs[...] = keep[...] + got[...]
    tables_far = [
        send(pairs.at[lax.rem(high + step, 4)], far.at[step - 1], pair_peers[step - 1])
        for step in (1, 2, 3)
    ]
    for copy in bias_near:
        copy.wait()
    middle[...] = near[0] + near[1] + near[2] + near[3]
    send(middle, beside_sum, beside).wait()
    pair_sum[...] = middle[...] + beside_sum[...]
    rows = bias_total.shape[0] // 4
    mine = pl.ds(pl.multiple_of(across * rows, 8), rows)
    far_sum[high] = pair_sum[mine, :]
    bias_far = [send(pair_sum.at[mine], far_sum.at[high], peer) for peer in pair_peers]
    for copy in tables_far:
        copy.wait()
    own[...] = pairs[high] + far[0] + far[1] + far[2]
    tables[across] = own[...]
    tables_all = [send(own, tables.at[across], peer) for peer in tensor_peers]
    for copy in bias_far:
        copy.wait()
    bias_total[mine, :] = far_sum[0] + far_sum[1] + far_sum[2] + far_sum[3]
    bias_all = [send(bias_total.at[mine], bias_total.at[mine], peer) for peer in tensor_peers]
    for copy in tables_all + bias_all:
        copy.wait()


def tail_exchange(tables, bias):
    low = lax.axis_index(dp_axis) % 2
    slab, columns = tables.shape[0] // 8, tables.shape[1]
    blocks = tables.reshape(4, 2 * slab, columns)
    keep = lax.dynamic_slice_in_dim(blocks, low * slab, slab, 1)
    give = lax.dynamic_slice_in_dim(blocks, (1 - low) * slab, slab, 1)
    four, one = keep.shape, (slab, columns)
    vmem = pl.BlockSpec(memory_space=pltpu.VMEM)
    return pl.pallas_call(
        tail_kernel,
        out_shape=[
            jax.ShapeDtypeStruct(four, jnp.float32),
            jax.ShapeDtypeStruct(bias.shape, jnp.float32),
        ],
        in_specs=[vmem] * 3,
        out_specs=[vmem] * 2,
        scratch_shapes=[
            pltpu.VMEM(four, jnp.float32),
            pltpu.VMEM(four, jnp.float32),
            pltpu.VMEM((3,) + one, jnp.float32),
            pltpu.VMEM(one, jnp.float32),
            pltpu.VMEM((4,) + bias.shape, jnp.float32),
            pltpu.VMEM(bias.shape, jnp.float32),
            pltpu.VMEM(bias.shape, jnp.float32),
            pltpu.VMEM(bias.shape, jnp.float32),
            pltpu.VMEM((4, bias.shape[0] // 4, bias.shape[1]), jnp.float32),
            pltpu.SemaphoreType.DMA((17,)),
            pltpu.SemaphoreType.DMA((17,)),
        ],
        compiler_params=pltpu.CompilerParams(
            collective_id=last_exchange, has_side_effects=True, vmem_limit_bytes=24 << 20
        ),
    )(give, keep, bias)


class Traffic:
    def __init__(self, plan):
        self.plan, self.groups = plan, {}

    def add(self, name, group):
        self.groups[name] = group
        return group

    def tie(self, value, near, far, arrived):
        near_messages = [group.near_message() for group in near]
        parts = [group.parts for group in arrived]
        if far:
            value, gots = lax.optimization_barrier((value, [group.got for group in far]))
            for group, got in zip(far, gots):
                group.got = got
        far_messages = [group.far_messages() for group in far]
        value, near_messages, far_messages, parts = lax.optimization_barrier(
            (value, near_messages, far_messages, parts)
        )
        for group, message in zip(near, near_messages):
            group.send_near(message)
        for group, messages in zip(far, far_messages):
            group.send_far(messages)
        for group, part in zip(arrived, parts):
            group.parts = part
        return value

    def input_sum(self, partial_term, kernel):
        if lax.axis_size(dp_axis) != 8:
            return tensor_sum(partial_term, jnp.bfloat16, kernel)[0]
        near, far, arrived = [[self.groups[group] for group in part] for part in self.plan[kernel]]
        partial_term = self.tie(partial_term, near, [], [])
        if kernel == back_encoder + 1:
            group = self.groups[back_encoder]
            done = [self.groups[key] for key in (back_head, back_head + 1, rest_group)]
            totals = [(item.total(), item.square()) for item in done]
            partial_term, group.got[1], totals = lax.optimization_barrier(
                (partial_term, group.got[1], totals)
            )
            for item, (total, square) in zip(done, totals):
                item.owned, item.owned_square = total, square
        total = tensor_sum(partial_term, jnp.bfloat16, kernel)[0]
        total = self.tie(total, [], far, arrived)
        if kernel == back_encoder + 1:
            mix = self.groups[mix_group]
            rest = self.groups[back_encoder]
            total, mix.got, rest.got[2] = lax.optimization_barrier((total, mix.got, rest.got[2]))
            decoder = self.groups[back_decoder]
            total, messages, decoder.parts = lax.optimization_barrier(
                (total, self.encoder_messages(), decoder.parts)
            )
            self.encoder_parts = [
                swap(message, dp_axis, 2 * step) for step, message in zip((1, 2, 3), messages)
            ]
        return total

    def arrive(self, value, index):
        if lax.axis_size(dp_axis) != 8:
            return value
        value, self.encoder_parts[index] = lax.optimization_barrier(
            (value, self.encoder_parts[index])
        )
        return value

    def encoder_share(self, place):
        mix, rest = self.groups[mix_group], self.groups[back_encoder]
        return jnp.where(place == 0, mix.share(place), rest.share(place))

    def encoder_messages(self):
        mix, rest = self.groups[mix_group], self.groups[back_encoder]
        high = lax.axis_index(dp_axis) // 2
        level = jnp.maximum(
            jnp.maximum(mix.level, mix.got_level()), jnp.maximum(rest.level, rest.got_level())
        )
        return [
            coded(self.encoder_share(high ^ step), level + 1.0) for step in (1, 2, 3)
        ]

    def encoder_total(self, ahead):
        parts, ahead = lax.optimization_barrier((self.encoder_parts, ahead))
        slab = self.groups[mix_group].slab()
        total = self.encoder_share(lax.axis_index(dp_axis) // 2)
        for part in parts:
            total = total + decoded(part, slab)
        return total, ahead


def first_kernel(
    images,
    notes,
    class_table,
    table_share,
    block_share,
    all_notes,
    classes,
    tables,
    blocks,
    found,
    note_send,
    note_recv,
    class_send,
    class_recv,
    own_sem,
    across_send,
    across_recv,
    *ring_sems,
):
    rank, place_across = lax.axis_index(dp_axis), lax.axis_index(tensor_axis)
    low = lax.rem(place_across, 2)
    partner, across = place_across + 1 - 2 * low, lax.rem(place_across + 2, 4)
    others = [{tensor_axis: partner}, {tensor_axis: across}]
    greet(pltpu.get_barrier_semaphore(), (dp_axis,), others)
    table_ring = RingGather([table_share], [tables.at[place_across]], *ring_sems[:3])
    block_ring = RingGather([block_share], [blocks], *ring_sems[3:])
    note_copies = spread(notes, all_notes, dp_axis, note_send, note_recv)
    all_notes[rank] = notes[...]
    table_ring.begin()
    block_ring.begin()
    for copy in note_copies:
        copy.wait()
    for step in (1, 2, 3):
        table_ring.advance(step)
    block_ring.advance(1)
    table_ring.finish()

    def cross(owner, peer, slot):
        return pltpu.make_async_remote_copy(
            src_ref=tables.at[owner],
            dst_ref=tables.at[owner],
            send_sem=across_send.at[slot],
            recv_sem=across_recv.at[slot],
            device_id={tensor_axis: peer},
            device_id_type=MESH,
        )

    near = cross(place_across, partner, 0)
    far = cross(place_across, across, 1)
    near.start()
    far.start()
    place = lax.broadcasted_iota(jnp.int32, class_table.shape, 1).astype(jnp.float32)
    lane = lax.broadcasted_iota(jnp.int32, found.shape, 1)
    columns = jnp.zeros(found.shape, jnp.float32)
    for image in range(8 * images):
        label = all_notes[image // images, 0:1, image % images : image % images + 1]
        value = jnp.sum(
            jnp.where(place == label, class_table[...], 0.0), axis=1, keepdims=True
        )
        columns = jnp.where(lane == image, value, columns)
    found[...] = columns
    block_ring.advance(2)
    own = pltpu.make_async_copy(found, classes.at[rank], own_sem.at[0])
    own.start()
    class_copies = spread(found, classes, dp_axis, class_send, class_recv)
    near.wait()
    far.wait()
    forward = cross(across, partner, 2)
    forward.start()
    block_ring.advance(3)
    block_ring.finish()
    forward.wait()
    for copy in class_copies:
        copy.wait()
    own.wait()


def gather_first(notes, class_table, images, table_share, block_share):
    rows = class_table.shape[0]
    vmem, anywhere = pl.BlockSpec(memory_space=pltpu.VMEM), pl.BlockSpec(memory_space=pl.ANY)
    return pl.pallas_call(
        functools.partial(first_kernel, images),
        out_shape=[
            jax.ShapeDtypeStruct((8, 8, 128), jnp.float32),
            jax.ShapeDtypeStruct((8, rows, 128), jnp.float32),
            jax.ShapeDtypeStruct((4, 8) + table_share.shape, table_share.dtype),
            jax.ShapeDtypeStruct((8,) + block_share.shape, block_share.dtype),
        ],
        in_specs=[vmem, vmem, anywhere, anywhere],
        out_specs=[vmem, vmem, anywhere, anywhere],
        scratch_shapes=[pltpu.VMEM((rows, 128), jnp.float32)]
        + [pltpu.SemaphoreType.DMA((7,))] * 4
        + [pltpu.SemaphoreType.DMA((1,))]
        + [pltpu.SemaphoreType.DMA((3,))] * 2
        + ring_scratch(1)
        + ring_scratch(1),
        compiler_params=pltpu.CompilerParams(
            collective_id=first_gather, has_side_effects=True, vmem_limit_bytes=16 << 20
        ),
    )(notes, class_table, table_share, block_share)


def take_pieces(vector, starts, counts):
    return jnp.concatenate(
        [lax.dynamic_slice_in_dim(vector, start, count) for start, count in zip(starts, counts)]
    )


def place_pieces(total, pieces, starts):
    full = jnp.zeros((total,), jnp.float32)
    for piece, start in zip(pieces, starts):
        full = lax.dynamic_update_slice_in_dim(full, piece, start, 0)
    return full


def score_block(queries, key_rows, visible):
    scores = jnp.einsum(
        "bqhd,bkhd->bhqk", queries, key_rows, preferred_element_type=jnp.float32
    ) * HEAD ** (-0.5)
    return scores + (visible[:, None, None, :] - 1.0) * 1000000000.0


def attention(queries, key_rows, value_rows, visible):
    scores = score_block(queries, key_rows, visible)
    largest = jnp.max(scores, axis=-1, keepdims=True)
    exponent = jnp.exp(scores - largest)
    normaliser = jnp.sum(exponent, axis=-1, keepdims=True)
    chance = narrow(exponent / normaliser)
    attended = narrow(
        jnp.einsum("bhqk,bkhd->bqhd", chance, value_rows, preferred_element_type=jnp.float32)
    )
    return (attended, largest + jnp.log(normaliser))


def attention_back(queries, key_rows, value_rows, visible, log_total, grad_attended):
    chance = jnp.exp(score_block(queries, key_rows, visible) - log_total)
    grad_values = jnp.einsum(
        "bhqk,bqhd->bkhd", narrow(chance), grad_attended, preferred_element_type=jnp.float32
    )
    grad_chance = jnp.einsum(
        "bqhd,bkhd->bhqk", grad_attended, value_rows, preferred_element_type=jnp.float32
    )
    grad_scores = narrow(
        chance * (grad_chance - jnp.sum(chance * grad_chance, axis=-1, keepdims=True))
    )
    grad_queries = jnp.einsum(
        "bhqk,bkhd->bqhd", grad_scores, key_rows, preferred_element_type=jnp.float32
    ) * HEAD ** (-0.5)
    grad_keys = jnp.einsum(
        "bhqk,bqhd->bkhd", grad_scores, queries, preferred_element_type=jnp.float32
    ) * HEAD ** (-0.5)
    return (grad_queries, grad_keys, grad_values)


def block_forward(
    stream, visible, layer_rows, layer_bias, vectors, kernel, first_shares, last_shares
):
    images = visible.shape[0]
    local_width = D // lax.axis_size(tensor_axis)
    local_ff = FF // lax.axis_size(tensor_axis)
    heads_here = local_width // HEAD
    flat = stream.reshape(-1, D)
    normed = narrow(layer_norm(flat, vectors[0], vectors[1]))
    mixed = narrow(
        product_right(normed, layer_rows[: 3 * local_width]) + layer_bias[: 3 * local_width]
    )
    parts = [
        mixed[:, slot * local_width : (slot + 1) * local_width].reshape(
            images, -1, heads_here, HEAD
        )
        for slot in range(3)
    ]
    attended, log_total = attention(parts[0], parts[1], parts[2], visible)
    attended = attended.reshape(-1, local_width)
    branch, first_wholes = branch_sum(
        product(attended, layer_rows[3 * local_width + local_ff : 4 * local_width + local_ff]),
        kernel,
        first_shares,
    )
    middle = flat + branch + vectors[4]
    second = narrow(layer_norm(middle, vectors[2], vectors[3]))
    inner = (
        product_right(second, layer_rows[3 * local_width : 3 * local_width + local_ff])
        + layer_bias[3 * local_width :]
    )
    active = narrow(exact_gelu(inner))
    branch, last_wholes = branch_sum(
        product(active, layer_rows[4 * local_width + local_ff :]), kernel + 1, last_shares
    )
    result = middle + branch + vectors[5]
    return (
        result.reshape(stream.shape),
        (flat, normed, parts, log_total, attended, middle, second, inner, active),
        first_wholes,
        last_wholes,
    )


def block_back(incoming, visible, layer_rows, vectors, stored, kernel, traffic):
    flat, normed, parts, log_total, attended, middle, second, inner, active = stored
    local_width = D // lax.axis_size(tensor_axis)
    local_ff = FF // lax.axis_size(tensor_axis)
    mix_rows = layer_rows[: 3 * local_width]
    up_rows = layer_rows[3 * local_width : 3 * local_width + local_ff]
    proj_rows = layer_rows[3 * local_width + local_ff : 4 * local_width + local_ff]
    down_rows = layer_rows[4 * local_width + local_ff :]
    flow = incoming.reshape(-1, D)
    grad_branch = narrow(flow)
    grad_active = product_right(grad_branch, down_rows)
    grad_inner = narrow(local_back(exact_gelu, inner, grad_active))
    grad_second = traffic.input_sum(product(grad_inner, up_rows), kernel)
    grad_middle, grad_gain_two, grad_shift_two = jax.vjp(
        layer_norm, middle, vectors[2], vectors[3]
    )[1](grad_second)
    grad_middle = flow + grad_middle
    grad_attn = narrow(grad_middle)
    grad_attended = narrow(product_right(grad_attn, proj_rows)).reshape(parts[0].shape)
    later = [(grad_inner, second), (attended, grad_attn), (active, grad_branch)]
    apart = kernel == back_encoder and lax.axis_size(dp_axis) == 8
    if apart:
        owned_rows = [traffic.add(kernel, Scattered(later, 1, True))]
        grad_attended = traffic.tie(grad_attended, owned_rows, [], [])
    grads_mixed = attention_back(parts[0], parts[1], parts[2], visible, log_total, grad_attended)
    grad_mixed = narrow(
        jnp.concatenate([piece.reshape(-1, local_width) for piece in grads_mixed], axis=1)
    )
    mix = [(grad_mixed, normed)]
    if apart:
        grad_mixed, owned_rows[0].got[0] = lax.optimization_barrier(
            (grad_mixed, owned_rows[0].got[0])
        )
        traffic.add(mix_group, Scattered(mix, -1))
    else:
        owned_rows = [traffic.add(kernel, Scattered(mix + later))]
    grad_normed = traffic.input_sum(product(grad_mixed, mix_rows), kernel + 1)
    grad_flat, grad_gain_one, grad_shift_one = jax.vjp(layer_norm, flat, vectors[0], vectors[1])[1](
        grad_normed
    )
    grad_bias = jnp.concatenate([column_sum(grad_mixed), column_sum(grad_inner)])
    grad_vectors = jnp.stack(
        [
            grad_gain_one,
            grad_shift_one,
            grad_gain_two,
            grad_shift_two,
            column_sum(grad_attn),
            column_sum(grad_branch),
        ]
    )
    return ((grad_middle + grad_flat).reshape(incoming.shape), owned_rows, grad_bias, grad_vectors)


def gathered_parts(columns, count):
    width = columns.shape[1] // count
    blocks = [block.astype(jnp.float32) for block in tensor_blocks(narrow(columns))]
    return [
        jnp.concatenate([block[:, slot * width : (slot + 1) * width] for block in blocks], axis=1)
        for slot in range(count)
    ]


def adaptive_vectors(cond_act, segment_rows, segment_bias):
    local_hidden = HW // lax.axis_size(tensor_axis)
    adaptive = (
        product_right(cond_act, segment_rows[: 3 * local_hidden]) + segment_bias[: 3 * local_hidden]
    )
    return gathered_parts(adaptive, 3)


def head_block(hidden_state, vectors, segment_rows, segment_bias, last_bias, kernel):
    local_hidden = HW // lax.axis_size(tensor_axis)
    shift_vec, scale_vec, gate_vec = vectors
    modulated = narrow(modulate(hidden_state, shift_vec, scale_vec))
    inner = (
        product_right(modulated, segment_rows[3 * local_hidden : 4 * local_hidden])
        + segment_bias[3 * local_hidden :]
    )
    active = narrow(jax.nn.silu(inner))
    branch = branch_sum(product(active, segment_rows[4 * local_hidden :]), kernel)[0] + last_bias
    return (
        hidden_state + gate_vec * branch,
        (hidden_state, shift_vec, scale_vec, gate_vec, modulated, inner, active, branch),
    )


def head_block_back(incoming, cond_act, segment_rows, offset, stored, kernel, traffic):
    hidden_state, shift_vec, scale_vec, gate_vec, modulated, inner, active, branch = stored
    local_hidden = HW // lax.axis_size(tensor_axis)
    grad_gate = incoming * branch
    grad_branch = narrow(incoming * gate_vec)
    grad_active = product_right(grad_branch, segment_rows[4 * local_hidden :])
    grad_inner = narrow(local_back(jax.nn.silu, inner, grad_active))
    grad_modulated = traffic.input_sum(
        product(grad_inner, segment_rows[3 * local_hidden : 4 * local_hidden]), kernel
    )
    grad_hidden, grad_shift, grad_scale = jax.vjp(modulate, hidden_state, shift_vec, scale_vec)[1](
        grad_modulated
    )
    grad_adaptive = narrow(
        jnp.concatenate(
            [
                lax.dynamic_slice_in_dim(piece, offset, local_hidden, 1)
                for piece in (grad_shift, grad_scale, grad_gate)
            ],
            axis=1,
        )
    )
    grad_cond = product(grad_adaptive, segment_rows[: 3 * local_hidden])
    owned_rows = traffic.add(
        kernel,
        Scattered([(grad_adaptive, cond_act), (grad_inner, modulated), (active, grad_branch)]),
    )
    grad_bias = jnp.concatenate([column_sum(grad_adaptive), column_sum(grad_inner)])
    return (incoming + grad_hidden, grad_cond, owned_rows, grad_bias, column_sum(grad_branch))


def adam_update(weight, moment_one, moment_two, gradient, factor, step_num):
    gradient = gradient * factor
    moment_one = beta_first * moment_one + (1.0 - beta_first) * gradient
    moment_two = beta_second * moment_two + (1.0 - beta_second) * gradient * gradient
    fixed_one = moment_one / (1.0 - beta_first**step_num)
    fixed_two = moment_two / (1.0 - beta_second**step_num)
    weight = weight - learn_rate * (
        fixed_one / (jnp.sqrt(fixed_two) + adam_eps) + decay_rate * weight
    )
    return (weight, moment_one, moment_two)


def local(
    block_weights,
    head_weights,
    head_rest,
    embed_tables,
    bias_rows,
    first_blocks,
    second_blocks,
    first_head,
    second_head,
    first_rest,
    second_rest,
    first_tables,
    second_tables,
    first_bias,
    second_bias,
    patches,
    noise,
    token_mask,
    labels,
    drop_marks,
    timesteps,
    step_weights,
    step_count,
):
    tensor_size = lax.axis_size(tensor_axis)
    tensor_index = lax.axis_index(tensor_axis)
    local_width = D // tensor_size
    local_ff = FF // tensor_size
    local_hidden = HW // tensor_size
    offset = tensor_index * local_hidden
    column_starts = [slot * D + tensor_index * local_width for slot in range(3)] + [
        3 * D + tensor_index * local_ff
    ]
    column_counts = [local_width] * 3 + [local_ff]
    head_starts = [slot * HW + offset for slot in range(4)]
    dp_size = lax.axis_size(dp_axis)
    dp_index = lax.axis_index(dp_axis)
    images = patches.shape[0]
    all_images = dp_size * images
    mask_float = token_mask.astype(jnp.float32)
    matches = timesteps[..., None] == jnp.arange(T_STEPS)
    row_weight = (
        jnp.sum(jnp.where(matches, step_weights, 0.0), axis=-1) * mask_float[None]
    ).reshape(-1)
    chosen = jnp.where(drop_marks == 1, CLASSES, labels)
    class_at = TOKD + 1
    class_end = class_at + CLASSES + 1
    weight_here = jnp.sum(row_weight)
    table_share = jnp.concatenate(
        [embed_tables[:, :class_at], embed_tables[:, class_end:]], axis=1
    )
    class_share = embed_tables[:, class_at:class_end]
    block_share = narrow(block_weights)
    whole_here = dp_size == 8 and tensor_size == 4
    if whole_here:
        part = -(-table_share.shape[1] // 32) * 8
        table_share = jnp.pad(table_share, ((0, 0), (0, 4 * part - table_share.shape[1])))
        table_share = lax.dynamic_slice_in_dim(table_share, tensor_index * part, part, 1)
        notes = jnp.zeros((8, 128), jnp.float32)
        notes = lax.dynamic_update_slice(notes, chosen.astype(jnp.float32)[None], (0, 0))
        notes = lax.dynamic_update_slice(notes, weight_here[None, None], (1, 0))
        all_notes, classes, table_parts, first_block = gather_first(
            notes, class_share, images, table_share.T, block_share[0]
        )
        table_rows = table_parts.transpose(0, 2, 1, 3).reshape(4 * part, -1)
        all_chosen = all_notes[:, 0, :images].reshape(-1)
        weight_total = jnp.sum(all_notes[:, 1, 0])
        class_rows = lax.dynamic_slice_in_dim(
            classes.reshape(-1, classes.shape[-1]), dp_index * images, images, 1
        ).T
    else:
        all_chosen = lax.all_gather(chosen, dp_axis, axis=0, tiled=True).astype(jnp.float32)
        weight_total = lax.psum(weight_here, dp_axis)
        table_rows = lax.all_gather(table_share, dp_axis, axis=0, tiled=True).T
        first_block = lax.all_gather(block_share[0], dp_axis)
    picker = (all_chosen[:, None] == jnp.arange(CLASSES + 1)[None, :]).astype(jnp.float32)
    if not whole_here:
        found = lax.dot_general(
            class_share, picker, (((1,), (1,)), ((), ())), precision=highest
        )
        class_rows = lax.dynamic_slice_in_dim(
            lax.all_gather(found, dp_axis, axis=0, tiled=True), dp_index * images, images, 1
        ).T
    first_block = first_block.reshape(-1, D)
    share_rows = block_share[1].shape[0] // 2
    rest_share = narrow(head_rest)
    flat_bias = bias_rows.reshape(-1)
    rest_bias = flat_bias[: 6 * HW].reshape(6, HW)
    head_bias = flat_bias[6 * HW : 6 * HW + 5 * HB * HW].reshape(HB, 5 * HW)
    column_bias = flat_bias[6 * HW + 5 * HB * HW :].reshape(LAYERS, 3 * D + FF)
    table_parts = cut_rows(table_rows, (TOKD, 1, TOK + BUF, TOK + BUF, 1, 6 * LAYERS, 4))
    layer_vectors = table_parts[5].reshape(LAYERS, 6, D)
    final_norms = table_parts[6]
    patch_flat = patches.reshape(-1, TOKD)
    tokens = product(patch_flat, narrow(table_parts[0])) + table_parts[1][0]
    stream = (
        jnp.concatenate(
            [
                jnp.broadcast_to(class_rows[:, None, :], (images, BUF, D)),
                tokens.reshape(images, TOK, D),
            ],
            axis=1,
        )
        + table_parts[2]
    )
    buffer_ones = jnp.ones((images, BUF), jnp.float32)
    visible_enc = jnp.concatenate([buffer_ones, 1.0 - mask_float], axis=1)
    visible_all = jnp.ones((images, TOK + BUF), jnp.float32)
    hidden_rows = jnp.concatenate([0.0 * buffer_ones, mask_float], axis=1)[..., None]
    layer_bias = [
        take_pieces(column_bias[layer], column_starts, column_counts) for layer in range(LAYERS)
    ]
    encoded, stored_enc, first_half, last_half = block_forward(
        stream,
        visible_enc,
        first_block,
        layer_bias[0],
        layer_vectors[0],
        encoder_forward,
        [block_share[1][:share_rows]],
        [block_share[1][share_rows:]],
    )
    encoded, head_share = lax.optimization_barrier((encoded, narrow(head_weights)))
    head_all = lax.all_gather(head_share, dp_axis, axis=1, tiled=True)
    second_block = jnp.concatenate([first_half[0], last_half[0]], axis=1).reshape(-1, D)
    block_all = [first_block, second_block]
    enc_normed = layer_norm(encoded, final_norms[0], final_norms[1])
    decoder_in = enc_normed * (1.0 - hidden_rows) + table_parts[4][0] * hidden_rows + table_parts[3]
    decoded, stored_dec, first_half, last_half = block_forward(
        decoder_in,
        visible_all,
        second_block,
        layer_bias[1],
        layer_vectors[1],
        decoder_forward,
        [rest_share],
        [],
    )
    rest_rows = first_half[0].reshape(-1, rest_share.shape[-1])
    cond_mine, input_mine, output_mine, time_first, second_mine, final_shift, final_scale = cut_rows(
        rest_rows, (D, TOKD, TOKD, HW, HW, HW, HW)
    )
    cond_weight, input_weight, output_weight, time_second = cut_rows(
        tensor_columns(jnp.concatenate([cond_mine, input_mine, output_mine, second_mine], axis=0)),
        (D, TOKD, TOKD, HW),
    )
    latent = narrow(layer_norm(decoded, final_norms[2], final_norms[3])[:, BUF:].reshape(-1, D))
    condition = product(latent, cond_weight) + rest_bias[0]
    decoded, timesteps, noise, clean = lax.optimization_barrier(
        (decoded, timesteps, noise, patch_flat)
    )
    step_rows = timesteps.reshape(COPIES, -1)
    time_feat = narrow(sinusoid(step_rows).reshape(-1, HW))
    time_pre = product(time_feat, time_first) + lax.dynamic_slice_in_dim(
        rest_bias[2], offset, local_hidden
    )
    time_act = tensor_columns(narrow(jax.nn.silu(time_pre)))
    time_embed = product(time_act, time_second) + rest_bias[3]
    cond_vec = (condition[None] + time_embed.reshape(COPIES, -1, HW)).reshape(-1, HW)
    cond_vec, head_all = lax.optimization_barrier((cond_vec, head_all))
    cond_act = narrow(jax.nn.silu(cond_vec))
    phase = step_rows.astype(jnp.float32)[..., None] * (math.pi / (2 * T_STEPS))
    signal_coef = jnp.cos(phase)
    noise_coef = jnp.sin(phase)
    clean = clean.astype(jnp.float32)[None]
    noise_rows = noise.reshape(COPIES, -1, TOKD).astype(jnp.float32)
    noisy_rows = narrow((signal_coef * clean + noise_coef * noise_rows).reshape(-1, TOKD))
    target = (signal_coef * noise_rows - noise_coef * clean).reshape(-1, TOKD)
    hidden_state = product(noisy_rows, input_weight) + rest_bias[1]
    stored_head = []
    segment_biases = [
        take_pieces(head_bias[segment], head_starts, [local_hidden] * 4) for segment in range(HB)
    ]
    head_vectors = [
        adaptive_vectors(cond_act, head_all[segment], segment_biases[segment])
        for segment in range(HB)
    ]
    last_pair = jnp.concatenate(
        [product(cond_act, final_shift), product(cond_act, final_scale)], axis=1
    ) + take_pieces(flat_bias, [4 * HW + offset, 5 * HW + offset], [local_hidden] * 2)
    shift_last, scale_last = gathered_parts(last_pair, 2)
    for segment in range(HB):
        hidden_state, stored = head_block(
            hidden_state,
            head_vectors[segment],
            head_all[segment],
            segment_biases[segment],
            head_bias[segment, 4 * HW :],
            head_forward + segment,
        )
        stored_head.append(stored)
    final_in = narrow(modulate(hidden_state, shift_last, scale_last))
    predicted = product_right(final_in, output_weight)
    sq_error = jnp.mean((predicted - target) ** 2, axis=-1)
    numerator = jnp.sum(row_weight * sq_error)
    grad_pred = narrow(2.0 / (TOKD * weight_total) * row_weight[:, None] * (predicted - target))
    grad_final = product(grad_pred, output_weight)
    grad_hidden, grad_shift_last, grad_scale_last = jax.vjp(
        modulate, hidden_state, shift_last, scale_last
    )[1](grad_final)

    def own_columns(value):
        return lax.dynamic_slice_in_dim(value, offset, local_hidden, 1)

    grad_shift_last = narrow(own_columns(grad_shift_last))
    grad_scale_last = narrow(own_columns(grad_scale_last))
    traffic = Traffic(
        {
            back_head + 1: ([], [], []),
            back_head: ([back_head + 1], [], []),
            back_cond: ([back_head], [back_head + 1], []),
            back_decoder: ([rest_group], [back_head], [back_head + 1]),
            back_decoder + 1: ([back_decoder], [rest_group], [back_head]),
            back_encoder: ([], [back_decoder], [rest_group]),
            back_encoder + 1: ([mix_group], [], [back_decoder]),
        }
    )
    cond_split = product_right(grad_shift_last, final_shift) + product_right(
        grad_scale_last, final_scale
    )
    head_grads = []
    head_bias_grads = []
    for segment in reversed(range(HB)):
        grad_hidden, grad_cond, grad_segment, grad_segment_bias, grad_last_bias = head_block_back(
            grad_hidden,
            cond_act,
            head_all[segment],
            offset,
            stored_head[segment],
            back_head + segment,
            traffic,
        )
        cond_split = cond_split + grad_cond
        head_grads.insert(0, grad_segment)
        pieces = [
            grad_segment_bias[slot * local_hidden : (slot + 1) * local_hidden] for slot in range(4)
        ] + [grad_last_bias / tensor_size]
        head_bias_grads.insert(0, place_pieces(5 * HW, pieces, head_starts + [4 * HW]))
    grad_input = narrow(grad_hidden)
    grad_cond_vec = narrow(local_back(jax.nn.silu, cond_vec, traffic.input_sum(cond_split, back_cond)))
    cond_bias_grad = column_sum(grad_cond_vec)
    grad_time_act = product_right(
        grad_cond_vec, lax.dynamic_slice_in_dim(time_second, offset, local_hidden, 0)
    )
    grad_time_pre = narrow(local_back(jax.nn.silu, time_pre, grad_time_act))
    grad_latent = jnp.sum(product(grad_cond_vec, cond_weight.T).reshape(COPIES, -1, D), axis=0)
    grad_cond_mine = own_columns(grad_cond_vec)
    rest_scattered = Scattered(
        [
            (jnp.tile(latent, (COPIES, 1)), grad_cond_mine),
            (noisy_rows, own_columns(grad_input)),
            (grad_pred, own_columns(final_in)),
            (time_feat, grad_time_pre),
            (time_act, grad_cond_mine),
            (cond_act, grad_shift_last),
            (cond_act, grad_scale_last),
        ]
    )
    traffic.add(rest_group, rest_scattered)
    rest_bias_grad = place_pieces(
        6 * HW,
        [
            cond_bias_grad / tensor_size,
            column_sum(grad_input) / tensor_size,
            column_sum(grad_time_pre),
            cond_bias_grad / tensor_size,
            column_sum(grad_shift_last),
            column_sum(grad_scale_last),
        ],
        [0, HW, 2 * HW + offset, 3 * HW, 4 * HW + offset, 5 * HW + offset],
    )
    grad_top = jnp.concatenate(
        [jnp.zeros((images, BUF, D), jnp.float32), grad_latent.reshape(images, TOK, D)], axis=1
    )
    grad_decoded, grad_gain_dec, grad_shift_dec = jax.vjp(
        layer_norm, decoded, final_norms[2], final_norms[3]
    )[1](grad_top)
    grad_dec_in, grad_rows_dec, grad_bias_dec, grad_vec_dec = block_back(
        grad_decoded, visible_all, block_all[1], layer_vectors[1], stored_dec, back_decoder, traffic
    )
    grad_encoded, grad_gain_enc, grad_shift_enc = jax.vjp(
        layer_norm, encoded, final_norms[0], final_norms[1]
    )[1](grad_dec_in * (1.0 - hidden_rows))
    grad_stream, grad_rows_enc, grad_bias_enc, grad_vec_enc = block_back(
        grad_encoded, visible_enc, block_all[0], layer_vectors[0], stored_enc, back_encoder, traffic
    )
    grad_stream = traffic.arrive(grad_stream, 0)
    bias_parts = [rest_bias_grad] + head_bias_grads
    grad_tokens = narrow(grad_stream[:, BUF:].reshape(-1, D))
    grad_class = lax.dynamic_update_slice_in_dim(
        jnp.zeros((all_images, D), jnp.float32),
        jnp.sum(grad_stream[:, :BUF], axis=1),
        dp_index * images,
        0,
    )
    small_rows = jnp.concatenate(
        [
            column_sum(grad_tokens)[None],
            jnp.sum(grad_dec_in * hidden_rows, axis=(0, 1))[None],
            grad_vec_enc,
            grad_vec_dec,
            jnp.stack([grad_gain_enc, grad_shift_enc, grad_gain_dec, grad_shift_dec]),
            grad_class,
        ],
        axis=0,
    )
    seq_rows = TOK + BUF
    small_at = 2 * seq_rows + TOKD
    table_count = small_at + small_rows.shape[0]
    quarter = -(-table_count // (8 * tensor_size)) * 8
    small_rows = jnp.pad(small_rows, ((0, quarter * tensor_size - table_count), (0, 0)))
    grad_tables = jnp.concatenate(
        [
            jnp.sum(grad_stream, axis=0),
            jnp.sum(grad_dec_in, axis=0),
            product_left(patch_flat, grad_tokens),
            small_rows,
        ],
        axis=0,
    )
    grad_tables = lax.dynamic_slice_in_dim(grad_tables, tensor_index * quarter, quarter, 0)
    column_grads = []
    for grad_local in (grad_bias_enc, grad_bias_dec):
        pieces = [
            grad_local[slot * local_width : (slot + 1) * local_width] for slot in range(3)
        ] + [grad_local[3 * local_width :]]
        column_grads.append(place_pieces(3 * D + FF, pieces, column_starts))
    lanes = bias_rows.shape[1]
    bias_local = jnp.concatenate(bias_parts + column_grads).reshape(-1, lanes)
    if dp_size == 8 and tensor_size == 4:
        bias_count = bias_local.shape[0]
        bias_local = jnp.pad(bias_local, ((0, -bias_count % 32), (0, 0)))
        grad_tables = traffic.arrive(grad_tables, 1)
        owned_cols, bias_grad = tail_exchange(grad_tables.T, bias_local)
        encoder_owned, (owned_cols, bias_grad) = traffic.encoder_total((owned_cols, bias_grad))
        owned_cols = jnp.concatenate([owned_cols[index] for index in range(4)], axis=1)
        bias_grad = bias_grad[:bias_count]
    else:
        owned_cols = tensor_columns(
            lax.psum_scatter(grad_tables.T, dp_axis, scatter_dimension=0, tiled=True)
        )
        bias_grad = sum_everywhere(bias_local, (tensor_axis, dp_axis))
        encoder_owned = grad_rows_enc[0].total()
    class_cols = small_at + 6 * LAYERS + 6
    owned_tables = jnp.concatenate(
        [
            owned_cols[:, 2 * seq_rows : small_at + 1],
            jnp.dot(
                owned_cols[:, class_cols : class_cols + all_images], picker, precision=highest
            ),
            owned_cols[:, : 2 * seq_rows],
            owned_cols[:, small_at + 1 : class_cols],
        ],
        axis=1,
    )
    owned_blocks = jnp.stack([encoder_owned, grad_rows_dec[0].total()])
    owned_head = jnp.stack([group.total() for group in head_grads])
    owned_rest = rest_scattered.total()
    split_squares = (
        jnp.sum(encoder_owned * encoder_owned)
        + grad_rows_dec[0].square()
        + sum(group.square() for group in head_grads)
        + rest_scattered.square()
    )
    shared_squares = jnp.sum(owned_tables * owned_tables) / tensor_size
    every_squares = jnp.sum(bias_grad * bias_grad) / (tensor_size * lax.axis_size(dp_axis))
    last_sums = small_sums(
        [split_squares + shared_squares + every_squares, numerator / tensor_size]
    )
    norm_square = last_sums[0]
    loss_value = last_sums[1] / weight_total
    grad_norm = jnp.sqrt(norm_square)
    factor = jnp.minimum(1.0, clip_limit / (grad_norm + 1e-06))
    step_num = step_count[0].astype(jnp.float32)
    blocks_new, blocks_first, blocks_second = adam_update(
        block_weights, first_blocks, second_blocks, owned_blocks, factor, step_num
    )
    head_new, head_first, head_second = adam_update(
        head_weights, first_head, second_head, owned_head, factor, step_num
    )
    rest_new, rest_first, rest_second = adam_update(
        head_rest, first_rest, second_rest, owned_rest, factor, step_num
    )
    tables_new, tables_first, tables_second = adam_update(
        embed_tables, first_tables, second_tables, owned_tables, factor, step_num
    )
    bias_new, bias_first, bias_second = adam_update(
        bias_rows, first_bias, second_bias, bias_grad, factor, step_num
    )
    return (
        loss_value,
        grad_norm,
        blocks_new,
        blocks_first,
        blocks_second,
        narrow(blocks_new),
        head_new,
        head_first,
        head_second,
        narrow(head_new),
        rest_new,
        rest_first,
        rest_second,
        narrow(rest_new),
        tables_new,
        tables_first,
        tables_second,
        narrow(tables_new),
        bias_new,
        bias_first,
        bias_second,
        narrow(bias_new),
    )


def solution(mesh):
    in_specs = (
        P(None, (dp_axis, tensor_axis), None),
        P(None, (dp_axis, tensor_axis), None),
        P(dp_axis, tensor_axis),
        P(dp_axis, None),
        P(),
        P(None, (dp_axis, tensor_axis), None),
        P(None, (dp_axis, tensor_axis), None),
        P(None, (dp_axis, tensor_axis), None),
        P(None, (dp_axis, tensor_axis), None),
        P(dp_axis, tensor_axis),
        P(dp_axis, tensor_axis),
        P(dp_axis, None),
        P(dp_axis, None),
        P(),
        P(),
        P(dp_axis, None, None),
        P(None, dp_axis, None, None),
        P(dp_axis, None),
        P(dp_axis),
        P(dp_axis),
        P(None, dp_axis, None),
        P(),
        P(),
    )
    out_specs = (
        P(),
        P(),
        P(None, (dp_axis, tensor_axis), None),
        P(None, (dp_axis, tensor_axis), None),
        P(None, (dp_axis, tensor_axis), None),
        P(None, (dp_axis, tensor_axis), None),
        P(None, (dp_axis, tensor_axis), None),
        P(None, (dp_axis, tensor_axis), None),
        P(None, (dp_axis, tensor_axis), None),
        P(None, (dp_axis, tensor_axis), None),
        P(dp_axis, tensor_axis),
        P(dp_axis, tensor_axis),
        P(dp_axis, tensor_axis),
        P(dp_axis, tensor_axis),
        P(dp_axis, None),
        P(dp_axis, None),
        P(dp_axis, None),
        P(dp_axis, None),
        P(),
        P(),
        P(),
        P(),
    )
    return jax.shard_map(local, mesh=mesh, in_specs=in_specs, out_specs=out_specs, check_vma=False)
```

```python
import functools
import math

import jax
import jax.numpy as jnp
from jax import lax
from jax.experimental import pallas as pl
from jax.experimental.pallas import tpu as pltpu
from jax.sharding import PartitionSpec as P

D = 768
HEAD = 64
FF = 3072
HW = 1024
TOKD = 64
CLASSES = 1000
BUF = 64
TOK = 256
T_STEPS = 1000
COPIES = 1
LAYERS = 2
HB = 2


highest = lax.Precision.HIGHEST
norm_eps = 1e-06
beta_first = 0.9
beta_second = 0.95
adam_eps = 1e-08
learn_rate = 0.02
decay_rate = 0.05
clip_limit = 0.002
dp_axis, tensor_axis = "dp", "tensor"


def layer_norm(inputs, gain_vec, offset_vec):
    average = jnp.mean(inputs, axis=-1, keepdims=True)
    centred = inputs - average
    spread = jnp.mean(centred * centred, axis=-1, keepdims=True)
    return centred * lax.rsqrt(spread + norm_eps) * gain_vec + offset_vec


def modulate(inputs, shift_vec, scale_vec):
    return layer_norm(inputs, 1.0, 0.0) * (1.0 + scale_vec) + shift_vec


def exact_gelu(inputs):
    return jax.nn.gelu(inputs, approximate=False)


def local_back(function, inputs, incoming):
    return jax.vjp(function, inputs)[1](incoming)[0]


def sinusoid(step_ids):
    half_width = HW // 2
    frequency = jnp.exp(-math.log(10000.0) * jnp.arange(half_width, dtype=jnp.float32) / half_width)
    angles = step_ids.astype(jnp.float32)[..., None] * frequency
    return jnp.concatenate([jnp.cos(angles), jnp.sin(angles)], axis=-1)


def cut_rows(packed, counts):
    pieces = []
    begin_at = 0
    for count in counts:
        pieces.append(packed[begin_at : begin_at + count])
        begin_at = begin_at + count
    return pieces


def narrow(inputs):
    return inputs.astype(jnp.bfloat16)


def product(left, right):
    return jnp.dot(left, right, preferred_element_type=jnp.float32)


def product_left(left, right):
    return lax.dot_general(
        left, right, (((0,), (0,)), ((), ())), preferred_element_type=jnp.float32
    )


def product_right(left, right):
    return lax.dot_general(
        left, right, (((1,), (1,)), ((), ())), preferred_element_type=jnp.float32
    )


def column_sum(inputs):
    return jnp.sum(inputs.astype(jnp.float32), axis=0)


def swap(value, axis, step):
    return lax.ppermute(value, axis, [(i, i ^ step) for i in range(lax.axis_size(axis))])


MESH = pl.DeviceIdType.MESH
(
    first_gather,
    last_sums_kernel,
    encoder_forward,
    decoder_forward,
    head_forward,
    back_head,
    back_cond,
    back_decoder,
    back_encoder,
    last_exchange,
) = (0, 1, 2, 4, 6, 8, 10, 11, 13, 15)
rest_group, mix_group = 100, 101


class RingGather:
    def __init__(self, shares, wholes, local_sem, send_sem, recv_sem):
        rank = lax.axis_index(dp_axis)
        self.rank, self.low, self.high = rank, lax.rem(rank, 2), lax.div(rank, 2)
        self.beside = rank + 1 - 2 * self.low
        self.ahead = 2 * lax.rem(self.high + 1, 4) + self.low
        self.behind = 2 * lax.rem(self.high + 3, 4) + self.low
        self.shares, self.wholes = [], []
        for share, whole in zip(shares, wholes):
            rows = share.shape[0]
            cut = -(-rows // 32) * 16
            for start, size in ((0, cut), (cut, rows - cut)):
                self.shares.append(share.at[pl.ds(start, size)])
                self.wholes.append(whole.at[:, pl.ds(start, size)])
        shares, wholes = self.shares, self.wholes
        self.send_sem, self.recv_sem = send_sem, recv_sem
        self.items = range(len(shares))
        self.sent = []
        self.own = [
            pltpu.make_async_copy(shares[item], wholes[item].at[rank], local_sem.at[item])
            for item in self.items
        ]

    def copy(self, item, source, place, peer, slot):
        return pltpu.make_async_remote_copy(
            src_ref=source,
            dst_ref=self.wholes[item].at[place],
            send_sem=self.send_sem.at[item, slot],
            recv_sem=self.recv_sem.at[item, slot],
            device_id={dp_axis: peer},
            device_id_type=MESH,
        )

    def send(self, *arguments):
        self.sent.append(self.copy(*arguments))
        self.sent[-1].start()

    def begin(self):
        for item in self.items:
            self.send(item, self.shares[item], self.rank, self.ahead, 0)
            self.send(item, self.shares[item], self.rank, self.beside, 4)
            self.own[item].start()

    def advance(self, step):
        place = 2 * lax.rem(self.high + 4 - step, 4) + self.low
        for item in self.items:
            source = self.wholes[item].at[place]
            self.copy(item, source, place, self.ahead, step - 1).wait_recv()
            if step < 3:
                self.send(item, source, place, self.ahead, step)
            self.send(item, source, place, self.beside, 4 + step)

    def finish(self):
        for step in range(4):
            place = 2 * lax.rem(self.high + 4 - step, 4) + 1 - self.low
            for item in self.items:
                source = self.wholes[item].at[place]
                self.copy(item, source, place, self.beside, 4 + step).wait_recv()
        for sent in self.sent:
            sent.wait_send()
        for kept in self.own:
            kept.wait()


def ring_scratch(arrays):
    count = 2 * arrays
    return [
        pltpu.SemaphoreType.DMA((count,)),
        pltpu.SemaphoreType.DMA((count, 8)),
        pltpu.SemaphoreType.DMA((count, 8)),
    ]


def sum_kernel(count, cross_type, *refs):
    partial, shares = refs[0], refs[1 : 1 + count]
    total, wholes = refs[1 + count], refs[2 + count : 2 + 2 * count]
    near, pair, far, send_sem, recv_sem = refs[2 + 2 * count : 7 + 2 * count]
    rank = lax.axis_index(tensor_axis)
    low = lax.rem(rank, 2)
    partner, across = rank + 1 - 2 * low, lax.rem(rank + 2, 4)
    ring = RingGather(shares, wholes, *refs[7 + 2 * count :]) if count else None
    barrier = pltpu.get_barrier_semaphore()
    for peer in (partner, across):
        pl.semaphore_signal(barrier, inc=1, device_id={tensor_axis: peer}, device_id_type=MESH)
    if ring:
        for peer in (ring.beside, ring.behind):
            pl.semaphore_signal(barrier, inc=1, device_id={dp_axis: peer}, device_id_type=MESH)
    pl.semaphore_wait(barrier, 4 if ring else 2)
    half = partial.shape[0] // 2
    mine = pl.ds(pl.multiple_of(low * half, 8), half)
    others = pl.ds(pl.multiple_of((1 - low) * half, 8), half)

    def copy(source, target, peer, slot):
        return pltpu.make_async_remote_copy(
            src_ref=source,
            dst_ref=target,
            send_sem=send_sem.at[slot],
            recv_sem=recv_sem.at[slot],
            device_id={tensor_axis: peer},
            device_id_type=MESH,
        )

    give = copy(partial.at[others], near, partner, 0)
    cross = copy(pair, far, across, 1)
    back = copy(total.at[mine], total.at[mine], partner, 2)
    give.start()
    if ring:
        ring.begin()
    give.wait()
    pair[...] = (partial[mine, :] + near[...]).astype(cross_type)
    cross.start()
    if ring:
        ring.advance(1)
        ring.advance(2)
    cross.wait()
    total[mine, :] = pair[...].astype(jnp.float32) + far[...].astype(jnp.float32)
    back.start()
    if ring:
        ring.advance(3)
    back.wait()
    if ring:
        ring.finish()


def tensor_sum(partial_term, cross_type, kernel, shares=()):
    ring_here = lax.axis_size(dp_axis) == 8
    wholes = [] if ring_here else [lax.all_gather(share, dp_axis) for share in shares]
    shares = shares if ring_here else ()
    if lax.axis_size(tensor_axis) != 4:
        return lax.psum(partial_term, tensor_axis), wholes
    rows, columns = partial_term.shape
    count = len(shares)
    vmem, anywhere = pl.BlockSpec(memory_space=pltpu.VMEM), pl.BlockSpec(memory_space=pl.ANY)
    outs = pl.pallas_call(
        functools.partial(sum_kernel, count, cross_type),
        out_shape=[jax.ShapeDtypeStruct(partial_term.shape, jnp.float32)]
        + [jax.ShapeDtypeStruct((8,) + share.shape, share.dtype) for share in shares],
        in_specs=[vmem] + [anywhere] * count,
        out_specs=[vmem] + [anywhere] * count,
        scratch_shapes=[
            pltpu.VMEM((rows // 2, columns), jnp.float32),
            pltpu.VMEM((rows // 2, columns), cross_type),
            pltpu.VMEM((rows // 2, columns), cross_type),
            pltpu.SemaphoreType.DMA((3,)),
            pltpu.SemaphoreType.DMA((3,)),
        ]
        + (ring_scratch(count) if count else []),
        compiler_params=pltpu.CompilerParams(
            collective_id=kernel, has_side_effects=True, vmem_limit_bytes=16 << 20
        ),
        cost_estimate=pl.CostEstimate(flops=0, bytes_accessed=2_000_000, transcendentals=0),
    )(partial_term, *shares)
    return outs[0], outs[1:] if ring_here else wholes


def branch_sum(partial_term, kernel, shares=()):
    return tensor_sum(partial_term, jnp.bfloat16, kernel, shares)


def spread(block, slots, axis, send_sem, recv_sem):
    rank, size = lax.axis_index(axis), lax.axis_size(axis)
    copies = []
    for step in range(1, size):
        peer = lax.rem(rank + step, size)
        copies.append(
            pltpu.make_async_remote_copy(
                src_ref=block,
                dst_ref=slots.at[rank],
                send_sem=send_sem.at[step - 1],
                recv_sem=recv_sem.at[step - 1],
                device_id={axis: peer},
                device_id_type=MESH,
            )
        )
        copies[-1].start()
    return copies


def greet(barrier, axes, others=()):
    count = len(others)
    for peer in others:
        pl.semaphore_signal(barrier, inc=1, device_id=peer, device_id_type=MESH)
    for axis in axes:
        rank, size = lax.axis_index(axis), lax.axis_size(axis)
        for step in range(1, size):
            peer = lax.rem(rank + step, size)
            pl.semaphore_signal(barrier, inc=1, device_id={axis: peer}, device_id_type=MESH)
            count += 1
    pl.semaphore_wait(barrier, count)


def small_sum_kernel(value, total, middle, near, far, near_send, near_recv, far_send, far_recv):
    greet(pltpu.get_barrier_semaphore(), (tensor_axis, dp_axis))
    near[lax.axis_index(tensor_axis)] = value[...]
    for copy in spread(value, near, tensor_axis, near_send, near_recv):
        copy.wait()
    middle[...] = functools.reduce(jnp.add, [near[slot] for slot in range(near.shape[0])])
    far[lax.axis_index(dp_axis)] = middle[...]
    for copy in spread(middle, far, dp_axis, far_send, far_recv):
        copy.wait()
    total[...] = functools.reduce(jnp.add, [far[slot] for slot in range(far.shape[0])])


def small_sums(values):
    sizes = [lax.axis_size(tensor_axis), lax.axis_size(dp_axis)]
    if max(sizes) > 8:
        return sum_everywhere(jnp.stack(values), (tensor_axis, dp_axis))
    rows = lax.broadcasted_iota(jnp.int32, (8, 128), 0)
    block = jnp.zeros((8, 128), jnp.float32)
    for row, value in enumerate(values):
        block = jnp.where(rows == row, value, block)
    scratch = [pltpu.VMEM((8, 128), jnp.float32)]
    scratch += [pltpu.VMEM((size, 8, 128), jnp.float32) for size in sizes]
    for size in sizes:
        scratch += [pltpu.SemaphoreType.DMA((size - 1,))] * 2
    total = pl.pallas_call(
        small_sum_kernel,
        out_shape=jax.ShapeDtypeStruct((8, 128), jnp.float32),
        in_specs=[pl.BlockSpec(memory_space=pltpu.VMEM)],
        out_specs=pl.BlockSpec(memory_space=pltpu.VMEM),
        scratch_shapes=scratch,
        compiler_params=pltpu.CompilerParams(
            collective_id=last_sums_kernel, has_side_effects=True
        ),
    )(block)
    return total[:, 0]


def tensor_blocks(piece):
    if lax.axis_size(tensor_axis) != 4:
        return list(lax.all_gather(piece, tensor_axis))
    rank = lax.axis_index(tensor_axis)
    near = swap(piece, tensor_axis, 1)
    far = swap(piece, tensor_axis, 2)
    cross = swap(far, tensor_axis, 1)
    blocks = []
    for index in range(4):
        same_pair = jnp.where(rank == index, piece, near)
        other_pair = jnp.where(rank == index ^ 2, far, cross)
        blocks.append(jnp.where(rank // 2 == index // 2, same_pair, other_pair))
    return blocks


def tensor_columns(piece):
    return jnp.concatenate(tensor_blocks(piece), axis=1)


def sum_everywhere(value, axes):
    for axis in axes:
        step = 1
        while step < lax.axis_size(axis):
            value = value + swap(value, axis, step)
            step = 2 * step
    return value


def pick(blocks, index):
    return lax.dynamic_index_in_dim(blocks, index, 0, keepdims=False)


def bound_level(pairs):
    bounds = [
        left.shape[0]
        * jnp.max(jnp.abs(left.astype(jnp.float32)))
        * jnp.max(jnp.abs(right.astype(jnp.float32)))
        for left, right in pairs
    ]
    return jnp.ceil(jnp.log2(jnp.maximum(functools.reduce(jnp.maximum, bounds), 2.0**-100)))


def coded(values, level):
    rows = values.shape[0]
    padded = jnp.pad(values * jnp.exp2(13.0 - level), ((0, 16), (0, 0)))
    is_value = lax.broadcasted_iota(jnp.int32, padded.shape, 0) < rows
    return jnp.where(is_value, padded, level).astype(jnp.float16)


def decoded(message, rows):
    level = message[rows : rows + 1].astype(jnp.float32)
    return message[:rows].astype(jnp.float32) * jnp.exp2(level - 13.0)


class Scattered:
    def __init__(self, pairs, first=0, split=False):
        self.pairs, self.first, self.split = pairs, max(first, 0), split
        self.count = 4 - first if first >= 0 else -first
        self.got, self.parts, self.owned, self.owned_square = None, None, None, None
        self.level = bound_level(pairs)
        self.product = None

    def grad(self):
        if self.product is None:
            self.product = jnp.concatenate(
                [product_left(left, right) for left, right in self.pairs], axis=0
            )
        return self.product

    def slab(self):
        return self.grad().shape[0] // (2 * self.count)

    def near_message(self):
        grad, slab = self.grad(), self.slab()
        low = lax.axis_index(dp_axis) % 2
        blocks = grad.reshape(self.count, 2 * slab, grad.shape[1])
        give = lax.dynamic_slice_in_dim(blocks, (1 - low) * slab, slab, 1)
        if self.split:
            return [coded(give[place], self.level) for place in range(self.count)]
        return coded(give.reshape(-1, grad.shape[1]), self.level)

    def send_near(self, message):
        parts = [swap(part, dp_axis, 1) for part in (message if self.split else [message])]
        self.got = parts if self.split else parts[0]

    def got_level(self):
        slab = self.slab()
        got, at = (self.got[0], slab) if self.split else (self.got, self.count * slab)
        return got[at : at + 1].astype(jnp.float32)

    def share(self, place):
        grad, slab = self.grad(), self.slab()
        low = lax.axis_index(dp_axis) % 2
        place = jnp.clip(place - self.first, 0, self.count - 1)
        kept = lax.dynamic_slice_in_dim(grad, (2 * place + low) * slab, slab, 0)
        if self.split:
            arrived = self.got[0][:slab]
            for index in range(1, self.count):
                arrived = jnp.where(place == index, self.got[index][:slab], arrived)
        else:
            arrived = lax.dynamic_slice_in_dim(self.got, place * slab, slab, 0)
        return kept + arrived.astype(jnp.float32) * jnp.exp2(self.got_level() - 13.0)

    def far_messages(self):
        high = lax.axis_index(dp_axis) // 2
        level = jnp.maximum(self.level, self.got_level()) + 1.0
        return [coded(self.share(high ^ step), level) for step in (1, 2, 3)]

    def send_far(self, messages):
        self.parts = []
        for step, message in zip((1, 2, 3), messages):
            pairs = [
                (2 * source + side, 2 * (source ^ step) + side)
                for source in range(4)
                for side in range(2)
                if self.first <= source ^ step < self.first + self.count
            ]
            self.parts.append(lax.ppermute(message, dp_axis, pairs))

    def square(self):
        if self.owned_square is None:
            self.owned_square = jnp.sum(self.total() ** 2)
        return self.owned_square

    def total(self):
        if self.owned is None:
            self.owned = self.summed()
        return self.owned

    def summed(self):
        if lax.axis_size(dp_axis) != 8:
            return lax.psum_scatter(self.grad(), dp_axis, scatter_dimension=0, tiled=True)
        slab = self.slab()
        total = self.share(lax.axis_index(dp_axis) // 2)
        for part in self.parts:
            total = total + decoded(part, slab)
        return total


def tail_kernel(*refs):
    give, keep, bias, tables, bias_total = refs[:5]
    got, pairs, far, own, near, middle, beside_sum, pair_sum, far_sum, send_sem, recv_sem = refs[5:]
    rank, across = lax.axis_index(dp_axis), lax.axis_index(tensor_axis)
    low, high = lax.rem(rank, 2), lax.div(rank, 2)
    beside = {dp_axis: rank + 1 - 2 * low}
    pair_peers = [{dp_axis: 2 * lax.rem(high + step, 4) + low} for step in (1, 2, 3)]
    tensor_peers = [{tensor_axis: lax.rem(across + step, 4)} for step in (1, 2, 3)]
    barrier = pltpu.get_barrier_semaphore()
    peers = [beside] + pair_peers + tensor_peers
    for peer in peers:
        pl.semaphore_signal(barrier, inc=1, device_id=peer, device_id_type=MESH)
    pl.semaphore_wait(barrier, len(peers))
    slots = iter(range(17))

    def send(source, target, peer):
        slot = next(slots)
        copy = pltpu.make_async_remote_copy(
            src_ref=source,
            dst_ref=target,
            send_sem=send_sem.at[slot],
            recv_sem=recv_sem.at[slot],
            device_id=peer,
            device_id_type=MESH,
        )
        copy.start()
        return copy

    tables_near = send(give, got, beside)
    bias_near = [send(bias, near.at[across], peer) for peer in tensor_peers]
    near[across] = bias[...]
    tables_near.wait()
    pairs[...] = keep[...] + got[...]
    tables_far = [
        send(pairs.at[lax.rem(high + step, 4)], far.at[step - 1], pair_peers[step - 1])
        for step in (1, 2, 3)
    ]
    for copy in bias_near:
        copy.wait()
    middle[...] = near[0] + near[1] + near[2] + near[3]
    send(middle, beside_sum, beside).wait()
    pair_sum[...] = middle[...] + beside_sum[...]
    rows = bias_total.shape[0] // 4
    mine = pl.ds(pl.multiple_of(across * rows, 8), rows)
    far_sum[high] = pair_sum[mine, :]
    bias_far = [send(pair_sum.at[mine], far_sum.at[high], peer) for peer in pair_peers]
    for copy in tables_far:
        copy.wait()
    own[...] = pairs[high] + far[0] + far[1] + far[2]
    tables[across] = own[...]
    tables_all = [send(own, tables.at[across], peer) for peer in tensor_peers]
    for copy in bias_far:
        copy.wait()
    bias_total[mine, :] = far_sum[0] + far_sum[1] + far_sum[2] + far_sum[3]
    bias_all = [send(bias_total.at[mine], bias_total.at[mine], peer) for peer in tensor_peers]
    for copy in tables_all + bias_all:
        copy.wait()


def tail_exchange(tables, bias):
    low = lax.axis_index(dp_axis) % 2
    slab, columns = tables.shape[0] // 8, tables.shape[1]
    blocks = tables.reshape(4, 2 * slab, columns)
    keep = lax.dynamic_slice_in_dim(blocks, low * slab, slab, 1)
    give = lax.dynamic_slice_in_dim(blocks, (1 - low) * slab, slab, 1)
    four, one = keep.shape, (slab, columns)
    vmem = pl.BlockSpec(memory_space=pltpu.VMEM)
    return pl.pallas_call(
        tail_kernel,
        out_shape=[
            jax.ShapeDtypeStruct(four, jnp.float32),
            jax.ShapeDtypeStruct(bias.shape, jnp.float32),
        ],
        in_specs=[vmem] * 3,
        out_specs=[vmem] * 2,
        scratch_shapes=[
            pltpu.VMEM(four, jnp.float32),
            pltpu.VMEM(four, jnp.float32),
            pltpu.VMEM((3,) + one, jnp.float32),
            pltpu.VMEM(one, jnp.float32),
            pltpu.VMEM((4,) + bias.shape, jnp.float32),
            pltpu.VMEM(bias.shape, jnp.float32),
            pltpu.VMEM(bias.shape, jnp.float32),
            pltpu.VMEM(bias.shape, jnp.float32),
            pltpu.VMEM((4, bias.shape[0] // 4, bias.shape[1]), jnp.float32),
            pltpu.SemaphoreType.DMA((17,)),
            pltpu.SemaphoreType.DMA((17,)),
        ],
        compiler_params=pltpu.CompilerParams(
            collective_id=last_exchange, has_side_effects=True, vmem_limit_bytes=24 << 20
        ),
    )(give, keep, bias)


class Traffic:
    def __init__(self, plan):
        self.plan, self.groups = plan, {}

    def add(self, name, group):
        self.groups[name] = group
        return group

    def tie(self, value, near, far, arrived):
        near_messages = [group.near_message() for group in near]
        parts = [group.parts for group in arrived]
        if far:
            value, gots = lax.optimization_barrier((value, [group.got for group in far]))
            for group, got in zip(far, gots):
                group.got = got
        far_messages = [group.far_messages() for group in far]
        value, near_messages, far_messages, parts = lax.optimization_barrier(
            (value, near_messages, far_messages, parts)
        )
        for group, message in zip(near, near_messages):
            group.send_near(message)
        for group, messages in zip(far, far_messages):
            group.send_far(messages)
        for group, part in zip(arrived, parts):
            group.parts = part
        return value

    def input_sum(self, partial_term, kernel):
        if lax.axis_size(dp_axis) != 8:
            return tensor_sum(partial_term, jnp.bfloat16, kernel)[0]
        near, far, arrived = [[self.groups[group] for group in part] for part in self.plan[kernel]]
        partial_term = self.tie(partial_term, near, [], [])
        if kernel == back_encoder + 1:
            group = self.groups[back_encoder]
            done = [self.groups[key] for key in (back_head, back_head + 1, rest_group)]
            totals = [(item.total(), item.square()) for item in done]
            partial_term, group.got[1], totals = lax.optimization_barrier(
                (partial_term, group.got[1], totals)
            )
            for item, (total, square) in zip(done, totals):
                item.owned, item.owned_square = total, square
        total = tensor_sum(partial_term, jnp.bfloat16, kernel)[0]
        total = self.tie(total, [], far, arrived)
        if kernel == back_encoder + 1:
            mix = self.groups[mix_group]
            rest = self.groups[back_encoder]
            total, mix.got, rest.got[2] = lax.optimization_barrier((total, mix.got, rest.got[2]))
            decoder = self.groups[back_decoder]
            total, messages, decoder.parts = lax.optimization_barrier(
                (total, self.encoder_messages(), decoder.parts)
            )
            self.encoder_parts = [
                swap(message, dp_axis, 2 * step) for step, message in zip((1, 2, 3), messages)
            ]
        return total

    def arrive(self, value, index):
        if lax.axis_size(dp_axis) != 8:
            return value
        value, self.encoder_parts[index] = lax.optimization_barrier(
            (value, self.encoder_parts[index])
        )
        return value

    def encoder_share(self, place):
        mix, rest = self.groups[mix_group], self.groups[back_encoder]
        return jnp.where(place == 0, mix.share(place), rest.share(place))

    def encoder_messages(self):
        mix, rest = self.groups[mix_group], self.groups[back_encoder]
        high = lax.axis_index(dp_axis) // 2
        level = jnp.maximum(
            jnp.maximum(mix.level, mix.got_level()), jnp.maximum(rest.level, rest.got_level())
        )
        return [
            coded(self.encoder_share(high ^ step), level + 1.0) for step in (1, 2, 3)
        ]

    def encoder_total(self, ahead):
        parts, ahead = lax.optimization_barrier((self.encoder_parts, ahead))
        slab = self.groups[mix_group].slab()
        total = self.encoder_share(lax.axis_index(dp_axis) // 2)
        for part in parts:
            total = total + decoded(part, slab)
        return total, ahead


def first_kernel(
    images,
    notes,
    class_table,
    table_share,
    block_share,
    all_notes,
    classes,
    tables,
    blocks,
    found,
    note_send,
    note_recv,
    class_send,
    class_recv,
    own_sem,
    across_send,
    across_recv,
    *ring_sems,
):
    rank, place_across = lax.axis_index(dp_axis), lax.axis_index(tensor_axis)
    low = lax.rem(place_across, 2)
    partner, across = place_across + 1 - 2 * low, lax.rem(place_across + 2, 4)
    others = [{tensor_axis: partner}, {tensor_axis: across}]
    greet(pltpu.get_barrier_semaphore(), (dp_axis,), others)
    table_ring = RingGather([table_share], [tables.at[place_across]], *ring_sems[:3])
    block_ring = RingGather([block_share], [blocks], *ring_sems[3:])
    note_copies = spread(notes, all_notes, dp_axis, note_send, note_recv)
    all_notes[rank] = notes[...]
    table_ring.begin()
    block_ring.begin()
    for copy in note_copies:
        copy.wait()
    for step in (1, 2, 3):
        table_ring.advance(step)
    block_ring.advance(1)
    table_ring.finish()

    def cross(owner, peer, slot):
        return pltpu.make_async_remote_copy(
            src_ref=tables.at[owner],
            dst_ref=tables.at[owner],
            send_sem=across_send.at[slot],
            recv_sem=across_recv.at[slot],
            device_id={tensor_axis: peer},
            device_id_type=MESH,
        )

    near = cross(place_across, partner, 0)
    far = cross(place_across, across, 1)
    near.start()
    far.start()
    place = lax.broadcasted_iota(jnp.int32, class_table.shape, 1).astype(jnp.float32)
    lane = lax.broadcasted_iota(jnp.int32, found.shape, 1)
    columns = jnp.zeros(found.shape, jnp.float32)
    for image in range(8 * images):
        label = all_notes[image // images, 0:1, image % images : image % images + 1]
        value = jnp.sum(
            jnp.where(place == label, class_table[...], 0.0), axis=1, keepdims=True
        )
        columns = jnp.where(lane == image, value, columns)
    found[...] = columns
    block_ring.advance(2)
    own = pltpu.make_async_copy(found, classes.at[rank], own_sem.at[0])
    own.start()
    class_copies = spread(found, classes, dp_axis, class_send, class_recv)
    near.wait()
    far.wait()
    forward = cross(across, partner, 2)
    forward.start()
    block_ring.advance(3)
    block_ring.finish()
    forward.wait()
    for copy in class_copies:
        copy.wait()
    own.wait()


def gather_first(notes, class_table, images, table_share, block_share):
    rows = class_table.shape[0]
    vmem, anywhere = pl.BlockSpec(memory_space=pltpu.VMEM), pl.BlockSpec(memory_space=pl.ANY)
    return pl.pallas_call(
        functools.partial(first_kernel, images),
        out_shape=[
            jax.ShapeDtypeStruct((8, 8, 128), jnp.float32),
            jax.ShapeDtypeStruct((8, rows, 128), jnp.float32),
            jax.ShapeDtypeStruct((4, 8) + table_share.shape, table_share.dtype),
            jax.ShapeDtypeStruct((8,) + block_share.shape, block_share.dtype),
        ],
        in_specs=[vmem, vmem, anywhere, anywhere],
        out_specs=[vmem, vmem, anywhere, anywhere],
        scratch_shapes=[pltpu.VMEM((rows, 128), jnp.float32)]
        + [pltpu.SemaphoreType.DMA((7,))] * 4
        + [pltpu.SemaphoreType.DMA((1,))]
        + [pltpu.SemaphoreType.DMA((3,))] * 2
        + ring_scratch(1)
        + ring_scratch(1),
        compiler_params=pltpu.CompilerParams(
            collective_id=first_gather, has_side_effects=True, vmem_limit_bytes=16 << 20
        ),
    )(notes, class_table, table_share, block_share)


def take_pieces(vector, starts, counts):
    return jnp.concatenate(
        [lax.dynamic_slice_in_dim(vector, start, count) for start, count in zip(starts, counts)]
    )


def place_pieces(total, pieces, starts):
    full = jnp.zeros((total,), jnp.float32)
    for piece, start in zip(pieces, starts):
        full = lax.dynamic_update_slice_in_dim(full, piece, start, 0)
    return full


def score_block(queries, key_rows, visible):
    scores = jnp.einsum(
        "bqhd,bkhd->bhqk", queries, key_rows, preferred_element_type=jnp.float32
    ) * HEAD ** (-0.5)
    return scores + (visible[:, None, None, :] - 1.0) * 1000000000.0


def attention(queries, key_rows, value_rows, visible):
    scores = score_block(queries, key_rows, visible)
    largest = jnp.max(scores, axis=-1, keepdims=True)
    exponent = jnp.exp(scores - largest)
    normaliser = jnp.sum(exponent, axis=-1, keepdims=True)
    chance = narrow(exponent / normaliser)
    attended = narrow(
        jnp.einsum("bhqk,bkhd->bqhd", chance, value_rows, preferred_element_type=jnp.float32)
    )
    return (attended, largest + jnp.log(normaliser))


def attention_back(queries, key_rows, value_rows, visible, log_total, grad_attended):
    chance = jnp.exp(score_block(queries, key_rows, visible) - log_total)
    grad_values = jnp.einsum(
        "bhqk,bqhd->bkhd", narrow(chance), grad_attended, preferred_element_type=jnp.float32
    )
    grad_chance = jnp.einsum(
        "bqhd,bkhd->bhqk", grad_attended, value_rows, preferred_element_type=jnp.float32
    )
    grad_scores = narrow(
        chance * (grad_chance - jnp.sum(chance * grad_chance, axis=-1, keepdims=True))
    )
    grad_queries = jnp.einsum(
        "bhqk,bkhd->bqhd", grad_scores, key_rows, preferred_element_type=jnp.float32
    ) * HEAD ** (-0.5)
    grad_keys = jnp.einsum(
        "bhqk,bqhd->bkhd", grad_scores, queries, preferred_element_type=jnp.float32
    ) * HEAD ** (-0.5)
    return (grad_queries, grad_keys, grad_values)


def block_forward(
    stream, visible, layer_rows, layer_bias, vectors, kernel, first_shares, last_shares
):
    images = visible.shape[0]
    local_width = D // lax.axis_size(tensor_axis)
    local_ff = FF // lax.axis_size(tensor_axis)
    heads_here = local_width // HEAD
    flat = stream.reshape(-1, D)
    normed = narrow(layer_norm(flat, vectors[0], vectors[1]))
    mixed = narrow(
        product_right(normed, layer_rows[: 3 * local_width]) + layer_bias[: 3 * local_width]
    )
    parts = [
        mixed[:, slot * local_width : (slot + 1) * local_width].reshape(
            images, -1, heads_here, HEAD
        )
        for slot in range(3)
    ]
    attended, log_total = attention(parts[0], parts[1], parts[2], visible)
    attended = attended.reshape(-1, local_width)
    branch, first_wholes = branch_sum(
        product(attended, layer_rows[3 * local_width + local_ff : 4 * local_width + local_ff]),
        kernel,
        first_shares,
    )
    middle = flat + branch + vectors[4]
    second = narrow(layer_norm(middle, vectors[2], vectors[3]))
    inner = (
        product_right(second, layer_rows[3 * local_width : 3 * local_width + local_ff])
        + layer_bias[3 * local_width :]
    )
    active = narrow(exact_gelu(inner))
    branch, last_wholes = branch_sum(
        product(active, layer_rows[4 * local_width + local_ff :]), kernel + 1, last_shares
    )
    result = middle + branch + vectors[5]
    return (
        result.reshape(stream.shape),
        (flat, normed, parts, log_total, attended, middle, second, inner, active),
        first_wholes,
        last_wholes,
    )


def block_back(incoming, visible, layer_rows, vectors, stored, kernel, traffic):
    flat, normed, parts, log_total, attended, middle, second, inner, active = stored
    local_width = D // lax.axis_size(tensor_axis)
    local_ff = FF // lax.axis_size(tensor_axis)
    mix_rows = layer_rows[: 3 * local_width]
    up_rows = layer_rows[3 * local_width : 3 * local_width + local_ff]
    proj_rows = layer_rows[3 * local_width + local_ff : 4 * local_width + local_ff]
    down_rows = layer_rows[4 * local_width + local_ff :]
    flow = incoming.reshape(-1, D)
    grad_branch = narrow(flow)
    grad_active = product_right(grad_branch, down_rows)
    grad_inner = narrow(local_back(exact_gelu, inner, grad_active))
    grad_second = traffic.input_sum(product(grad_inner, up_rows), kernel)
    grad_middle, grad_gain_two, grad_shift_two = jax.vjp(
        layer_norm, middle, vectors[2], vectors[3]
    )[1](grad_second)
    grad_middle = flow + grad_middle
    grad_attn = narrow(grad_middle)
    grad_attended = narrow(product_right(grad_attn, proj_rows)).reshape(parts[0].shape)
    later = [(grad_inner, second), (attended, grad_attn), (active, grad_branch)]
    apart = kernel == back_encoder and lax.axis_size(dp_axis) == 8
    if apart:
        owned_rows = [traffic.add(kernel, Scattered(later, 1, True))]
        grad_attended = traffic.tie(grad_attended, owned_rows, [], [])
    grads_mixed = attention_back(parts[0], parts[1], parts[2], visible, log_total, grad_attended)
    grad_mixed = narrow(
        jnp.concatenate([piece.reshape(-1, local_width) for piece in grads_mixed], axis=1)
    )
    mix = [(grad_mixed, normed)]
    if apart:
        grad_mixed, owned_rows[0].got[0] = lax.optimization_barrier(
            (grad_mixed, owned_rows[0].got[0])
        )
        traffic.add(mix_group, Scattered(mix, -1))
    else:
        owned_rows = [traffic.add(kernel, Scattered(mix + later))]
    grad_normed = traffic.input_sum(product(grad_mixed, mix_rows), kernel + 1)
    grad_flat, grad_gain_one, grad_shift_one = jax.vjp(layer_norm, flat, vectors[0], vectors[1])[1](
        grad_normed
    )
    grad_bias = jnp.concatenate([column_sum(grad_mixed), column_sum(grad_inner)])
    grad_vectors = jnp.stack(
        [
            grad_gain_one,
            grad_shift_one,
            grad_gain_two,
            grad_shift_two,
            column_sum(grad_attn),
            column_sum(grad_branch),
        ]
    )
    return ((grad_middle + grad_flat).reshape(incoming.shape), owned_rows, grad_bias, grad_vectors)


def gathered_parts(columns, count):
    width = columns.shape[1] // count
    blocks = [block.astype(jnp.float32) for block in tensor_blocks(narrow(columns))]
    return [
        jnp.concatenate([block[:, slot * width : (slot + 1) * width] for block in blocks], axis=1)
        for slot in range(count)
    ]


def adaptive_vectors(cond_act, segment_rows, segment_bias):
    local_hidden = HW // lax.axis_size(tensor_axis)
    adaptive = (
        product_right(cond_act, segment_rows[: 3 * local_hidden]) + segment_bias[: 3 * local_hidden]
    )
    return gathered_parts(adaptive, 3)


def head_block(hidden_state, vectors, segment_rows, segment_bias, last_bias, kernel):
    local_hidden = HW // lax.axis_size(tensor_axis)
    shift_vec, scale_vec, gate_vec = vectors
    modulated = narrow(modulate(hidden_state, shift_vec, scale_vec))
    inner = (
        product_right(modulated, segment_rows[3 * local_hidden : 4 * local_hidden])
        + segment_bias[3 * local_hidden :]
    )
    active = narrow(jax.nn.silu(inner))
    branch = branch_sum(product(active, segment_rows[4 * local_hidden :]), kernel)[0] + last_bias
    return (
        hidden_state + gate_vec * branch,
        (hidden_state, shift_vec, scale_vec, gate_vec, modulated, inner, active, branch),
    )


def head_block_back(incoming, cond_act, segment_rows, offset, stored, kernel, traffic):
    hidden_state, shift_vec, scale_vec, gate_vec, modulated, inner, active, branch = stored
    local_hidden = HW // lax.axis_size(tensor_axis)
    grad_gate = incoming * branch
    grad_branch = narrow(incoming * gate_vec)
    grad_active = product_right(grad_branch, segment_rows[4 * local_hidden :])
    grad_inner = narrow(local_back(jax.nn.silu, inner, grad_active))
    grad_modulated = traffic.input_sum(
        product(grad_inner, segment_rows[3 * local_hidden : 4 * local_hidden]), kernel
    )
    grad_hidden, grad_shift, grad_scale = jax.vjp(modulate, hidden_state, shift_vec, scale_vec)[1](
        grad_modulated
    )
    grad_adaptive = narrow(
        jnp.concatenate(
            [
                lax.dynamic_slice_in_dim(piece, offset, local_hidden, 1)
                for piece in (grad_shift, grad_scale, grad_gate)
            ],
            axis=1,
        )
    )
    grad_cond = product(grad_adaptive, segment_rows[: 3 * local_hidden])
    owned_rows = traffic.add(
        kernel,
        Scattered([(grad_adaptive, cond_act), (grad_inner, modulated), (active, grad_branch)]),
    )
    grad_bias = jnp.concatenate([column_sum(grad_adaptive), column_sum(grad_inner)])
    return (incoming + grad_hidden, grad_cond, owned_rows, grad_bias, column_sum(grad_branch))


def adam_update(weight, moment_one, moment_two, gradient, factor, step_num):
    gradient = gradient * factor
    moment_one = beta_first * moment_one + (1.0 - beta_first) * gradient
    moment_two = beta_second * moment_two + (1.0 - beta_second) * gradient * gradient
    fixed_one = moment_one / (1.0 - beta_first**step_num)
    fixed_two = moment_two / (1.0 - beta_second**step_num)
    weight = weight - learn_rate * (
        fixed_one / (jnp.sqrt(fixed_two) + adam_eps) + decay_rate * weight
    )
    return (weight, moment_one, moment_two)


def local(
    block_weights,
    head_weights,
    head_rest,
    embed_tables,
    bias_rows,
    first_blocks,
    second_blocks,
    first_head,
    second_head,
    first_rest,
    second_rest,
    first_tables,
    second_tables,
    first_bias,
    second_bias,
    patches,
    noise,
    token_mask,
    labels,
    drop_marks,
    timesteps,
    step_weights,
    step_count,
):
    tensor_size = lax.axis_size(tensor_axis)
    tensor_index = lax.axis_index(tensor_axis)
    local_width = D // tensor_size
    local_ff = FF // tensor_size
    local_hidden = HW // tensor_size
    offset = tensor_index * local_hidden
    column_starts = [slot * D + tensor_index * local_width for slot in range(3)] + [
        3 * D + tensor_index * local_ff
    ]
    column_counts = [local_width] * 3 + [local_ff]
    head_starts = [slot * HW + offset for slot in range(4)]
    dp_size = lax.axis_size(dp_axis)
    dp_index = lax.axis_index(dp_axis)
    images = patches.shape[0]
    all_images = dp_size * images
    mask_float = token_mask.astype(jnp.float32)
    matches = timesteps[..., None] == jnp.arange(T_STEPS)
    row_weight = (
        jnp.sum(jnp.where(matches, step_weights, 0.0), axis=-1) * mask_float[None]
    ).reshape(-1)
    chosen = jnp.where(drop_marks == 1, CLASSES, labels)
    class_at = TOKD + 1
    class_end = class_at + CLASSES + 1
    weight_here = jnp.sum(row_weight)
    table_share = jnp.concatenate(
        [embed_tables[:, :class_at], embed_tables[:, class_end:]], axis=1
    )
    class_share = embed_tables[:, class_at:class_end]
    block_share = narrow(block_weights)
    whole_here = dp_size == 8 and tensor_size == 4
    if whole_here:
        part = -(-table_share.shape[1] // 32) * 8
        table_share = jnp.pad(table_share, ((0, 0), (0, 4 * part - table_share.shape[1])))
        table_share = lax.dynamic_slice_in_dim(table_share, tensor_index * part, part, 1)
        notes = jnp.zeros((8, 128), jnp.float32)
        notes = lax.dynamic_update_slice(notes, chosen.astype(jnp.float32)[None], (0, 0))
        notes = lax.dynamic_update_slice(notes, weight_here[None, None], (1, 0))
        all_notes, classes, table_parts, first_block = gather_first(
            notes, class_share, images, table_share.T, block_share[0]
        )
        table_rows = table_parts.transpose(0, 2, 1, 3).reshape(4 * part, -1)
        all_chosen = all_notes[:, 0, :images].reshape(-1)
        weight_total = jnp.sum(all_notes[:, 1, 0])
        class_rows = lax.dynamic_slice_in_dim(
            classes.reshape(-1, classes.shape[-1]), dp_index * images, images, 1
        ).T
    else:
        all_chosen = lax.all_gather(chosen, dp_axis, axis=0, tiled=True).astype(jnp.float32)
        weight_total = lax.psum(weight_here, dp_axis)
        table_rows = lax.all_gather(table_share, dp_axis, axis=0, tiled=True).T
        first_block = lax.all_gather(block_share[0], dp_axis)
    picker = (all_chosen[:, None] == jnp.arange(CLASSES + 1)[None, :]).astype(jnp.float32)
    if not whole_here:
        found = lax.dot_general(
            class_share, picker, (((1,), (1,)), ((), ())), precision=highest
        )
        class_rows = lax.dynamic_slice_in_dim(
            lax.all_gather(found, dp_axis, axis=0, tiled=True), dp_index * images, images, 1
        ).T
    first_block = first_block.reshape(-1, D)
    share_rows = block_share[1].shape[0] // 2
    rest_share = narrow(head_rest)
    flat_bias = bias_rows.reshape(-1)
    rest_bias = flat_bias[: 6 * HW].reshape(6, HW)
    head_bias = flat_bias[6 * HW : 6 * HW + 5 * HB * HW].reshape(HB, 5 * HW)
    column_bias = flat_bias[6 * HW + 5 * HB * HW :].reshape(LAYERS, 3 * D + FF)
    table_parts = cut_rows(table_rows, (TOKD, 1, TOK + BUF, TOK + BUF, 1, 6 * LAYERS, 4))
    layer_vectors = table_parts[5].reshape(LAYERS, 6, D)
    final_norms = table_parts[6]
    patch_flat = patches.reshape(-1, TOKD)
    tokens = product(patch_flat, narrow(table_parts[0])) + table_parts[1][0]
    stream = (
        jnp.concatenate(
            [
                jnp.broadcast_to(class_rows[:, None, :], (images, BUF, D)),
                tokens.reshape(images, TOK, D),
            ],
            axis=1,
        )
        + table_parts[2]
    )
    buffer_ones = jnp.ones((images, BUF), jnp.float32)
    visible_enc = jnp.concatenate([buffer_ones, 1.0 - mask_float], axis=1)
    visible_all = jnp.ones((images, TOK + BUF), jnp.float32)
    hidden_rows = jnp.concatenate([0.0 * buffer_ones, mask_float], axis=1)[..., None]
    layer_bias = [
        take_pieces(column_bias[layer], column_starts, column_counts) for layer in range(LAYERS)
    ]
    encoded, stored_enc, first_half, last_half = block_forward(
        stream,
        visible_enc,
        first_block,
        layer_bias[0],
        layer_vectors[0],
        encoder_forward,
        [block_share[1][:share_rows]],
        [block_share[1][share_rows:]],
    )
    encoded, head_share = lax.optimization_barrier((encoded, narrow(head_weights)))
    head_all = lax.all_gather(head_share, dp_axis, axis=1, tiled=True)
    second_block = jnp.concatenate([first_half[0], last_half[0]], axis=1).reshape(-1, D)
    block_all = [first_block, second_block]
    enc_normed = layer_norm(encoded, final_norms[0], final_norms[1])
    decoder_in = enc_normed * (1.0 - hidden_rows) + table_parts[4][0] * hidden_rows + table_parts[3]
    decoded, stored_dec, first_half, last_half = block_forward(
        decoder_in,
        visible_all,
        second_block,
        layer_bias[1],
        layer_vectors[1],
        decoder_forward,
        [rest_share],
        [],
    )
    rest_rows = first_half[0].reshape(-1, rest_share.shape[-1])
    cond_mine, input_mine, output_mine, time_first, second_mine, final_shift, final_scale = cut_rows(
        rest_rows, (D, TOKD, TOKD, HW, HW, HW, HW)
    )
    cond_weight, input_weight, output_weight, time_second = cut_rows(
        tensor_columns(jnp.concatenate([cond_mine, input_mine, output_mine, second_mine], axis=0)),
        (D, TOKD, TOKD, HW),
    )
    latent = narrow(layer_norm(decoded, final_norms[2], final_norms[3])[:, BUF:].reshape(-1, D))
    condition = product(latent, cond_weight) + rest_bias[0]
    decoded, timesteps, noise, clean = lax.optimization_barrier(
        (decoded, timesteps, noise, patch_flat)
    )
    step_rows = timesteps.reshape(COPIES, -1)
    time_feat = narrow(sinusoid(step_rows).reshape(-1, HW))
    time_pre = product(time_feat, time_first) + lax.dynamic_slice_in_dim(
        rest_bias[2], offset, local_hidden
    )
    time_act = tensor_columns(narrow(jax.nn.silu(time_pre)))
    time_embed = product(time_act, time_second) + rest_bias[3]
    cond_vec = (condition[None] + time_embed.reshape(COPIES, -1, HW)).reshape(-1, HW)
    cond_vec, head_all = lax.optimization_barrier((cond_vec, head_all))
    cond_act = narrow(jax.nn.silu(cond_vec))
    phase = step_rows.astype(jnp.float32)[..., None] * (math.pi / (2 * T_STEPS))
    signal_coef = jnp.cos(phase)
    noise_coef = jnp.sin(phase)
    clean = clean.astype(jnp.float32)[None]
    noise_rows = noise.reshape(COPIES, -1, TOKD).astype(jnp.float32)
    noisy_rows = narrow((signal_coef * clean + noise_coef * noise_rows).reshape(-1, TOKD))
    target = (signal_coef * noise_rows - noise_coef * clean).reshape(-1, TOKD)
    hidden_state = product(noisy_rows, input_weight) + rest_bias[1]
    stored_head = []
    segment_biases = [
        take_pieces(head_bias[segment], head_starts, [local_hidden] * 4) for segment in range(HB)
    ]
    head_vectors = [
        adaptive_vectors(cond_act, head_all[segment], segment_biases[segment])
        for segment in range(HB)
    ]
    last_pair = jnp.concatenate(
        [product(cond_act, final_shift), product(cond_act, final_scale)], axis=1
    ) + take_pieces(flat_bias, [4 * HW + offset, 5 * HW + offset], [local_hidden] * 2)
    shift_last, scale_last = gathered_parts(last_pair, 2)
    for segment in range(HB):
        hidden_state, stored = head_block(
            hidden_state,
            head_vectors[segment],
            head_all[segment],
            segment_biases[segment],
            head_bias[segment, 4 * HW :],
            head_forward + segment,
        )
        stored_head.append(stored)
    final_in = narrow(modulate(hidden_state, shift_last, scale_last))
    predicted = product_right(final_in, output_weight)
    sq_error = jnp.mean((predicted - target) ** 2, axis=-1)
    numerator = jnp.sum(row_weight * sq_error)
    grad_pred = narrow(2.0 / (TOKD * weight_total) * row_weight[:, None] * (predicted - target))
    grad_final = product(grad_pred, output_weight)
    grad_hidden, grad_shift_last, grad_scale_last = jax.vjp(
        modulate, hidden_state, shift_last, scale_last
    )[1](grad_final)

    def own_columns(value):
        return lax.dynamic_slice_in_dim(value, offset, local_hidden, 1)

    grad_shift_last = narrow(own_columns(grad_shift_last))
    grad_scale_last = narrow(own_columns(grad_scale_last))
    traffic = Traffic(
        {
            back_head + 1: ([], [], []),
            back_head: ([back_head + 1], [], []),
            back_cond: ([back_head], [back_head + 1], []),
            back_decoder: ([rest_group], [back_head], [back_head + 1]),
            back_decoder + 1: ([back_decoder], [rest_group], [back_head]),
            back_encoder: ([], [back_decoder], [rest_group]),
            back_encoder + 1: ([mix_group], [], [back_decoder]),
        }
    )
    cond_split = product_right(grad_shift_last, final_shift) + product_right(
        grad_scale_last, final_scale
    )
    head_grads = []
    head_bias_grads = []
    for segment in reversed(range(HB)):
        grad_hidden, grad_cond, grad_segment, grad_segment_bias, grad_last_bias = head_block_back(
            grad_hidden,
            cond_act,
            head_all[segment],
            offset,
            stored_head[segment],
            back_head + segment,
            traffic,
        )
        cond_split = cond_split + grad_cond
        head_grads.insert(0, grad_segment)
        pieces = [
            grad_segment_bias[slot * local_hidden : (slot + 1) * local_hidden] for slot in range(4)
        ] + [grad_last_bias / tensor_size]
        head_bias_grads.insert(0, place_pieces(5 * HW, pieces, head_starts + [4 * HW]))
    grad_input = narrow(grad_hidden)
    grad_cond_vec = narrow(local_back(jax.nn.silu, cond_vec, traffic.input_sum(cond_split, back_cond)))
    cond_bias_grad = column_sum(grad_cond_vec)
    grad_time_act = product_right(
        grad_cond_vec, lax.dynamic_slice_in_dim(time_second, offset, local_hidden, 0)
    )
    grad_time_pre = narrow(local_back(jax.nn.silu, time_pre, grad_time_act))
    grad_latent = jnp.sum(product(grad_cond_vec, cond_weight.T).reshape(COPIES, -1, D), axis=0)
    grad_cond_mine = own_columns(grad_cond_vec)
    rest_scattered = Scattered(
        [
            (jnp.tile(latent, (COPIES, 1)), grad_cond_mine),
            (noisy_rows, own_columns(grad_input)),
            (grad_pred, own_columns(final_in)),
            (time_feat, grad_time_pre),
            (time_act, grad_cond_mine),
            (cond_act, grad_shift_last),
            (cond_act, grad_scale_last),
        ]
    )
    traffic.add(rest_group, rest_scattered)
    rest_bias_grad = place_pieces(
        6 * HW,
        [
            cond_bias_grad / tensor_size,
            column_sum(grad_input) / tensor_size,
            column_sum(grad_time_pre),
            cond_bias_grad / tensor_size,
            column_sum(grad_shift_last),
            column_sum(grad_scale_last),
        ],
        [0, HW, 2 * HW + offset, 3 * HW, 4 * HW + offset, 5 * HW + offset],
    )
    grad_top = jnp.concatenate(
        [jnp.zeros((images, BUF, D), jnp.float32), grad_latent.reshape(images, TOK, D)], axis=1
    )
    grad_decoded, grad_gain_dec, grad_shift_dec = jax.vjp(
        layer_norm, decoded, final_norms[2], final_norms[3]
    )[1](grad_top)
    grad_dec_in, grad_rows_dec, grad_bias_dec, grad_vec_dec = block_back(
        grad_decoded, visible_all, block_all[1], layer_vectors[1], stored_dec, back_decoder, traffic
    )
    grad_encoded, grad_gain_enc, grad_shift_enc = jax.vjp(
        layer_norm, encoded, final_norms[0], final_norms[1]
    )[1](grad_dec_in * (1.0 - hidden_rows))
    grad_stream, grad_rows_enc, grad_bias_enc, grad_vec_enc = block_back(
        grad_encoded, visible_enc, block_all[0], layer_vectors[0], stored_enc, back_encoder, traffic
    )
    grad_stream = traffic.arrive(grad_stream, 0)
    bias_parts = [rest_bias_grad] + head_bias_grads
    grad_tokens = narrow(grad_stream[:, BUF:].reshape(-1, D))
    grad_class = lax.dynamic_update_slice_in_dim(
        jnp.zeros((all_images, D), jnp.float32),
        jnp.sum(grad_stream[:, :BUF], axis=1),
        dp_index * images,
        0,
    )
    small_rows = jnp.concatenate(
        [
            column_sum(grad_tokens)[None],
            jnp.sum(grad_dec_in * hidden_rows, axis=(0, 1))[None],
            grad_vec_enc,
            grad_vec_dec,
            jnp.stack([grad_gain_enc, grad_shift_enc, grad_gain_dec, grad_shift_dec]),
            grad_class,
        ],
        axis=0,
    )
    seq_rows = TOK + BUF
    small_at = 2 * seq_rows + TOKD
    table_count = small_at + small_rows.shape[0]
    quarter = -(-table_count // (8 * tensor_size)) * 8
    small_rows = jnp.pad(small_rows, ((0, quarter * tensor_size - table_count), (0, 0)))
    grad_tables = jnp.concatenate(
        [
            jnp.sum(grad_stream, axis=0),
            jnp.sum(grad_dec_in, axis=0),
            product_left(patch_flat, grad_tokens),
            small_rows,
        ],
        axis=0,
    )
    grad_tables = lax.dynamic_slice_in_dim(grad_tables, tensor_index * quarter, quarter, 0)
    column_grads = []
    for grad_local in (grad_bias_enc, grad_bias_dec):
        pieces = [
            grad_local[slot * local_width : (slot + 1) * local_width] for slot in range(3)
        ] + [grad_local[3 * local_width :]]
        column_grads.append(place_pieces(3 * D + FF, pieces, column_starts))
    lanes = bias_rows.shape[1]
    bias_local = jnp.concatenate(bias_parts + column_grads).reshape(-1, lanes)
    if dp_size == 8 and tensor_size == 4:
        bias_count = bias_local.shape[0]
        bias_local = jnp.pad(bias_local, ((0, -bias_count % 32), (0, 0)))
        owned_cols, bias_grad = tail_exchange(grad_tables.T, bias_local)
        encoder_owned, (owned_cols, bias_grad) = traffic.encoder_total((owned_cols, bias_grad))
        owned_cols = jnp.concatenate([owned_cols[index] for index in range(4)], axis=1)
        bias_grad = bias_grad[:bias_count]
    else:
        owned_cols = tensor_columns(
            lax.psum_scatter(grad_tables.T, dp_axis, scatter_dimension=0, tiled=True)
        )
        bias_grad = sum_everywhere(bias_local, (tensor_axis, dp_axis))
        encoder_owned = grad_rows_enc[0].total()
    class_cols = small_at + 6 * LAYERS + 6
    owned_tables = jnp.concatenate(
        [
            owned_cols[:, 2 * seq_rows : small_at + 1],
            jnp.dot(
                owned_cols[:, class_cols : class_cols + all_images], picker, precision=highest
            ),
            owned_cols[:, : 2 * seq_rows],
            owned_cols[:, small_at + 1 : class_cols],
        ],
        axis=1,
    )
    owned_blocks = jnp.stack([encoder_owned, grad_rows_dec[0].total()])
    owned_head = jnp.stack([group.total() for group in head_grads])
    owned_rest = rest_scattered.total()
    split_squares = (
        jnp.sum(encoder_owned * encoder_owned)
        + grad_rows_dec[0].square()
        + sum(group.square() for group in head_grads)
        + rest_scattered.square()
    )
    shared_squares = jnp.sum(owned_tables * owned_tables) / tensor_size
    every_squares = jnp.sum(bias_grad * bias_grad) / (tensor_size * lax.axis_size(dp_axis))
    last_sums = small_sums(
        [split_squares + shared_squares + every_squares, numerator / tensor_size]
    )
    norm_square = last_sums[0]
    loss_value = last_sums[1] / weight_total
    grad_norm = jnp.sqrt(norm_square)
    factor = jnp.minimum(1.0, clip_limit / (grad_norm + 1e-06))
    step_num = step_count[0].astype(jnp.float32)
    blocks_new, blocks_first, blocks_second = adam_update(
        block_weights, first_blocks, second_blocks, owned_blocks, factor, step_num
    )
    head_new, head_first, head_second = adam_update(
        head_weights, first_head, second_head, owned_head, factor, step_num
    )
    rest_new, rest_first, rest_second = adam_update(
        head_rest, first_rest, second_rest, owned_rest, factor, step_num
    )
    tables_new, tables_first, tables_second = adam_update(
        embed_tables, first_tables, second_tables, owned_tables, factor, step_num
    )
    bias_new, bias_first, bias_second = adam_update(
        bias_rows, first_bias, second_bias, bias_grad, factor, step_num
    )
    return (
        loss_value,
        grad_norm,
        blocks_new,
        blocks_first,
        blocks_second,
        narrow(blocks_new),
        head_new,
        head_first,
        head_second,
        narrow(head_new),
        rest_new,
        rest_first,
        rest_second,
        narrow(rest_new),
        tables_new,
        tables_first,
        tables_second,
        narrow(tables_new),
        bias_new,
        bias_first,
        bias_second,
        narrow(bias_new),
    )


def solution(mesh):
    in_specs = (
        P(None, (dp_axis, tensor_axis), None),
        P(None, (dp_axis, tensor_axis), None),
        P(dp_axis, tensor_axis),
        P(dp_axis, None),
        P(),
        P(None, (dp_axis, tensor_axis), None),
        P(None, (dp_axis, tensor_axis), None),
        P(None, (dp_axis, tensor_axis), None),
        P(None, (dp_axis, tensor_axis), None),
        P(dp_axis, tensor_axis),
        P(dp_axis, tensor_axis),
        P(dp_axis, None),
        P(dp_axis, None),
        P(),
        P(),
        P(dp_axis, None, None),
        P(None, dp_axis, None, None),
        P(dp_axis, None),
        P(dp_axis),
        P(dp_axis),
        P(None, dp_axis, None),
        P(),
        P(),
    )
    out_specs = (
        P(),
        P(),
        P(None, (dp_axis, tensor_axis), None),
        P(None, (dp_axis, tensor_axis), None),
        P(None, (dp_axis, tensor_axis), None),
        P(None, (dp_axis, tensor_axis), None),
        P(None, (dp_axis, tensor_axis), None),
        P(None, (dp_axis, tensor_axis), None),
        P(None, (dp_axis, tensor_axis), None),
        P(None, (dp_axis, tensor_axis), None),
        P(dp_axis, tensor_axis),
        P(dp_axis, tensor_axis),
        P(dp_axis, tensor_axis),
        P(dp_axis, tensor_axis),
        P(dp_axis, None),
        P(dp_axis, None),
        P(dp_axis, None),
        P(dp_axis, None),
        P(),
        P(),
        P(),
        P(),
    )
    return jax.shard_map(local, mesh=mesh, in_specs=in_specs, out_specs=out_specs, check_vma=False)
```
